256 devices in a mesh: gx: 32 (over z, x), gy: 8 (over y, core).
Axes of the slice: x: 4, y: 4, z: 8, core: 2. Of those that a mesh axis runs over, the one named last changes fastest.
Arguments:
- body_force: float32 [3, 512, 256, 128], P(None, 'gx', 'gy'), may hold values from -30 to 30, as said below
- fixed_dofs: int32 [3, 512, 256, 128], P(None, 'gx', 'gy'), may hold values 0 or 1
- load_nodes: int32 [512, 3], replicated, may hold values from 0 to 511, as said below
- load_forces: float32 [3, 512], replicated, may hold values from -32 to 32
- frequencies: float32 [3, 64], replicated, may hold values from -24 to 24
- hidden_weights: float32 [3, 128, 128], replicated, may hold values from -0.5 to 0.5
- hidden_biases: float32 [3, 128], replicated, may hold values from -6 to 6
- output_weights: float32 [128], replicated, may hold values from -3 to 3
- output_bias: float32 [1], replicated, may hold values from -3 to 3
Outputs:
- displacement: float32 [3, 512, 256, 128], P(None, 'gx', 'gy')
- density: float32 [512, 256, 128], P('gx', 'gy')
The draws below stay inside these ranges and needn't reach their ends.
Inputs may be any that keep to these rules, and one draw needn't show every extreme that they name: `load_nodes`: row p gives the x, y and z index of point load p's node: column 0 below 512, column 1 below 256, column 2 below 128; several loads may share a node. `body_force`: finite values of order one to ten.
All inputs are finite; a program needn't handle non-finite values. No bound on the sum of `fixed_dofs` on one device may be relied on, other than what follows from the above.
Results may differ from the reference program's by a relative error of at most 0.00013.
Values sent between devices are 32-bit elements; how exact they have to be, the bound alone decides.
No kernel may reach another device: no remote copies, remote signals or barrier semaphores. Data moves between devices by JAX's collectives and lax.ppermute only.
A program may use at most 128 MiB of HBM per device.

```python
import math
import jax
import jax.numpy as jnp
import numpy as np
from jax import lax

CF = 4
WIDTH = 128
FREQS = 64
LAYERS = 3
ITERS = 2
NLOAD = 512
NX = 512
NY = 256
NZ = 128


def period_sign(count):
    index = jnp.arange(count, dtype=jnp.int32)
    return (1 - 2 * (index // 2 % 2)).astype(jnp.float32)


def draw_body_force(key, part):
    grid_shape = (3, NX, NY, NZ)
    along_x = (jnp.arange(NX, dtype=jnp.float32) / NX)[None, :, None, None]
    along_y = (jnp.arange(NY, dtype=jnp.float32) / NY)[None, None, :, None]
    along_z = (jnp.arange(NZ, dtype=jnp.float32) / NZ)[None, None, None, :]
    ramp = 10.0 ** (along_x - 0.5)
    pattern = period_sign(NX)[None, :, None, None] * period_sign(NY)[None, None, :, None] * period_sign(NZ)[None, None, None, :]
    rough = jax.random.truncated_normal(key, -4.0, 4.0, grid_shape, jnp.float32)
    smooth = 1.5 * (1.0 + 0.3 * jnp.sin(2.0 * along_x + 3.0 * along_y + 1.5 * along_z))
    return (ramp * pattern * (rough + smooth)).astype(jnp.float32)


def draw_load_nodes(key, part):
    keys = jax.random.split(jax.random.fold_in(key, 7), 3)
    index_x = jax.random.randint(keys[0], (NLOAD,), 0, NX, dtype=jnp.int32)
    index_y = jax.random.randint(keys[1], (NLOAD,), 0, NY, dtype=jnp.int32)
    index_z = jax.random.randint(keys[2], (NLOAD,), 0, NZ, dtype=jnp.int32)
    index_y = index_y.at[0].set(NY - 1)
    index_x = index_x.at[1].set(0)
    index_x = index_x.at[2].set(NX - 1)
    index_z = index_z.at[3].set(NZ - 1)
    return jnp.stack([index_x, index_y, index_z], axis=1).astype(jnp.int32)


def place_ends(values, rng, smallest, high):
    dims = values.shape
    place = [jax.random.randint(jax.random.fold_in(rng, axis), (), 0, dims[axis]) for axis in range(len(dims))]
    values = values.at[tuple(place)].set(smallest)
    longest = dims.index(max(dims))
    place[longest] = (place[longest] + 1) % dims[longest]
    return values.at[tuple(place)].set(high)


def normal_values(key, extent, width, limit, kind=jnp.bfloat16):
    drawn = jax.random.normal(key, extent, jnp.float32) * width
    return jnp.minimum(jnp.maximum(drawn, -limit), limit).astype(kind)


def setup_inputs(seed: int = 0) -> dict:
    arg_keys = jax.random.split(jax.random.key(seed), 10)
    return {
        "body_force": draw_body_force(jax.random.fold_in(arg_keys[9], 71), 0),
        "fixed_dofs": place_ends((jax.random.randint(arg_keys[1], (3, NX, NY, NZ), 0, 16) < 1).astype(jnp.int32), jax.random.fold_in(arg_keys[1], 1), 0, 1),
        "load_nodes": draw_load_nodes(jax.random.fold_in(arg_keys[9], 71), 0),
        "load_forces": normal_values(arg_keys[3], (3, NLOAD), 5.0, 32.0, jnp.float32),
        "frequencies": normal_values(arg_keys[4], (3, FREQS), 4.0, 24.0, jnp.float32),
        "hidden_weights": normal_values(arg_keys[5], (LAYERS, WIDTH, WIDTH), WIDTH ** -0.5, 0.5, jnp.float32),
        "hidden_biases": normal_values(arg_keys[6], (LAYERS, WIDTH), 0.5, 6.0, jnp.float32),
        "output_weights": normal_values(arg_keys[7], (WIDTH,), 0.2, 3.0, jnp.float32),
        "output_bias": normal_values(arg_keys[8], (1,), 1.0, 3.0, jnp.float32),
    }


full_turn = 2.0 * math.pi
highest = lax.Precision.HIGHEST

def element_stiffness():
    poisson = 0.3
    lame_first = poisson / ((1.0 + poisson) * (1.0 - 2.0 * poisson))
    lame_second = 1.0 / (2.0 * (1.0 + poisson))
    elastic = np.zeros((6, 6))
    elastic[:3, :3] = lame_first
    elastic[np.arange(3), np.arange(3)] += 2.0 * lame_second
    elastic[np.arange(3, 6), np.arange(3, 6)] = lame_second
    gauss = 1.0 / math.sqrt(3.0)
    stiffness = np.zeros((24, 24))
    for point in range(8):
        where_at = [gauss * (2 * (point >> which & 1) - 1) for which in range(3)]
        strain = np.zeros((6, 24))
        for corner in range(8):
            signs = [2 * (corner >> which & 1) - 1 for which in range(3)]
            slopes = []
            for which in range(3):
                value = 0.25 * signs[which]
                for other in range(3):
                    if other != which:
                        value = value * (1.0 + signs[other] * where_at[other])
                slopes.append(value)
            column = 3 * corner
            strain[0, column] = slopes[0]
            strain[1, column + 1] = slopes[1]
            strain[2, column + 2] = slopes[2]
            strain[3, column] = slopes[1]
            strain[3, column + 1] = slopes[0]
            strain[4, column + 1] = slopes[2]
            strain[4, column + 2] = slopes[1]
            strain[5, column] = slopes[2]
            strain[5, column + 2] = slopes[0]
        stiffness = stiffness + strain.T @ elastic @ strain * 0.125
    return jnp.asarray(stiffness, dtype=jnp.float32)

def corner_offsets(corner):
    return (corner & 1, corner >> 1 & 1, corner >> 2 & 1)

def z_shift(values, offset):
    widths = [(0, 0)] * (values.ndim - 1)
    if offset > 0:
        return jnp.pad(values[..., 1:], widths + [(0, 1)])
    return jnp.pad(values[..., :-1], widths + [(1, 0)])

def coarse_density(begin_x, begin_y, count_x, count_y, count_z, total_x, total_y, total_z, frequencies, hidden_weights, hidden_biases, output_weights, output_bias):
    along_x = ((begin_x + jnp.arange(count_x, dtype=jnp.int32)).astype(jnp.float32) + 0.5) / float(total_x)
    along_y = ((begin_y + jnp.arange(count_y, dtype=jnp.int32)).astype(jnp.float32) + 0.5) / float(total_y)
    along_z = (jnp.arange(count_z, dtype=jnp.int32).astype(jnp.float32) + 0.5) / float(total_z)
    grid_shape = (count_x, count_y, count_z)
    centres = jnp.stack([jnp.broadcast_to(along_x[:, None, None], grid_shape).reshape(-1), jnp.broadcast_to(along_y[None, :, None], grid_shape).reshape(-1), jnp.broadcast_to(along_z[None, None, :], grid_shape).reshape(-1)], axis=0)
    phases = jnp.dot(frequencies.T, centres, precision=highest, preferred_element_type=jnp.float32) * full_turn
    hidden = jnp.concatenate([jnp.sin(phases), jnp.cos(phases)], axis=0)
    for layer in range(hidden_weights.shape[0]):
        mixed = jnp.dot(hidden_weights[layer].T, hidden, precision=highest, preferred_element_type=jnp.float32)
        hidden = jax.nn.silu(mixed + hidden_biases[layer][:, None])
    logits = jnp.dot(output_weights, hidden, precision=highest, preferred_element_type=jnp.float32) + output_bias[0]
    return jax.nn.sigmoid(logits).reshape(grid_shape)

def upsample(coarse):
    across, along, height = coarse.shape
    spread = jnp.broadcast_to(coarse[:, None, :, None, :, None], (across, CF, along, CF, height, CF))
    return spread.reshape(across * CF, along * CF, height * CF)

def cone_filter(padded, count_x, count_y):
    result = jnp.zeros((count_x, count_y, padded.shape[2]), jnp.float32)
    for shift_x in (-1, 0, 1):
        for shift_y in (-1, 0, 1):
            for shift_z in (-1, 0, 1):
                weight = 2.0 - math.sqrt(shift_x * shift_x + shift_y * shift_y + shift_z * shift_z)
                piece = padded[1 + shift_x:1 + shift_x + count_x, 1 + shift_y:1 + shift_y + count_y]
                if shift_z != 0:
                    piece = z_shift(piece, shift_z)
                result = result + weight * piece
    return result

def corner_products(nodes, young, stiffness):
    across, along, height = young.shape
    pieces = []
    for corner in range(8):
        off_x, off_y, off_z = corner_offsets(corner)
        piece = nodes[:, off_x:off_x + across, off_y:off_y + along]
        if off_z:
            piece = z_shift(piece, 1)
        pieces.append(piece)
    stacked = jnp.concatenate(pieces, axis=0).reshape(24, across * along * height)
    products = jnp.dot(stiffness, stacked, precision=highest, preferred_element_type=jnp.float32)
    return products.reshape(24, across, along, height) * young[None]

def interior_forces(products):
    across, along = (products.shape[1], products.shape[2])
    result = jnp.zeros((3, across - 1, along - 1, products.shape[3]), jnp.float32)
    for corner in range(8):
        off_x, off_y, off_z = corner_offsets(corner)
        piece = products[3 * corner:3 * corner + 3, 1 - off_x:across - off_x, 1 - off_y:along - off_y]
        if off_z:
            piece = z_shift(piece, -1)
        result = result + piece
    return result

def recompute_forces(nodes_ext, young_ext, stiffness):
    planes = nodes_ext.shape[1] - 2
    count = planes // CF

    def block(index):
        begin = index * CF
        nodes_block = lax.dynamic_slice_in_dim(nodes_ext, begin, CF + 2, 1)
        young_block = lax.dynamic_slice_in_dim(young_ext, begin, CF + 1, 0)
        return interior_forces(corner_products(nodes_block, young_block, stiffness))
    blocks = lax.map(block, jnp.arange(count, dtype=jnp.int32))
    return jnp.moveaxis(blocks, 0, 1).reshape(3, planes, nodes_ext.shape[2] - 2, nodes_ext.shape[3])

def stiffness_diagonal(young_ext, stiffness):
    across, along = (young_ext.shape[0] - 1, young_ext.shape[1] - 1)
    entries = jnp.diagonal(stiffness)
    result = jnp.zeros((3, across, along, young_ext.shape[2]), jnp.float32)
    for corner in range(8):
        off_x, off_y, off_z = corner_offsets(corner)
        piece = young_ext[1 - off_x:1 - off_x + across, 1 - off_y:1 - off_y + along]
        if off_z:
            piece = z_shift(piece, -1)
        result = result + entries[3 * corner:3 * corner + 3][:, None, None, None] * piece[None]
    return result

def reference(body_force, fixed_dofs, load_nodes, load_forces, frequencies, hidden_weights, hidden_biases, output_weights, output_bias):
    stiffness = element_stiffness()
    coarse = coarse_density(0, 0, NX // CF, NY // CF, NZ // CF, NX // CF, NY // CF, NZ // CF, frequencies, hidden_weights, hidden_biases, output_weights, output_bias)
    raw = upsample(coarse)
    rim_widths = ((1, 1), (1, 1), (0, 0))
    inside = jnp.pad(jnp.ones((NX, NY, NZ), jnp.float32), rim_widths)
    density = cone_filter(jnp.pad(raw, rim_widths), NX, NY) / cone_filter(inside, NX, NY)
    young = 0.02 + 0.98 * density ** 3
    young_ext = jnp.pad(young, ((1, 0), (1, 0), (0, 0)))
    free_dofs = 1.0 - fixed_dofs.astype(jnp.float32)
    jacobi = free_dofs * stiffness_diagonal(young_ext, stiffness) + (1.0 - free_dofs)
    loaded = body_force.at[:, load_nodes[:, 0], load_nodes[:, 1], load_nodes[:, 2]].add(load_forces)
    rhs = free_dofs * loaded

    def apply_operator(field):
        padded = jnp.pad(field, ((0, 0), (1, 1), (1, 1), (0, 0)))
        return free_dofs * recompute_forces(padded, young_ext, stiffness)
    displacement = jnp.zeros_like(rhs)
    residual = rhs
    scaled = residual / jacobi
    direction = scaled
    norm_now = jnp.sum(residual * scaled)
    for iteration in range(ITERS):
        image = apply_operator(direction)
        alpha = norm_now / jnp.sum(direction * image)
        displacement = displacement + alpha * direction
        residual = residual - alpha * image
        if iteration + 1 < ITERS:
            scaled = residual / jacobi
            norm_next = jnp.sum(residual * scaled)
            direction = scaled + norm_next / norm_now * direction
            norm_now = norm_next
    return (displacement, density)
```

```python
import functools
import math

import jax
import jax.numpy as jnp
from jax import lax
from jax.experimental import pallas as pl
from jax.experimental.pallas import tpu as pltpu
from jax.sharding import PartitionSpec as P

CF = 4
NX, NY, NZ = 16, 32, 128
TOTAL_X, TOTAL_Y = 512, 256
CX, CY, CZ = NX // CF, NY // CF, NZ // CF
GX, GY = CX + 2, CY + 2
EX, EY = GX * CF, GY * CF
SIZE = EX * EY
LOADS = 512
NU, MU = 0.3, 1.0 / 2.6
LAM = 0.3 / (1.3 * 0.4)
RATIO = LAM / MU
DIAG = (LAM + 4.0 * MU) / 9.0
VMEM = pltpu.VMEM
SMEM = pltpu.SMEM
highest = lax.Precision.HIGHEST
f32 = jnp.float32


def spec(space=VMEM):
    return pl.BlockSpec(memory_space=space)


def call(kernel, out_shape, in_spaces, args, scratch=(), cost=None):
    return pl.pallas_call(
        kernel,
        out_shape=out_shape,
        in_specs=[spec(s) for s in in_spaces],
        out_specs=jax.tree.map(lambda _: spec(), out_shape),
        scratch_shapes=list(scratch),
        compiler_params=pltpu.CompilerParams(vmem_limit_bytes=48 << 20),
        cost_estimate=cost,
    )(*args)


def shape(*dims):
    return jax.ShapeDtypeStruct(dims, f32)


def pack_kernel(ids, nodes_s, forces_s, body, fixed, nodes_v, r_out, lo_out, hi_out):
    start_x = ids[0] * NX
    start_y = ids[1] * NY
    r_out[...] = body[...]
    lx = nodes_v[0:1, :] - start_x
    ly = nodes_v[1:2, :] - start_y
    mine = (lx >= 0) & (lx < NX) & (ly >= 0) & (ly < NY)
    index = lax.broadcasted_iota(jnp.int32, (1, LOADS), 1)
    todo = jnp.where(mine, index, LOADS)
    lane = lax.broadcasted_iota(jnp.int32, (1, NZ), 1)

    def more(p):
        return p < LOADS

    def add_one(p):
        x = nodes_s[0, p] - start_x
        y = nodes_s[1, p] - start_y
        hit = lane == nodes_s[2, p]
        for c in range(3):
            row = pl.ds((c * NX + x) * NY + y, 1)
            r_out[row, :] = r_out[row, :] + jnp.where(hit, forces_s[c, p], 0.0)
        return jnp.min(jnp.where(todo > p, todo, LOADS))

    lax.while_loop(more, add_one, jnp.min(todo))

    def mask(i, carry):
        rows = pl.ds(pl.multiple_of(i * NY, NY), NY)
        r_out[rows, :] = jnp.where(fixed[rows, :] == 0, r_out[rows, :], 0.0)
        return carry

    lax.fori_loop(0, 3 * NX, mask, 0, unroll=4)
    for c in range(3):
        for j in range(2):
            lo_out[pl.ds((c * 2 + j) * NX, NX), :] = r_out[pl.ds(c * NX * NY + j, NX, stride=NY), :]
            hi_out[pl.ds((c * 2 + j) * NX, NX), :] = r_out[
                pl.ds(c * NX * NY + NY - 2 + j, NX, stride=NY), :
            ]
        free = fixed[pl.ds(c * NX * NY, NX, stride=NY), :] == 0
        lo_out[pl.ds((6 + c) * NX, NX), :] = jnp.where(free, 1.0, 0.0)
        free = fixed[pl.ds(c * NX * NY + NY - 1, NX, stride=NY), :] == 0
        hi_out[pl.ds((6 + c) * NX, NX), :] = jnp.where(free, 1.0, 0.0)


def planes_kernel(r, fixed, ylo, yhi, lo_out, hi_out):
    for out, first in ((lo_out, 0), (hi_out, NX - 2)):
        out[...] = jnp.zeros_like(out)
        for c in range(3):
            for j in range(2):
                x = first + j
                base = (c * 2 + j) * EY
                out[pl.ds(base + 4, NY), :] = r[pl.ds((c * NX + x) * NY, NY), :]
                for k in range(2):
                    out[pl.ds(base + 2 + k, 1), :] = ylo[pl.ds((c * 2 + k) * NX + x, 1), :]
                    out[pl.ds(base + 36 + k, 1), :] = yhi[pl.ds((c * 2 + k) * NX + x, 1), :]
            x = 0 if first == 0 else NX - 1
            base = (6 + c) * EY
            free = fixed[pl.ds((c * NX + x) * NY, NY), :] == 0
            out[pl.ds(base + 4, NY), :] = jnp.where(free, 1.0, 0.0)
            out[pl.ds(base + 3, 1), :] = ylo[pl.ds((6 + c) * NX + x, 1), :]
            out[pl.ds(base + 36, 1), :] = yhi[pl.ds((6 + c) * NX + x, 1), :]


def split2(v):
    hi = v.astype(jnp.bfloat16)
    return hi, (v - hi.astype(f32)).astype(jnp.bfloat16)


def sigmoid(v):
    return 1.0 / (1.0 + jnp.exp(-v))


def mlp_kernel(ids, freq, weights, biases, wout, bout, coarse, axy, bxy, w2):
    cx0 = ids[0] * CX - 1
    cy0 = ids[1] * CY - 1
    f = freq[...]
    ff = jnp.concatenate([f, f], axis=1)
    quarter = jnp.where(lax.broadcasted_iota(jnp.int32, (1, 128), 1) < 64, 0.0, 0.25)

    def waves(row, coords):
        turns = ff[row : row + 1, :] * coords
        turns = turns - jnp.round(turns)
        wave = jnp.sin((turns + quarter) * (2.0 * math.pi))
        other = jnp.sin((turns + (0.25 - quarter)) * (2.0 * math.pi))
        return wave, other

    def coords(start, rows, total):
        i = lax.broadcasted_iota(jnp.int32, (rows, 128), 0) + start
        return (i.astype(f32) + 0.5) * (1.0 / total)

    first = lax.broadcasted_iota(jnp.int32, (1, 128), 1) < 64
    wx, ox = waves(0, coords(cx0, 8, TOTAL_X // CF))
    wy, oy = waves(1, coords(cy0, 16, TOTAL_Y // CF))
    wz, oz = waves(2, coords(0, CZ, CZ))
    cosx, sinx = jnp.where(first, ox, wx), jnp.where(first, wx, ox)
    cosz, sinz = jnp.where(first, oz, wz), jnp.where(first, wz, oz)
    turnedy = jnp.where(first, oy, -oy)
    cosy, siny = jnp.where(first, oy, wy), jnp.where(first, wy, oy)
    for i in range(GX):
        both = wy * cosx[i : i + 1, :] + turnedy * sinx[i : i + 1, :]
        axy[pl.ds(16 * i, 16), :] = both
        c = cosy * cosx[i : i + 1, :] - siny * sinx[i : i + 1, :]
        s = siny * cosx[i : i + 1, :] + cosy * sinx[i : i + 1, :]
        bxy[pl.ds(16 * i, 16), :] = jnp.where(first, c, -s)

    for l in range(3):
        hi, lo = split2(weights[l])
        both = jnp.concatenate([hi, lo], axis=1)
        w2[l] = jnp.concatenate([both, both], axis=0)

    rows = GY * CZ
    wrow = jnp.broadcast_to(wout[...], (16, 128))
    ri = lax.broadcasted_iota(jnp.int32, (16, rows), 0)
    li = lax.broadcasted_iota(jnp.int32, (16, rows), 1)
    pick = (li // CZ) == ((ri + 1) & 15)
    ui = lax.broadcasted_iota(jnp.int32, (rows, 128), 0)
    uj = lax.broadcasted_iota(jnp.int32, (rows, 128), 1)
    up = jnp.where((ui & (CZ - 1)) == (uj // CF), 1.0, 0.0)

    def body(i, carry):
        parts = []
        for j in range(GY):
            a = axy[pl.ds(16 * i + j, 1), :]
            b = bxy[pl.ds(16 * i + j, 1), :]
            parts.append(a * cosz + b * sinz)
        h = jnp.concatenate(parts, axis=0)
        for l in range(3):
            hi, lo = split2(h)
            both = jnp.concatenate([hi, lo], axis=1)
            out = jnp.dot(both, w2[l], preferred_element_type=f32)
            v = out[:, :128] + out[:, 128:] + biases[l : l + 1, :]
            h = v * sigmoid(v)
        logits = lax.dot_general(
            wrow, h, (((1,), (1,)), ((), ())), precision=highest, preferred_element_type=f32
        )
        picked = jnp.where(pick, logits, 0.0)
        wide = jnp.dot(picked, up, precision=highest, preferred_element_type=f32)
        coarse[i] = sigmoid(wide + bout[0])
        return carry

    lax.fori_loop(0, GX, body, 0)


W0, W1, W2, W3 = 2.0, 1.0, 2.0 - math.sqrt(2.0), 2.0 - math.sqrt(3.0)


def density_kernel(ids, coarse, young, inverse, density):
    lane = lax.broadcasted_iota(jnp.int32, (16, NZ), 1)
    not_last, not_first = lane < NZ - 1, lane > 0
    y_cell = ids[1] * CY + jnp.where(
        lax.broadcasted_iota(jnp.int32, (16, NZ), 0) == 15,
        -1,
        lax.broadcasted_iota(jnp.int32, (16, NZ), 0),
    )
    inside_y = (y_cell >= 0) & (y_cell < TOTAL_Y // CF)

    def layers(v):
        side = jnp.where(not_last, pltpu.roll(v, NZ - 1, 1), 0.0) + jnp.where(
            not_first, pltpu.roll(v, 1, 1), 0.0
        )
        return W0 * v + W1 * side, W1 * v + W2 * side, W2 * v + W3 * side

    zero = jnp.zeros((16, NZ), f32)
    values, insides = [], []
    for i in range(GX):
        x_cell = ids[0] * CX - 1 + i
        ok = inside_y & (x_cell >= 0) & (x_cell < TOTAL_X // CF)
        insides.append(jnp.where(ok, 1.0, 0.0))
        values.append(jnp.where(ok, coarse[i], 0.0))
    stacks = [[layers(v) for v in group] for group in (values, insides)]

    for i in range(GX):
        for kind in range(3):
            low = max(i - 1, 0) if kind == 0 else i
            high = min(i + 1, GX - 1) if kind == 2 else i
            sums = []
            for stack in stacks:
                t0 = stack[i][0] + (stack[low][1] + stack[high][1])
                t1 = stack[i][1] + (stack[low][2] + stack[high][2])
                down = pltpu.roll(t1, 1, 0)
                above = pltpu.roll(t1, 15, 0)
                sums.append((t0 + (down + t1), t0 + (t1 + t1), t0 + (t1 + above)))
            planes = {0: (0,), 1: (1, 2), 2: (3,)}[kind]
            for row_kind in range(3):
                count = sums[1][row_kind]
                inside = insides[i] > 0.0
                rho = sums[0][row_kind] / jnp.where(inside, count, 1.0)
                modulus = jnp.where(inside, 0.02 + 0.98 * (rho * rho * rho), 0.0)
                for ox in planes:
                    x = i * CF + ox
                    for oy in {0: (0,), 1: (1, 2), 2: (3,)}[row_kind]:
                        young[pl.ds(x * EY + CF + oy, 8, stride=CF), :] = modulus[0:8, :]
                        young[pl.ds(x * EY + 36 + oy, 1), :] = modulus[8:9, :]
                        young[pl.ds(x * EY + oy, 1), :] = modulus[15:16, :]
                        if 1 <= i <= CX:
                            density[pl.ds((x - CF) * NY + oy, 8, stride=CF), :] = rho[0:8, :]

    lane8 = lax.broadcasted_iota(jnp.int32, (EY, NZ), 1) > 0
    inverse[pl.ds(0, EY), :] = jnp.zeros((EY, NZ), f32)

    def plane(x, carry):
        rows = pl.ds(pl.multiple_of(x * EY, 8), EY)
        before = pl.ds(pl.multiple_of((x - 1) * EY, 8), EY)
        total = young[rows, :] + young[before, :]
        total = total + pltpu.roll(total, 1, 0)
        total = total + jnp.where(lane8, pltpu.roll(total, 1, 1), 0.0)
        inverse[rows, :] = jnp.where(total > 0.0, 1.0 / (DIAG * jnp.where(total > 0.0, total, 1.0)), 0.0)
        return carry

    lax.fori_loop(1, EX, plane, 0, unroll=2)


QUANTITIES = 7


def operator_pass(field, young, yb, begin, end, finish, carry0, rows_above):
    lane = lax.broadcasted_iota(jnp.int32, (8, NZ), 1)
    not_last, not_first = lane < NZ - 1, lane > 0
    r0 = yb * 8

    def transform(x):
        out = []
        for c in range(3):
            at = c * SIZE + x * EY + r0
            v = field[pl.ds(at, 8), :]
            u = field[pl.ds(at + 1, 8), :]
            modes = []
            for t in (v + u, u - v):
                n = jnp.where(not_last, pltpu.roll(t, NZ - 1, 1), 0.0)
                modes += [t + n, n - t]
            out += modes
        return out

    def step(x, state):
        a, held, carry = state
        b = transform(x + 1)
        e1 = young[pl.ds(x * EY + r0, 8), :] * (MU / 16.0)
        e3 = e1 * (1.0 / 3.0)
        e31 = e1 * 0.5
        e9 = e1 * ((RATIO + 4.0) / 9.0)
        s = [p + q for p, q in zip(a, b)]
        d = [q - p for p, q in zip(a, b)]
        u = lambda c, p, q, r: (d if p else s)[4 * c + 2 * q + r]
        g = {}
        ux, uy, uz = u(0, 1, 0, 0), u(1, 0, 1, 0), u(2, 0, 0, 1)
        trace = RATIO * (ux + uy + uz)
        g[0, 1, 0, 0] = e1 * ((ux + ux) + trace)
        g[1, 0, 1, 0] = e1 * ((uy + uy) + trace)
        g[2, 0, 0, 1] = e1 * ((uz + uz) + trace)
        g[0, 0, 1, 0] = g[1, 1, 0, 0] = e1 * (u(0, 0, 1, 0) + u(1, 1, 0, 0))
        g[0, 0, 0, 1] = g[2, 1, 0, 0] = e1 * (u(0, 0, 0, 1) + u(2, 1, 0, 0))
        g[1, 0, 0, 1] = g[2, 0, 1, 0] = e1 * (u(1, 0, 0, 1) + u(2, 0, 1, 0))
        for one, two in (
            ((0, 1, 0, 1), (1, 0, 1, 1)),
            ((0, 1, 1, 0), (2, 0, 1, 1)),
            ((1, 1, 1, 0), (2, 1, 0, 1)),
        ):
            p, q = u(*one), u(*two)
            g[one] = e31 * (3.0 * p + q)
            g[two] = e31 * (3.0 * q + p)
        p, q, r = u(0, 0, 1, 1), u(1, 1, 0, 1), u(2, 1, 1, 0)
        total = p + q + r
        g[0, 0, 1, 1] = e3 * (p + total)
        g[1, 1, 0, 1] = e3 * (q + total)
        g[2, 1, 1, 0] = e3 * (r + total)
        for c in range(3):
            g[c, 1, 1, 1] = e9 * u(c, 1, 1, 1)
        forces, kept = [], []
        for c in range(3):
            f = []
            for q in range(2):
                for r in range(2):
                    one = g[c, 1, q, r]
                    h = held[4 * c + 2 * q + r]
                    if q == 0 and r == 0:
                        f.append(h - one)
                        kept.append(one)
                    else:
                        zero = g[c, 0, q, r]
                        f.append((zero - one) + h)
                        kept.append(zero + one)
            h = []
            for q in range(2):
                low, high = f[2 * q], f[2 * q + 1]
                h.append((low - high) + jnp.where(not_first, pltpu.roll(low + high, 1, 1), 0.0))
            at = (c * EX + x) * 48 + 8 + r0
            rows_above[pl.ds(at, 8), :] = h[0] + h[1]
            forces.append((h[0] - h[1]) + rows_above[pl.ds(at - 1, 8), :])
        return b, kept, finish(x, forces, carry)

    zeros = [jnp.zeros((8, NZ), f32)] * 12
    state = (transform(begin), zeros, carry0)
    return lax.fori_loop(begin, end, step, state)[2]


def main_kernel(
    r, fixed, ylo, yhi, xlo, xhi, young, inverse,
    z_out, y_out, dots_out,
    field, free, load, image, second, above,
):
    def clear(i, carry):
        rows = pl.ds(pl.multiple_of(i * EY, 8), EY)
        zero = jnp.zeros((EY, NZ), f32)
        load[rows, :] = zero
        free[rows, :] = zero
        second[rows, :] = zero
        return carry

    lax.fori_loop(0, 3 * EX, clear, 0)
    for ref in (field, second):
        ref[pl.ds(3 * SIZE, 8), :] = jnp.zeros((8, NZ), f32)

    def own(i, carry):
        c = i // NX
        x = i - c * NX
        src = pl.ds(pl.multiple_of(i * NY, NY), NY)
        dst = pl.ds(c * SIZE + (x + CF) * EY + CF, NY)
        load[dst, :] = r[src, :]
        free[dst, :] = jnp.where(fixed[src, :] == 0, 1.0, 0.0)
        return carry

    lax.fori_loop(0, 3 * NX, own, 0)
    for c in range(3):
        for k in range(2):
            for strip, row in ((ylo, 2 + k), (yhi, 36 + k)):
                load[pl.ds(c * SIZE + CF * EY + row, NX, stride=EY), :] = strip[
                    pl.ds((c * 2 + k) * NX, NX), :
                ]
            for plane, x in ((xlo, 2 + k), (xhi, 20 + k)):
                load[pl.ds(c * SIZE + x * EY, EY), :] = plane[pl.ds((c * 2 + k) * EY, EY), :]
        for strip, row in ((ylo, 3), (yhi, 36)):
            free[pl.ds(c * SIZE + CF * EY + row, NX, stride=EY), :] = strip[pl.ds((6 + c) * NX, NX), :]
        for plane, x in ((xlo, 3), (xhi, 20)):
            free[pl.ds(c * SIZE + x * EY, EY), :] = plane[pl.ds((6 + c) * EY, EY), :]

    def scale(i, carry):
        c = i // EX
        rows = pl.ds(pl.multiple_of(i * EY, 8), EY)
        field[rows, :] = load[rows, :] * inverse[pl.ds(pl.multiple_of((i - c * EX) * EY, 8), EY), :]
        return carry

    lax.fori_loop(0, 3 * EX, scale, 0)

    zero = jnp.zeros((8, NZ), f32)
    row = lax.broadcasted_iota(jnp.int32, (8, NZ), 0)

    def clear_above(i, carry):
        above[pl.ds(pl.multiple_of(i * 48, 8), 8), :] = zero
        return carry

    lax.fori_loop(0, 3 * EX, clear_above, 0)

    def block_one(yb, dots):
        r0 = yb * 8
        own_row = (row + r0 >= CF) & (row + r0 < CF + NY)

        def finish(x, forces, dots):
            keep = jnp.where(own_row & (x >= CF) & (x < CF + NX), 1.0, 0.0)
            inv = inverse[pl.ds(x * EY + r0, 8), :]
            sums = [zero] * 5
            for c in range(3):
                at = pl.ds(c * SIZE + x * EY + r0, 8)
                w = free[at, :] * forces[c]
                y = w * inv
                z = field[at, :]
                rr = load[at, :]
                zt = z - y
                rt = rr - w
                second[at, :] = zt
                image[at, :] = w
                for k, t in enumerate((z * rr, z * w, y * w, z * rt, zt * rt)):
                    sums[k] = sums[k] + t
            return [d + keep * s for d, s in zip(dots, sums)]

        return operator_pass(field, young, yb, 2, 21, finish, dots, above)

    dots = lax.fori_loop(0, 5, block_one, [zero] * 5)

    def block_two(yb, dots):
        r0 = yb * 8
        own_row = (row + r0 >= CF) & (row + r0 < CF + NY)

        def finish(x, forces, dots):
            keep = jnp.where(own_row & (x >= CF), 1.0, 0.0)
            sums = [zero] * 2
            for c in range(3):
                at = pl.ds(c * SIZE + x * EY + r0, 8)
                q = free[at, :] * forces[c]
                w = image[at, :]
                zt = second[at, :]
                z = field[at, :]
                sums[0] = sums[0] + zt * q
                sums[1] = sums[1] + (z - zt) * (w - q)
            return [d + keep * s for d, s in zip(dots, sums)]

        return operator_pass(second, young, yb, 3, 20, finish, dots, above)

    dots = dots + lax.fori_loop(0, 5, block_two, [zero] * 2)

    def copy_out(i, carry):
        c = i // NX
        x = i - c * NX
        src = pl.ds(c * SIZE + (x + CF) * EY + CF, NY)
        dst = pl.ds(pl.multiple_of(i * NY, NY), NY)
        z = field[src, :]
        z_out[dst, :] = z
        y_out[dst, :] = z - second[src, :]
        return carry

    lax.fori_loop(0, 3 * NX, copy_out, 0)
    lane = lax.broadcasted_iota(jnp.int32, (1, NZ), 1)
    line = jnp.zeros((1, NZ), f32)
    for k, d in enumerate(dots):
        line = jnp.where(lane == k, jnp.sum(d), line)
    dots_out[...] = line


def final_kernel(parts, z, y, out):
    total = jnp.sum(parts[...], axis=0, keepdims=True)
    lane = lax.broadcasted_iota(jnp.int32, (1, NZ), 1)
    rz, zw, yw, a, b, c, d = (
        jnp.sum(jnp.where(lane == k, total, 0.0), axis=1, keepdims=True) for k in range(QUANTITIES)
    )
    alpha = rz / zw
    far = zw < 0.5 * rz
    less = -(a / zw)
    rz1 = jnp.where(far, alpha * (alpha * yw) - rz, alpha * (alpha * b + less * a))
    energy = jnp.where(
        far,
        zw - 2.0 * alpha * yw + alpha * (alpha * d),
        less * (less * zw) + 2.0 * alpha * (less * (a - b)) + alpha * (alpha * c),
    )
    beta = rz1 / rz
    curve = energy - beta * (rz1 / alpha)
    alpha1 = rz1 / curve
    c1 = alpha + alpha1 * (1.0 + beta)
    c2 = -(alpha * alpha1)
    c1 = jnp.broadcast_to(c1, (8, NZ))[0:1, :]
    c2 = jnp.broadcast_to(c2, (8, NZ))[0:1, :]

    def body(i, carry):
        rows = pl.ds(pl.multiple_of(i * NY, NY), NY)
        out[rows, :] = c1 * z[rows, :] + c2 * y[rows, :]
        return carry

    lax.fori_loop(0, 3 * NX, body, 0, unroll=4)


def per_device(
    body_force, fixed_dofs, load_nodes, load_forces, frequencies,
    hidden_weights, hidden_biases, output_weights, output_bias,
):
    bx, by = lax.axis_index("gx"), lax.axis_index("gy")
    ids = jnp.stack([bx, by]).astype(jnp.int32)
    rows = 3 * NX * NY
    body = body_force.reshape(rows, NZ)
    fixed = fixed_dofs.reshape(rows, NZ)
    nodes = load_nodes.T
    strip = shape(9 * NX, NZ)
    r, ylo_send, yhi_send = call(
        pack_kernel, (shape(rows, NZ), strip, strip),
        [SMEM, SMEM, SMEM, VMEM, VMEM, VMEM],
        (ids, nodes, load_forces, body, fixed, nodes),
        cost=pl.CostEstimate(flops=400000, transcendentals=0, bytes_accessed=2400000),
    )
    ny, nx = lax.axis_size("gy"), lax.axis_size("gx")
    up_y = [(i, i + 1) for i in range(ny - 1)]
    down_y = [(i + 1, i) for i in range(ny - 1)]
    up_x = [(i, i + 1) for i in range(nx - 1)]
    down_x = [(i + 1, i) for i in range(nx - 1)]
    ylo = lax.ppermute(yhi_send, "gy", up_y)
    yhi = lax.ppermute(ylo_send, "gy", down_y)

    coarse = call(
        mlp_kernel, shape(GX, 16, 128),
        [SMEM, VMEM, VMEM, VMEM, VMEM, SMEM],
        (ids, frequencies, hidden_weights, hidden_biases, output_weights.reshape(1, 128), output_bias),
        scratch=[VMEM((16 * GX, 128), f32), VMEM((16 * GX, 128), f32), VMEM((3, 256, 256), jnp.bfloat16)],
        cost=pl.CostEstimate(flops=1500000000, transcendentals=800000, bytes_accessed=300000),
    )
    plane = shape(9 * EY, NZ)
    xlo_send, xhi_send = call(
        planes_kernel, (plane, plane), [VMEM] * 4, (r, fixed, ylo, yhi),
    )
    xlo = lax.ppermute(xhi_send, "gx", up_x)
    xhi = lax.ppermute(xlo_send, "gx", down_x)
    young, inverse, density = call(
        density_kernel, (shape(SIZE, NZ), shape(SIZE, NZ), shape(NX * NY, NZ)),
        [SMEM, VMEM], (ids, coarse),
        cost=pl.CostEstimate(flops=8000000, transcendentals=0, bytes_accessed=1300000),
    )
    z, y, dots = call(
        main_kernel, (shape(rows, NZ), shape(rows, NZ), shape(1, NZ)),
        [VMEM] * 8, (r, fixed, ylo, yhi, xlo, xhi, young, inverse),
        scratch=[VMEM((3 * SIZE + 8, NZ), f32), VMEM((3 * SIZE, NZ), f32), VMEM((3 * SIZE, NZ), f32),
                 VMEM((3 * SIZE, NZ), f32), VMEM((3 * SIZE + 8, NZ), f32), VMEM((3 * EX * 48, NZ), f32)],
    )
    parts = lax.all_to_all(
        jnp.broadcast_to(dots, (nx * ny, NZ)), ("gx", "gy"), 0, 0, tiled=True
    )
    out = call(final_kernel, shape(rows, NZ), [VMEM] * 3, (parts, z, y))
    return out.reshape(3, NX, NY, NZ), density.reshape(NX, NY, NZ)


def solution(mesh):
    return jax.shard_map(
        per_device,
        mesh=mesh,
        in_specs=(P(None, "gx", "gy", None), P(None, "gx", "gy", None)) + (P(),) * 7,
        out_specs=(P(None, "gx", "gy", None), P("gx", "gy", None)),
        check_vma=False,
    )
```

```python
import functools
import math

import jax
import jax.numpy as jnp
from jax import lax
from jax.experimental import pallas as pl
from jax.experimental.pallas import tpu as pltpu
from jax.sharding import PartitionSpec as P

CF = 4
NX, NY, NZ = 16, 32, 128
TOTAL_X, TOTAL_Y = 512, 256
CX, CY, CZ = NX // CF, NY // CF, NZ // CF
GX, GY = CX + 2, CY + 2
EX, EY = GX * CF, GY * CF
SIZE = EX * EY
LOADS = 512
NU, MU = 0.3, 1.0 / 2.6
LAM = 0.3 / (1.3 * 0.4)
RATIO = LAM / MU
DIAG = (LAM + 4.0 * MU) / 9.0
VMEM = pltpu.VMEM
SMEM = pltpu.SMEM
highest = lax.Precision.HIGHEST
f32 = jnp.float32


def spec(space=VMEM):
    return pl.BlockSpec(memory_space=space)


def call(kernel, out_shape, in_spaces, args, scratch=(), cost=None):
    return pl.pallas_call(
        kernel,
        out_shape=out_shape,
        in_specs=[spec(s) for s in in_spaces],
        out_specs=jax.tree.map(lambda _: spec(), out_shape),
        scratch_shapes=list(scratch),
        compiler_params=pltpu.CompilerParams(vmem_limit_bytes=48 << 20),
        cost_estimate=cost,
    )(*args)


def shape(*dims):
    return jax.ShapeDtypeStruct(dims, f32)


def pack_kernel(ids, nodes_s, forces_s, body, fixed, nodes_v, r_out, lo_out, hi_out):
    start_x = ids[0] * NX
    start_y = ids[1] * NY
    r_out[...] = body[...]
    lx = nodes_v[0:1, :] - start_x
    ly = nodes_v[1:2, :] - start_y
    mine = (lx >= 0) & (lx < NX) & (ly >= 0) & (ly < NY)
    index = lax.broadcasted_iota(jnp.int32, (1, LOADS), 1)
    todo = jnp.where(mine, index, LOADS)
    lane = lax.broadcasted_iota(jnp.int32, (1, NZ), 1)

    def more(p):
        return p < LOADS

    def add_one(p):
        x = nodes_s[0, p] - start_x
        y = nodes_s[1, p] - start_y
        hit = lane == nodes_s[2, p]
        for c in range(3):
            row = pl.ds((c * NX + x) * NY + y, 1)
            r_out[row, :] = r_out[row, :] + jnp.where(hit, forces_s[c, p], 0.0)
        return jnp.min(jnp.where(todo > p, todo, LOADS))

    lax.while_loop(more, add_one, jnp.min(todo))

    def mask(i, carry):
        rows = pl.ds(pl.multiple_of(i * NY, NY), NY)
        r_out[rows, :] = jnp.where(fixed[rows, :] == 0, r_out[rows, :], 0.0)
        return carry

    lax.fori_loop(0, 3 * NX, mask, 0, unroll=4)
    for c in range(3):
        for j in range(2):
            lo_out[pl.ds((c * 2 + j) * NX, NX), :] = r_out[pl.ds(c * NX * NY + j, NX, stride=NY), :]
            hi_out[pl.ds((c * 2 + j) * NX, NX), :] = r_out[
                pl.ds(c * NX * NY + NY - 2 + j, NX, stride=NY), :
            ]
        free = fixed[pl.ds(c * NX * NY, NX, stride=NY), :] == 0
        lo_out[pl.ds((6 + c) * NX, NX), :] = jnp.where(free, 1.0, 0.0)
        free = fixed[pl.ds(c * NX * NY + NY - 1, NX, stride=NY), :] == 0
        hi_out[pl.ds((6 + c) * NX, NX), :] = jnp.where(free, 1.0, 0.0)


def planes_kernel(r, fixed, ylo, yhi, lo_out, hi_out):
    for out, first in ((lo_out, 0), (hi_out, NX - 2)):
        out[...] = jnp.zeros_like(out)
        for c in range(3):
            for j in range(2):
                x = first + j
                base = (c * 2 + j) * EY
                out[pl.ds(base + 4, NY), :] = r[pl.ds((c * NX + x) * NY, NY), :]
                for k in range(2):
                    out[pl.ds(base + 2 + k, 1), :] = ylo[pl.ds((c * 2 + k) * NX + x, 1), :]
                    out[pl.ds(base + 36 + k, 1), :] = yhi[pl.ds((c * 2 + k) * NX + x, 1), :]
            x = 0 if first == 0 else NX - 1
            base = (6 + c) * EY
            free = fixed[pl.ds((c * NX + x) * NY, NY), :] == 0
            out[pl.ds(base + 4, NY), :] = jnp.where(free, 1.0, 0.0)
            out[pl.ds(base + 3, 1), :] = ylo[pl.ds((6 + c) * NX + x, 1), :]
            out[pl.ds(base + 36, 1), :] = yhi[pl.ds((6 + c) * NX + x, 1), :]


def split2(v):
    hi = v.astype(jnp.bfloat16)
    return hi, (v - hi.astype(f32)).astype(jnp.bfloat16)


def sigmoid(v):
    return 1.0 / (1.0 + jnp.exp(-v))


def mlp_kernel(ids, freq, weights, biases, wout, bout, coarse, axy, bxy, w2):
    cx0 = ids[0] * CX - 1
    cy0 = ids[1] * CY - 1
    f = freq[...]
    ff = jnp.concatenate([f, f], axis=1)
    quarter = jnp.where(lax.broadcasted_iota(jnp.int32, (1, 128), 1) < 64, 0.0, 0.25)

    def waves(row, coords):
        turns = ff[row : row + 1, :] * coords
        turns = turns - jnp.round(turns)
        wave = jnp.sin((turns + quarter) * (2.0 * math.pi))
        other = jnp.sin((turns + (0.25 - quarter)) * (2.0 * math.pi))
        return wave, other

    def coords(start, rows, total):
        i = lax.broadcasted_iota(jnp.int32, (rows, 128), 0) + start
        return (i.astype(f32) + 0.5) * (1.0 / total)

    first = lax.broadcasted_iota(jnp.int32, (1, 128), 1) < 64
    wx, ox = waves(0, coords(cx0, 8, TOTAL_X // CF))
    wy, oy = waves(1, coords(cy0, 16, TOTAL_Y // CF))
    wz, oz = waves(2, coords(0, CZ, CZ))
    cosx, sinx = jnp.where(first, ox, wx), jnp.where(first, wx, ox)
    cosz, sinz = jnp.where(first, oz, wz), jnp.where(first, wz, oz)
    turnedy = jnp.where(first, oy, -oy)
    cosy, siny = jnp.where(first, oy, wy), jnp.where(first, wy, oy)
    for i in range(GX):
        both = wy * cosx[i : i + 1, :] + turnedy * sinx[i : i + 1, :]
        axy[pl.ds(16 * i, 16), :] = both
        c = cosy * cosx[i : i + 1, :] - siny * sinx[i : i + 1, :]
        s = siny * cosx[i : i + 1, :] + cosy * sinx[i : i + 1, :]
        bxy[pl.ds(16 * i, 16), :] = jnp.where(first, c, -s)

    for l in range(3):
        hi, lo = split2(weights[l])
        both = jnp.concatenate([hi, lo], axis=1)
        w2[l] = jnp.concatenate([both, both], axis=0)

    rows = GY * CZ
    wrow = jnp.broadcast_to(wout[...], (16, 128))
    ri = lax.broadcasted_iota(jnp.int32, (16, rows), 0)
    li = lax.broadcasted_iota(jnp.int32, (16, rows), 1)
    pick = (li // CZ) == ((ri + 1) & 15)
    ui = lax.broadcasted_iota(jnp.int32, (rows, 128), 0)
    uj = lax.broadcasted_iota(jnp.int32, (rows, 128), 1)
    up = jnp.where((ui & (CZ - 1)) == (uj // CF), 1.0, 0.0)

    def body(i, carry):
        parts = []
        for j in range(GY):
            a = axy[pl.ds(16 * i + j, 1), :]
            b = bxy[pl.ds(16 * i + j, 1), :]
            parts.append(a * cosz + b * sinz)
        h = jnp.concatenate(parts, axis=0)
        for l in range(3):
            hi, lo = split2(h)
            both = jnp.concatenate([hi, lo], axis=1)
            out = jnp.dot(both, w2[l], preferred_element_type=f32)
            v = out[:, :128] + out[:, 128:] + biases[l : l + 1, :]
            h = v * sigmoid(v)
        logits = lax.dot_general(
            wrow, h, (((1,), (1,)), ((), ())), precision=highest, preferred_element_type=f32
        )
        picked = jnp.where(pick, logits, 0.0)
        wide = jnp.dot(picked, up, precision=highest, preferred_element_type=f32)
        coarse[i] = sigmoid(wide + bout[0])
        return carry

    lax.fori_loop(0, GX, body, 0)


W0, W1, W2, W3 = 2.0, 1.0, 2.0 - math.sqrt(2.0), 2.0 - math.sqrt(3.0)


def density_kernel(ids, coarse, young, inverse, density):
    lane = lax.broadcasted_iota(jnp.int32, (16, NZ), 1)
    not_last, not_first = lane < NZ - 1, lane > 0
    y_cell = ids[1] * CY + jnp.where(
        lax.broadcasted_iota(jnp.int32, (16, NZ), 0) == 15,
        -1,
        lax.broadcasted_iota(jnp.int32, (16, NZ), 0),
    )
    inside_y = (y_cell >= 0) & (y_cell < TOTAL_Y // CF)

    def layers(v):
        side = jnp.where(not_last, pltpu.roll(v, NZ - 1, 1), 0.0) + jnp.where(
            not_first, pltpu.roll(v, 1, 1), 0.0
        )
        return W0 * v + W1 * side, W1 * v + W2 * side, W2 * v + W3 * side

    zero = jnp.zeros((16, NZ), f32)
    values, insides = [], []
    for i in range(GX):
        x_cell = ids[0] * CX - 1 + i
        ok = inside_y & (x_cell >= 0) & (x_cell < TOTAL_X // CF)
        insides.append(jnp.where(ok, 1.0, 0.0))
        values.append(jnp.where(ok, coarse[i], 0.0))
    stacks = [[layers(v) for v in group] for group in (values, insides)]

    for i in range(GX):
        for kind in range(3):
            low = max(i - 1, 0) if kind == 0 else i
            high = min(i + 1, GX - 1) if kind == 2 else i
            sums = []
            for stack in stacks:
                t0 = stack[i][0] + (stack[low][1] + stack[high][1])
                t1 = stack[i][1] + (stack[low][2] + stack[high][2])
                down = pltpu.roll(t1, 1, 0)
                above = pltpu.roll(t1, 15, 0)
                sums.append((t0 + (down + t1), t0 + (t1 + t1), t0 + (t1 + above)))
            planes = {0: (0,), 1: (1, 2), 2: (3,)}[kind]
            for row_kind in range(3):
                count = sums[1][row_kind]
                inside = insides[i] > 0.0
                rho = sums[0][row_kind] / jnp.where(inside, count, 1.0)
                modulus = jnp.where(inside, 0.02 + 0.98 * (rho * rho * rho), 0.0)
                for ox in planes:
                    x = i * CF + ox
                    for oy in {0: (0,), 1: (1, 2), 2: (3,)}[row_kind]:
                        young[pl.ds(x * EY + CF + oy, 8, stride=CF), :] = modulus[0:8, :]
                        young[pl.ds(x * EY + 36 + oy, 1), :] = modulus[8:9, :]
                        young[pl.ds(x * EY + oy, 1), :] = modulus[15:16, :]
                        if 1 <= i <= CX:
                            density[pl.ds((x - CF) * NY + oy, 8, stride=CF), :] = rho[0:8, :]

    lane8 = lax.broadcasted_iota(jnp.int32, (EY, NZ), 1) > 0
    inverse[pl.ds(0, EY), :] = jnp.zeros((EY, NZ), f32)

    def plane(x, carry):
        rows = pl.ds(pl.multiple_of(x * EY, 8), EY)
        before = pl.ds(pl.multiple_of((x - 1) * EY, 8), EY)
        total = young[rows, :] + young[before, :]
        total = total + pltpu.roll(total, 1, 0)
        total = total + jnp.where(lane8, pltpu.roll(total, 1, 1), 0.0)
        inverse[rows, :] = jnp.where(total > 0.0, 1.0 / (DIAG * jnp.where(total > 0.0, total, 1.0)), 0.0)
        return carry

    lax.fori_loop(1, EX, plane, 0, unroll=2)


QUANTITIES = 7
BLOCKS = EY // 8
TALL = EY + 8


def operator_pass(zsum, zdiff, young, above, minus, plus, begin, end, unroll):
    def block(yb, carry):
        r0 = yb * 8

        def transform(x):
            out = []
            for c in range(3):
                at = c * SIZE + x * EY + r0
                pairs = [(t[pl.ds(at, 8), :], t[pl.ds(at + 1, 8), :]) for t in (zsum, zdiff)]
                out += [v + u for v, u in pairs] + [u - v for v, u in pairs]
            return out

        def modal(x, a, b):
            e1 = young[pl.ds(x * EY + r0, 8), :] * (MU / 16.0)
            e3 = e1 * (1.0 / 3.0)
            e31 = e1 * 0.5
            e9 = e1 * ((RATIO + 4.0) / 9.0)
            s = [p + q for p, q in zip(a, b)]
            d = [q - p for p, q in zip(a, b)]
            u = lambda c, p, q, r: (d if p else s)[4 * c + 2 * q + r]
            g = {}
            ux, uy, uz = u(0, 1, 0, 0), u(1, 0, 1, 0), u(2, 0, 0, 1)
            trace = RATIO * (ux + uy + uz)
            g[0, 1, 0, 0] = e1 * ((ux + ux) + trace)
            g[1, 0, 1, 0] = e1 * ((uy + uy) + trace)
            g[2, 0, 0, 1] = e1 * ((uz + uz) + trace)
            g[0, 0, 1, 0] = g[1, 1, 0, 0] = e1 * (u(0, 0, 1, 0) + u(1, 1, 0, 0))
            g[0, 0, 0, 1] = g[2, 1, 0, 0] = e1 * (u(0, 0, 0, 1) + u(2, 1, 0, 0))
            g[1, 0, 0, 1] = g[2, 0, 1, 0] = e1 * (u(1, 0, 0, 1) + u(2, 0, 1, 0))
            for one, two in (
                ((0, 1, 0, 1), (1, 0, 1, 1)),
                ((0, 1, 1, 0), (2, 0, 1, 1)),
                ((1, 1, 1, 0), (2, 1, 0, 1)),
            ):
                p, q = u(*one), u(*two)
                g[one] = e31 * (3.0 * p + q)
                g[two] = e31 * (3.0 * q + p)
            p, q, r = u(0, 0, 1, 1), u(1, 1, 0, 1), u(2, 1, 1, 0)
            total = p + q + r
            g[0, 0, 1, 1] = e3 * (p + total)
            g[1, 1, 0, 1] = e3 * (q + total)
            g[2, 1, 1, 0] = e3 * (r + total)
            for c in range(3):
                g[c, 1, 1, 1] = e9 * u(c, 1, 1, 1)
            return g

        def keep(g):
            out = []
            for c in range(3):
                out.append(g[c, 1, 0, 0])
                for q, r in ((0, 1), (1, 0), (1, 1)):
                    out.append(g[c, 0, q, r] + g[c, 1, q, r])
            return out

        def step(x, state):
            a, held = state
            b = transform(x + 1)
            g = modal(x, a, b)
            for c in range(3):
                f = [held[4 * c] - g[c, 1, 0, 0]]
                for k, (q, r) in enumerate(((0, 1), (1, 0), (1, 1))):
                    f.append((g[c, 0, q, r] - g[c, 1, q, r]) + held[4 * c + 1 + k])
                h = []
                for r in range(2):
                    at = ((2 * c + r) * EX + x) * TALL + 8 + r0
                    above[pl.ds(at, 8), :] = f[r] + f[2 + r]
                    h.append((f[r] - f[2 + r]) + above[pl.ds(at - 1, 8), :])
                rows = pl.ds(pl.multiple_of(c * SIZE + x * EY + r0, 8), 8)
                minus[rows, :] = h[0] - h[1]
                plus[rows, :] = h[0] + h[1]
            return b, keep(g)

        a = transform(begin)
        b = transform(begin + 1)
        lax.fori_loop(begin + 1, end, step, (b, keep(modal(begin, a, b))), unroll=unroll)
        return carry

    lax.fori_loop(0, BLOCKS, block, 0)


def main_kernel(
    r, fixed, ylo, yhi, xlo, xhi, young, inverse,
    field, scaled, dots_out,
    free, load, image, zsum, zdiff, above, minus, plus,
):
    zero = jnp.zeros((8, NZ), f32)
    lane = lax.broadcasted_iota(jnp.int32, (8, NZ), 1)
    not_last, not_first = lane < NZ - 1, lane > 0

    def own(i, carry):
        c = i // NX
        x = i - c * NX
        src = pl.ds(pl.multiple_of(i * NY, NY), NY)
        base = pl.multiple_of(c * SIZE + (x + CF) * EY, 8)
        for ref in (load, free):
            ref[pl.ds(base, 8), :] = zero
            ref[pl.ds(base + EY - 8, 8), :] = zero
        load[pl.ds(base + CF, NY), :] = r[src, :]
        free[pl.ds(base + CF, NY), :] = jnp.where(fixed[src, :] == 0, 1.0, 0.0)
        return carry

    lax.fori_loop(0, 3 * NX, own, 0, unroll=2)
    for c in range(3):
        for k in range(2):
            for strip, row in ((ylo, 2 + k), (yhi, 36 + k)):
                load[pl.ds(c * SIZE + CF * EY + row, NX, stride=EY), :] = strip[
                    pl.ds((c * 2 + k) * NX, NX), :
                ]
            for plane, x in ((xlo, 2 + k), (xhi, 20 + k)):
                load[pl.ds(c * SIZE + x * EY, EY), :] = plane[pl.ds((c * 2 + k) * EY, EY), :]
        for strip, row in ((ylo, 3), (yhi, 36)):
            free[pl.ds(c * SIZE + CF * EY + row, NX, stride=EY), :] = strip[pl.ds((6 + c) * NX, NX), :]
        for plane, x in ((xlo, 3), (xhi, 20)):
            free[pl.ds(c * SIZE + x * EY, EY), :] = plane[pl.ds((6 + c) * EY, EY), :]
    for ref in (zsum, zdiff):
        ref[pl.ds(3 * SIZE, 8), :] = zero

    def z_stage(at, v):
        n = jnp.where(not_last, pltpu.roll(v, NZ - 1, 1), 0.0)
        zsum[at, :] = v + n
        zdiff[at, :] = n - v

    def prepare(x, carry):
        for j in range(BLOCKS):
            base = pl.multiple_of(x * EY, 8) + 8 * j
            inv = inverse[pl.ds(base, 8), :]
            for c in range(3):
                at = pl.ds(base + c * SIZE, 8)
                v = load[at, :] * inv
                field[at, :] = v
                z_stage(at, v)
        return carry

    lax.fori_loop(2, 22, prepare, 0)

    for c in range(3):
        for ref in (zsum, zdiff):
            ref[pl.ds(c * SIZE + 22 * EY, 8), :] = zero

    def clear_above(i, carry):
        above[pl.ds(pl.multiple_of(i * TALL, 8), 8), :] = zero
        return carry

    lax.fori_loop(0, 6 * EX, clear_above, 0, unroll=8)

    operator_pass(zsum, zdiff, young, above, minus, plus, 2, 21, 3)

    row = lax.broadcasted_iota(jnp.int32, (8, NZ), 0)
    first_rows = jnp.where(row >= CF, 1.0, 0.0)
    last_rows = jnp.where(row < CF, 1.0, 0.0)

    def gather(totals, j, terms):
        for k, t in enumerate(terms):
            if j == 0:
                t = t * first_rows
            if j == BLOCKS - 1:
                t = t * last_rows
            totals[k] = t if totals[k] is None else totals[k] + t

    def force(at):
        return minus[at, :] + jnp.where(not_first, pltpu.roll(plus[at, :], 1, 1), 0.0)

    def finish_one(x, dots):
        totals = [None] * 5
        for j in range(BLOCKS):
            base = pl.multiple_of(x * EY, 8) + 8 * j
            inv = inverse[pl.ds(base, 8), :]
            sums = None
            for c in range(3):
                at = pl.ds(base + c * SIZE, 8)
                w = free[at, :] * force(at)
                y = w * inv
                z = field[at, :]
                zt = z - y
                scaled[at, :] = y
                image[at, :] = w
                z_stage(at, zt)
                if dots is not None:
                    rr = load[at, :]
                    rt = rr - w
                    terms = (z * rr, z * w, y * w, z * rt, zt * rt)
                    sums = terms if sums is None else [p + q for p, q in zip(sums, terms)]
            if dots is not None:
                gather(totals, j, sums)
        return dots if dots is None else [p + q for p, q in zip(dots, totals)]

    finish_one(CF - 1, None)
    finish_one(CF + NX, None)
    dots = lax.fori_loop(CF, CF + NX, finish_one, [zero] * 5)

    operator_pass(zsum, zdiff, young, above, minus, plus, 3, 20, 4)

    def finish_two(x, dots):
        totals = [None] * 2
        for j in range(BLOCKS):
            base = pl.multiple_of(x * EY, 8) + 8 * j
            sums = None
            for c in range(3):
                at = pl.ds(base + c * SIZE, 8)
                q = free[at, :] * force(at)
                y = scaled[at, :]
                terms = ((field[at, :] - y) * q, y * (image[at, :] - q))
                sums = terms if sums is None else [a + b for a, b in zip(sums, terms)]
            gather(totals, j, sums)
        return [p + q for p, q in zip(dots, totals)]

    dots = dots + lax.fori_loop(CF, CF + NX, finish_two, [zero] * 2)
    one = lax.broadcasted_iota(jnp.int32, (1, NZ), 1)
    line = jnp.zeros((1, NZ), f32)
    for k, d in enumerate(dots):
        line = jnp.where(one == k, jnp.sum(d), line)
    dots_out[...] = line


def final_kernel(parts, z, y, out):
    total = jnp.sum(parts[...], axis=0, keepdims=True)
    lane = lax.broadcasted_iota(jnp.int32, (1, NZ), 1)
    rz, zw, yw, a, b, c, d = (
        jnp.sum(jnp.where(lane == k, total, 0.0), axis=1, keepdims=True) for k in range(QUANTITIES)
    )
    alpha = rz / zw
    far = zw < 0.5 * rz
    less = -(a / zw)
    rz1 = jnp.where(far, alpha * (alpha * yw) - rz, alpha * (alpha * b + less * a))
    energy = jnp.where(
        far,
        zw - 2.0 * alpha * yw + alpha * (alpha * d),
        less * (less * zw) + 2.0 * alpha * (less * (a - b)) + alpha * (alpha * c),
    )
    beta = rz1 / rz
    curve = energy - beta * (rz1 / alpha)
    alpha1 = rz1 / curve
    c1 = alpha + alpha1 * (1.0 + beta)
    c2 = -(alpha * alpha1)
    c1 = jnp.broadcast_to(c1, (8, NZ))[0:1, :]
    c2 = jnp.broadcast_to(c2, (8, NZ))[0:1, :]

    def body(i, carry):
        c = i // NX
        src = pl.ds(c * SIZE + (i - c * NX + CF) * EY + CF, NY)
        out[pl.ds(pl.multiple_of(i * NY, NY), NY), :] = c1 * z[src, :] + c2 * y[src, :]
        return carry

    lax.fori_loop(0, 3 * NX, body, 0, unroll=4)


def per_device(
    body_force, fixed_dofs, load_nodes, load_forces, frequencies,
    hidden_weights, hidden_biases, output_weights, output_bias,
):
    bx, by = lax.axis_index("gx"), lax.axis_index("gy")
    ids = jnp.stack([bx, by]).astype(jnp.int32)
    rows = 3 * NX * NY
    body = body_force.reshape(rows, NZ)
    fixed = fixed_dofs.reshape(rows, NZ)
    nodes = load_nodes.T
    strip = shape(9 * NX, NZ)
    r, ylo_send, yhi_send = call(
        pack_kernel, (shape(rows, NZ), strip, strip),
        [SMEM, SMEM, SMEM, VMEM, VMEM, VMEM],
        (ids, nodes, load_forces, body, fixed, nodes),
        cost=pl.CostEstimate(flops=400000, transcendentals=0, bytes_accessed=2400000),
    )
    ny, nx = lax.axis_size("gy"), lax.axis_size("gx")
    up_y = [(i, i + 1) for i in range(ny - 1)]
    down_y = [(i + 1, i) for i in range(ny - 1)]
    up_x = [(i, i + 1) for i in range(nx - 1)]
    down_x = [(i + 1, i) for i in range(nx - 1)]
    ylo = lax.ppermute(yhi_send, "gy", up_y)
    yhi = lax.ppermute(ylo_send, "gy", down_y)

    coarse = call(
        mlp_kernel, shape(GX, 16, 128),
        [SMEM, VMEM, VMEM, VMEM, VMEM, SMEM],
        (ids, frequencies, hidden_weights, hidden_biases, output_weights.reshape(1, 128), output_bias),
        scratch=[VMEM((16 * GX, 128), f32), VMEM((16 * GX, 128), f32), VMEM((3, 256, 256), jnp.bfloat16)],
        cost=pl.CostEstimate(flops=1500000000, transcendentals=800000, bytes_accessed=300000),
    )
    plane = shape(9 * EY, NZ)
    xlo_send, xhi_send = call(
        planes_kernel, (plane, plane), [VMEM] * 4, (r, fixed, ylo, yhi),
    )
    xlo = lax.ppermute(xhi_send, "gx", up_x)
    xhi = lax.ppermute(xlo_send, "gx", down_x)
    young, inverse, density = call(
        density_kernel, (shape(SIZE, NZ), shape(SIZE, NZ), shape(NX * NY, NZ)),
        [SMEM, VMEM], (ids, coarse),
        cost=pl.CostEstimate(flops=8000000, transcendentals=0, bytes_accessed=1300000),
    )
    ext = VMEM((3 * SIZE, NZ), f32)
    tail = VMEM((3 * SIZE + 8, NZ), f32)
    z, y, dots = call(
        main_kernel, (shape(3 * SIZE, NZ), shape(3 * SIZE, NZ), shape(1, NZ)),
        [VMEM] * 8, (r, fixed, ylo, yhi, xlo, xhi, young, inverse),
        scratch=[ext, ext, ext, tail, tail, VMEM((6 * EX * TALL, NZ), f32), ext, ext],
    )
    parts = lax.all_to_all(
        jnp.broadcast_to(dots, (nx * ny, NZ)), ("gx", "gy"), 0, 0, tiled=True
    )
    out = call(final_kernel, shape(rows, NZ), [VMEM] * 3, (parts, z, y))
    return out.reshape(3, NX, NY, NZ), density.reshape(NX, NY, NZ)


def solution(mesh):
    return jax.shard_map(
        per_device,
        mesh=mesh,
        in_specs=(P(None, "gx", "gy", None), P(None, "gx", "gy", None)) + (P(),) * 7,
        out_specs=(P(None, "gx", "gy", None), P("gx", "gy", None)),
        check_vma=False,
    )
```

```python
import functools
import math

import jax
import jax.numpy as jnp
from jax import lax
from jax.experimental import pallas as pl
from jax.experimental.pallas import tpu as pltpu
from jax.sharding import PartitionSpec as P

CF = 4
NX, NY, NZ = 16, 32, 128
TOTAL_X, TOTAL_Y = 512, 256
CX, CY, CZ = NX // CF, NY // CF, NZ // CF
GX, GY = CX + 2, CY + 2
EX, EY = GX * CF, GY * CF
SIZE = EX * EY
LOADS = 512
NU, MU = 0.3, 1.0 / 2.6
LAM = 0.3 / (1.3 * 0.4)
RATIO = LAM / MU
DIAG = (LAM + 4.0 * MU) / 9.0
VMEM = pltpu.VMEM
SMEM = pltpu.SMEM
highest = lax.Precision.HIGHEST
f32 = jnp.float32


def spec(space=VMEM):
    return pl.BlockSpec(memory_space=space)


def call(kernel, out_shape, in_spaces, args, scratch=(), cost=None, out_spaces=None, aliases=None, limit=16):
    out_specs = jax.tree.map(lambda _: spec(), out_shape)
    if out_spaces is not None:
        out_specs = jax.tree.map(lambda _, space: spec(space), out_shape, out_spaces)
    args = [
        pltpu.with_memory_space_constraint(a, space) if space is pltpu.HBM else a
        for a, space in zip(args, in_spaces)
    ]
    if out_spaces is not None:
        out_shape = jax.tree.map(
            lambda a, space: pltpu.HBM(a.shape, a.dtype) if space is pltpu.HBM else a, out_shape, out_spaces
        )
    return pl.pallas_call(
        kernel,
        out_shape=out_shape,
        in_specs=[spec(s) for s in in_spaces],
        out_specs=out_specs,
        scratch_shapes=list(scratch),
        input_output_aliases=aliases or {},
        compiler_params=pltpu.CompilerParams(vmem_limit_bytes=limit << 20),
        cost_estimate=cost,
    )(*args)


def shape(*dims):
    return jax.ShapeDtypeStruct(dims, f32)


def pack_kernel(
    ids, nodes, forces, body, fixed,
    load, free, lo_out, hi_out,
    body_v, fixed_v, nodes_v, nodes_s, forces_s, sem,
):
    part = NX * NY
    copies = [
        pltpu.make_async_copy(nodes, nodes_v, sem.at[0]),
        pltpu.make_async_copy(nodes, nodes_s, sem.at[1]),
        pltpu.make_async_copy(forces, forces_s, sem.at[2]),
    ]
    for c in range(3):
        for k, (src, dst) in enumerate(((body, body_v), (fixed, fixed_v))):
            rows = pl.ds(c * part, part)
            copies.append(pltpu.make_async_copy(src.at[rows, :], dst.at[rows, :], sem.at[3 + 2 * c + k]))
    for copy in copies:
        copy.start()

    zero = jnp.zeros((8, NZ), f32)

    def clear(x, carry):
        for c in range(3):
            base = pl.multiple_of(c * SIZE + x * EY, 8)
            for ref in (load, free):
                ref[pl.ds(base, 8), :] = zero
                ref[pl.ds(base + EY - 8, 8), :] = zero
        return carry

    lax.fori_loop(CF, CF + NX, clear, 0, unroll=2)

    start_x = ids[0] * NX
    start_y = ids[1] * NY
    for copy in copies[:3]:
        copy.wait()
    lx = nodes_v[0:1, :] - start_x
    ly = nodes_v[1:2, :] - start_y
    mine = (lx >= 0) & (lx < NX) & (ly >= 0) & (ly < NY)
    index = lax.broadcasted_iota(jnp.int32, (1, LOADS), 1)
    todo = jnp.where(mine, index, LOADS)
    lane = lax.broadcasted_iota(jnp.int32, (1, NZ), 1)
    first = jnp.min(todo)
    for copy in copies[3:]:
        copy.wait()

    def more(p):
        return p < LOADS

    def add_one(p):
        x = nodes_s[0, p] - start_x
        y = nodes_s[1, p] - start_y
        hit = lane == nodes_s[2, p]
        for c in range(3):
            row = pl.ds((c * NX + x) * NY + y, 1)
            body_v[row, :] = body_v[row, :] + jnp.where(hit, forces_s[c, p], 0.0)
        return jnp.min(jnp.where(todo > p, todo, LOADS))

    lax.while_loop(more, add_one, first)

    def mask(x, carry):
        for c in range(3):
            src = pl.ds(pl.multiple_of((c * NX + x) * NY, NY), NY)
            dst = pl.ds(c * SIZE + (x + CF) * EY + CF, NY)
            ok = fixed_v[src, :] == 0
            load[dst, :] = jnp.where(ok, body_v[src, :], 0.0)
            free[dst, :] = jnp.where(ok, 1.0, 0.0)
        return carry

    lax.fori_loop(0, NX, mask, 0, unroll=2)
    for c in range(3):
        base = c * SIZE + CF * EY + CF
        for j in range(2):
            to = pl.ds((c * 2 + j) * NX, NX)
            lo_out[to, :] = load[pl.ds(base + j, NX, stride=EY), :]
            hi_out[to, :] = load[pl.ds(base + NY - 2 + j, NX, stride=EY), :]
        to = pl.ds((6 + c) * NX, NX)
        lo_out[to, :] = free[pl.ds(base, NX, stride=EY), :]
        hi_out[to, :] = free[pl.ds(base + NY - 1, NX, stride=EY), :]


def planes_kernel(load, free, ylo, yhi, coarse, lo_out, hi_out):
    del coarse
    for out, first in ((lo_out, CF), (hi_out, CF + NX - 2)):
        for c in range(3):
            for j in range(2):
                x = first + j
                base = (c * 2 + j) * EY
                out[pl.ds(base, EY), :] = load[pl.ds(c * SIZE + x * EY, EY), :]
                for k in range(2):
                    at = pl.ds((c * 2 + k) * NX + x - CF, 1)
                    out[pl.ds(base + 2 + k, 1), :] = ylo[at, :]
                    out[pl.ds(base + 36 + k, 1), :] = yhi[at, :]
            x = CF if first == CF else CF + NX - 1
            base = (6 + c) * EY
            out[pl.ds(base, EY), :] = free[pl.ds(c * SIZE + x * EY, EY), :]
            at = pl.ds((6 + c) * NX + x - CF, 1)
            out[pl.ds(base + 3, 1), :] = ylo[at, :]
            out[pl.ds(base + 36, 1), :] = yhi[at, :]


def split2(v):
    hi = v.astype(jnp.bfloat16)
    return hi, (v - hi.astype(f32)).astype(jnp.bfloat16)


def doubled(w):
    hi, lo = split2(w)
    both = jnp.concatenate([hi, lo], axis=1)
    return jnp.concatenate([both, both], axis=0)


def sine_of_turns(t):
    t = t - jnp.round(t)
    a = jnp.abs(t)
    x = jnp.minimum(a, 0.5 - a) * (2.0 * math.pi)
    x2 = x * x
    p = 1.0 / 6227020800.0
    for k in (39916800.0, 362880.0, 5040.0, 120.0, 6.0, 1.0):
        p = 1.0 / k - x2 * p
    p = x * p
    return jnp.where(t < 0.0, -p, p)


GROUP = 3


def mlp_kernel(ids, freq, weights, biases, wout, bout, coarse, axy, bxy, w2):
    cx0 = ids[0] * CX - 1
    cy0 = ids[1] * CY - 1
    f = freq[...]
    ff = jnp.concatenate([f, f], axis=1)
    first = lax.broadcasted_iota(jnp.int32, (1, 128), 1) < 64
    quarter = jnp.where(first, 0.0, 0.25)

    def waves(row, start, rows, total):
        i = lax.broadcasted_iota(jnp.int32, (rows, 128), 0) + start
        turns = ff[row : row + 1, :] * ((i.astype(f32) + 0.5) * (1.0 / total))
        turns = turns - jnp.round(turns)
        wave = sine_of_turns(turns + quarter)
        return wave, pltpu.roll(wave, 64, 1)

    wx, ox = waves(0, cx0, 8, TOTAL_X // CF)
    wy, oy = waves(1, cy0, 16, TOTAL_Y // CF)
    wz, oz = waves(2, 0, CZ, CZ)
    cosx, sinx = jnp.where(first, ox, wx), jnp.where(first, wx, ox)
    cosz, sinz = jnp.where(first, oz, wz), jnp.where(first, wz, oz)
    turnedy = jnp.where(first, oy, -oy)
    for i in range(GX):
        c, s = cosx[i : i + 1, :], sinx[i : i + 1, :]
        axy[pl.ds(16 * i, 16), :] = wy * c + turnedy * s
        bxy[pl.ds(16 * i, 16), :] = turnedy * c - wy * s

    for l in range(3):
        w2[l] = doubled(weights[l] * 0.5)
    w2[3] = doubled(jnp.broadcast_to(wout[...], (128, 128)).T)
    pick = lax.broadcasted_iota(jnp.int32, (CZ, 128), 0) == (
        lax.broadcasted_iota(jnp.int32, (CZ, 128), 1) // CF
    )
    row16 = lax.broadcasted_iota(jnp.int32, (16, 128), 0)

    def body(i, carry):
        parts = []
        for k in range(GROUP):
            for j in range(GY):
                at = pl.ds(16 * (GROUP * i + k) + j, 1)
                parts.append(axy[at, :] * cosz + bxy[at, :] * sinz)
        h = jnp.concatenate(parts, axis=0)
        for l in range(4):
            hi, lo = split2(h)
            both = jnp.concatenate([hi, lo], axis=1)
            out = jnp.dot(both, w2[l], preferred_element_type=f32)
            h = out[:, :128] + out[:, 128:]
            if l < 3:
                h = h + biases[l : l + 1, :] * 0.5
                h = h + h * jnp.tanh(h)
        for k in range(GROUP):
            logits = jnp.zeros((16, 128), f32)
            for j in range(GY):
                cell = (k * GY + j) * CZ
                line = jnp.sum(jnp.where(pick, h[cell : cell + CZ, :], 0.0), axis=0, keepdims=True)
                logits = jnp.where(row16 == (j + 15) % 16, line, logits)
            coarse[GROUP * i + k] = 1.0 / (1.0 + jnp.exp(-(logits + bout[0])))
        return carry

    lax.fori_loop(0, GX // GROUP, body, 0)


W0, W1, W2, W3 = 2.0, 1.0, 2.0 - math.sqrt(2.0), 2.0 - math.sqrt(3.0)
SCALE = MU / 16.0


def density_kernel(ids, coarse, young, inverse, density, density_v, sem):
    lane = lax.broadcasted_iota(jnp.int32, (16, NZ), 1)
    not_last, not_first = lane < NZ - 1, lane > 0
    row16 = lax.broadcasted_iota(jnp.int32, (16, NZ), 0)
    y_cell = ids[1] * CY + jnp.where(row16 == 15, -1, row16)
    inside_y = (y_cell >= 0) & (y_cell < TOTAL_Y // CF)

    ri = lax.broadcasted_iota(jnp.int32, (EY + NY, 144), 0)
    ci = lax.broadcasted_iota(jnp.int32, (EY + NY, 144), 1)
    r = jnp.where(ri < EY, ri, ri - EY + CF)
    oy = r & 3
    kind = jnp.where(oy == 0, 0, jnp.where(oy == 3, 2, 1))
    want = kind * 16 + (((r >> 2) + 15) & 15)
    spread = jnp.where(
        (ci == want) | (ci == want + 48) | (ci == want + 96), 1.0, 0.0
    ).astype(jnp.bfloat16)
    y_fine = ids[1] * NY - CF + lax.broadcasted_iota(jnp.int32, (EY, NZ), 0)
    inside_rows = jnp.where((y_fine >= 0) & (y_fine < TOTAL_Y), SCALE, 0.0)

    def layers(v):
        side = jnp.where(not_last, pltpu.roll(v, NZ - 1, 1), 0.0) + jnp.where(
            not_first, pltpu.roll(v, 1, 1), 0.0
        )
        return W0 * v + W1 * side, W1 * v + W2 * side, W2 * v + W3 * side

    side = jnp.where(not_last, 1.0, 0.0) + jnp.where(not_first, 1.0, 0.0)
    ones = (W0 + W1 * side, W1 + W2 * side, W2 + W3 * side)
    rows_in = jnp.where(inside_y, 1.0, 0.0)
    stacks = []
    for i in range(GX):
        x_cell = ids[0] * CX - 1 + i
        ok_x = (x_cell >= 0) & (x_cell < TOTAL_X // CF)
        inside = jnp.where(inside_y & ok_x, 1.0, 0.0)
        stacks.append((
            layers(jnp.where(inside > 0.0, coarse[i], 0.0)),
            [inside * w for w in ones],
            inside > 0.0,
            jnp.where(ok_x, 1.0, 0.0),
        ))

    for i in range(GX):
        for plane_kind in range(3):
            low = max(i - 1, 0) if plane_kind == 0 else i
            high = min(i + 1, GX - 1) if plane_kind == 2 else i
            sums = []
            for which in range(2):
                here, below, over = stacks[i][which], stacks[low][which], stacks[high][which]
                t0 = here[0] + (below[1] + over[1])
                t1 = here[1] + (below[2] + over[2])
                down = pltpu.roll(t1, 1, 0)
                above = pltpu.roll(t1, 15, 0)
                sums.append((t0 + (down + t1), t0 + (t1 + t1), t0 + (t1 + above)))
            rho = jnp.concatenate(
                [a / jnp.where(stacks[i][2], b, 1.0) for a, b in zip(*sums)], axis=0
            )
            hi = rho.astype(jnp.bfloat16)
            rest = rho - hi.astype(f32)
            mid = rest.astype(jnp.bfloat16)
            lo = (rest - mid.astype(f32)).astype(jnp.bfloat16)
            fine = jnp.dot(spread, jnp.concatenate([hi, mid, lo], axis=0), preferred_element_type=f32)
            ext = fine[:EY, :]
            modulus = (0.02 + 0.98 * (ext * ext * ext)) * (inside_rows * stacks[i][3])
            for ox in {0: (0,), 1: (1, 2), 2: (3,)}[plane_kind]:
                x = i * CF + ox
                young[pl.ds(x * EY, EY), :] = modulus
                if 1 <= i <= CX:
                    density_v[pl.ds((x - CF) * NY, NY), :] = fine[EY:, :]

    copy = pltpu.make_async_copy(density_v, density, sem)
    copy.start()
    lane8 = lax.broadcasted_iota(jnp.int32, (8, NZ), 1) > 0

    def plane(x, carry):
        for j in range(EY // 8):
            at = x * EY + 8 * j
            if j == 0:
                at = pl.multiple_of(at, 8)
            total = (young[pl.ds(at, 8), :] + young[pl.ds(at - 1, 8), :]) + (
                young[pl.ds(at - EY, 8), :] + young[pl.ds(at - EY - 1, 8), :]
            )
            total = total + jnp.where(lane8, pltpu.roll(total, 1, 1), 0.0)
            inverse[pl.ds(at, 8), :] = 1.0 / (DIAG / SCALE * total + 1e-30)
        return carry

    lax.fori_loop(2, 22, plane, 0, unroll=2)
    copy.wait()


QUANTITIES = 4
BLOCKS = EY // 8
TALL = EY + 8


def operator_pass(zsum, zdiff, young, above, minus, plus, begin, end, unroll):
    def block(yb, carry):
        r0 = yb * 8

        def transform(x):
            out = []
            for c in range(3):
                at = c * SIZE + x * EY + r0
                pairs = [(t[pl.ds(at, 8), :], t[pl.ds(at + 1, 8), :]) for t in (zsum, zdiff)]
                out += [v + u for v, u in pairs] + [u - v for v, u in pairs]
            return out

        def modal(x, a, b):
            e1 = young[pl.ds(pl.multiple_of(x * EY + r0, 8), 8), :]
            e3 = e1 * (1.0 / 3.0)
            e31 = e1 * 0.5
            e9 = e1 * ((RATIO + 4.0) / 9.0)
            s = [p + q for p, q in zip(a, b)]
            d = [q - p for p, q in zip(a, b)]
            u = lambda c, p, q, r: (d if p else s)[4 * c + 2 * q + r]
            g = {}
            ux, uy, uz = u(0, 1, 0, 0), u(1, 0, 1, 0), u(2, 0, 0, 1)
            trace = RATIO * (ux + uy + uz)
            g[0, 1, 0, 0] = e1 * ((ux + ux) + trace)
            g[1, 0, 1, 0] = e1 * ((uy + uy) + trace)
            g[2, 0, 0, 1] = e1 * ((uz + uz) + trace)
            g[0, 0, 1, 0] = g[1, 1, 0, 0] = e1 * (u(0, 0, 1, 0) + u(1, 1, 0, 0))
            g[0, 0, 0, 1] = g[2, 1, 0, 0] = e1 * (u(0, 0, 0, 1) + u(2, 1, 0, 0))
            g[1, 0, 0, 1] = g[2, 0, 1, 0] = e1 * (u(1, 0, 0, 1) + u(2, 0, 1, 0))
            for one, two in (
                ((0, 1, 0, 1), (1, 0, 1, 1)),
                ((0, 1, 1, 0), (2, 0, 1, 1)),
                ((1, 1, 1, 0), (2, 1, 0, 1)),
            ):
                p, q = u(*one), u(*two)
                g[one] = e31 * (3.0 * p + q)
                g[two] = e31 * (3.0 * q + p)
            p, q, r = u(0, 0, 1, 1), u(1, 1, 0, 1), u(2, 1, 1, 0)
            total = p + q + r
            g[0, 0, 1, 1] = e3 * (p + total)
            g[1, 1, 0, 1] = e3 * (q + total)
            g[2, 1, 1, 0] = e3 * (r + total)
            for c in range(3):
                g[c, 1, 1, 1] = e9 * u(c, 1, 1, 1)
            return g

        def keep(g):
            out = []
            for c in range(3):
                out.append(g[c, 1, 0, 0])
                for q, r in ((0, 1), (1, 0), (1, 1)):
                    out.append(g[c, 0, q, r] + g[c, 1, q, r])
            return out

        def step(x, state):
            a, held = state
            b = transform(x + 1)
            g = modal(x, a, b)
            for c in range(3):
                f = [held[4 * c] - g[c, 1, 0, 0]]
                for k, (q, r) in enumerate(((0, 1), (1, 0), (1, 1))):
                    f.append((g[c, 0, q, r] - g[c, 1, q, r]) + held[4 * c + 1 + k])
                h = []
                for r in range(2):
                    at = ((2 * c + r) * EX + x) * TALL + 8 + r0
                    above[pl.ds(at, 8), :] = f[r] + f[2 + r]
                    h.append((f[r] - f[2 + r]) + above[pl.ds(at - 1, 8), :])
                rows = pl.ds(pl.multiple_of(c * SIZE + x * EY + r0, 8), 8)
                minus[rows, :] = h[0] - h[1]
                plus[rows, :] = h[0] + h[1]
            return b, keep(g)

        a = transform(begin)
        b = transform(begin + 1)
        lax.fori_loop(begin + 1, end, step, (b, keep(modal(begin, a, b))), unroll=unroll)
        return carry

    lax.fori_loop(0, BLOCKS, block, 0)


def main_kernel(
    load_in, free_in, ylo, yhi, xlo, xhi, young, inverse,
    load, free, field, scaled, dots_out,
    zsum, zdiff, above, minus, plus,
):
    del load_in, free_in
    zero = jnp.zeros((8, NZ), f32)
    lane = lax.broadcasted_iota(jnp.int32, (8, NZ), 1)
    not_last, not_first = lane < NZ - 1, lane > 0

    for c in range(3):
        for k in range(2):
            for strip, row in ((ylo, 2 + k), (yhi, 36 + k)):
                load[pl.ds(c * SIZE + CF * EY + row, NX, stride=EY), :] = strip[
                    pl.ds((c * 2 + k) * NX, NX), :
                ]
            for plane, x in ((xlo, 2 + k), (xhi, 20 + k)):
                load[pl.ds(c * SIZE + x * EY, EY), :] = plane[pl.ds((c * 2 + k) * EY, EY), :]
        for strip, row in ((ylo, 3), (yhi, 36)):
            free[pl.ds(c * SIZE + CF * EY + row, NX, stride=EY), :] = strip[pl.ds((6 + c) * NX, NX), :]
        for plane, x in ((xlo, 3), (xhi, 20)):
            free[pl.ds(c * SIZE + x * EY, EY), :] = plane[pl.ds((6 + c) * EY, EY), :]
    for ref in (zsum, zdiff):
        ref[pl.ds(3 * SIZE, 8), :] = zero

    def z_stage(at, v):
        n = jnp.where(not_last, pltpu.roll(v, NZ - 1, 1), 0.0)
        zsum[at, :] = v + n
        zdiff[at, :] = n - v

    def prepare(x, carry):
        for j in range(BLOCKS):
            base = pl.multiple_of(x * EY, 8) + 8 * j
            inv = inverse[pl.ds(base, 8), :]
            for c in range(3):
                at = pl.ds(base + c * SIZE, 8)
                v = load[at, :] * inv
                field[at, :] = v
                z_stage(at, v)
        return carry

    lax.fori_loop(2, 22, prepare, 0, unroll=2)

    for c in range(3):
        for ref in (zsum, zdiff):
            ref[pl.ds(c * SIZE + 22 * EY, 8), :] = zero

    def clear_above(i, carry):
        above[pl.ds(pl.multiple_of(i * TALL, 8), 8), :] = zero
        return carry

    lax.fori_loop(0, 6 * EX, clear_above, 0, unroll=8)

    operator_pass(zsum, zdiff, young, above, minus, plus, 2, 21, 3)

    row = lax.broadcasted_iota(jnp.int32, (8, NZ), 0)
    first_rows = jnp.where(row >= CF, 1.0, 0.0)
    last_rows = jnp.where(row < CF, 1.0, 0.0)

    def gather(totals, j, terms):
        for k, t in enumerate(terms):
            if j == 0:
                t = t * first_rows
            if j == BLOCKS - 1:
                t = t * last_rows
            totals[k] = t if totals[k] is None else totals[k] + t

    def force(at):
        return minus[at, :] + jnp.where(not_first, pltpu.roll(plus[at, :], 1, 1), 0.0)

    def finish_one(x, dots):
        totals = [None] * 3
        for j in range(BLOCKS):
            base = pl.multiple_of(x * EY, 8) + 8 * j
            inv = inverse[pl.ds(base, 8), :]
            sums = None
            for c in range(3):
                at = pl.ds(base + c * SIZE, 8)
                w = free[at, :] * force(at)
                y = w * inv
                z = field[at, :]
                zt = z - y
                scaled[at, :] = y
                z_stage(at, zt)
                if dots is not None:
                    rt = load[at, :] - w
                    terms = (z * w, z * rt, zt * rt)
                    sums = terms if sums is None else [p + q for p, q in zip(sums, terms)]
            if dots is not None:
                gather(totals, j, sums)
        return dots if dots is None else [p + q for p, q in zip(dots, totals)]

    finish_one(CF - 1, None)
    finish_one(CF + NX, None)
    dots = lax.fori_loop(CF, CF + NX, finish_one, [zero] * 3, unroll=2)

    operator_pass(zsum, zdiff, young, above, minus, plus, 3, 20, 4)

    def finish_two(x, dots):
        totals = [None] * 1
        for j in range(BLOCKS):
            base = pl.multiple_of(x * EY, 8) + 8 * j
            sums = None
            for c in range(3):
                at = pl.ds(base + c * SIZE, 8)
                q = free[at, :] * force(at)
                terms = ((field[at, :] - scaled[at, :]) * q,)
                sums = terms if sums is None else [a + b for a, b in zip(sums, terms)]
            gather(totals, j, sums)
        return [p + q for p, q in zip(dots, totals)]

    dots = dots + lax.fori_loop(CF, CF + NX, finish_two, [zero], unroll=2)
    one = lax.broadcasted_iota(jnp.int32, (1, NZ), 1)
    line = jnp.zeros((1, NZ), f32)
    for k, d in enumerate(dots):
        line = jnp.where(one == k, jnp.sum(d), line)
    dots_out[...] = line


def final_kernel(parts, z, y, out, out_v, sem):
    total = jnp.sum(parts[...], axis=0, keepdims=True)
    lane = lax.broadcasted_iota(jnp.int32, (1, NZ), 1)
    zw, a, b, c = (
        jnp.sum(jnp.where(lane == k, total, 0.0), axis=1, keepdims=True) for k in range(QUANTITIES)
    )
    rz = zw + a
    alpha = rz / zw
    less = -(a / zw)
    rz1 = alpha * (alpha * b + less * a)
    energy = less * (less * zw) + 2.0 * alpha * (less * (a - b)) + alpha * (alpha * c)
    beta = rz1 / rz
    alpha1 = rz1 / (energy - beta * (rz1 / alpha))
    c1 = jnp.broadcast_to(alpha + alpha1 * (1.0 + beta), (8, NZ))[0:1, :]
    c2 = jnp.broadcast_to(-(alpha * alpha1), (8, NZ))[0:1, :]
    copies = []
    for c in range(3):
        def body(x, carry, c=c):
            src = pl.ds(c * SIZE + (x + CF) * EY + CF, NY)
            to = pl.ds(pl.multiple_of((c * NX + x) * NY, NY), NY)
            out_v[to, :] = c1 * z[src, :] + c2 * y[src, :]
            return carry

        lax.fori_loop(0, NX, body, 0, unroll=4)
        rows = pl.ds(c * NX * NY, NX * NY)
        copy = pltpu.make_async_copy(out_v.at[rows, :], out.at[rows, :], sem.at[c])
        copy.start()
        copies.append(copy)
    for copy in copies:
        copy.wait()


def per_device(
    body_force, fixed_dofs, load_nodes, load_forces, frequencies,
    hidden_weights, hidden_biases, output_weights, output_bias,
):
    bx, by = lax.axis_index("gx"), lax.axis_index("gy")
    ids = jnp.stack([bx, by]).astype(jnp.int32)
    rows = 3 * NX * NY
    body = body_force.reshape(rows, NZ)
    fixed = fixed_dofs.reshape(rows, NZ)
    nodes = load_nodes.T
    strip = shape(9 * NX, NZ)
    ext = shape(3 * SIZE, NZ)
    load, free, ylo_send, yhi_send = call(
        pack_kernel, (ext, ext, strip, strip),
        [SMEM] + [pltpu.HBM] * 4, (ids, nodes, load_forces, body, fixed),
        scratch=[VMEM((rows, NZ), f32), VMEM((rows, NZ), jnp.int32), VMEM((3, LOADS), jnp.int32),
                 SMEM((3, LOADS), jnp.int32), SMEM((3, LOADS), f32), pltpu.SemaphoreType.DMA((9,))],
        cost=pl.CostEstimate(flops=400000, transcendentals=0, bytes_accessed=2400000),
    )
    ny, nx = lax.axis_size("gy"), lax.axis_size("gx")
    up_y = [(i, i + 1) for i in range(ny - 1)]
    down_y = [(i + 1, i) for i in range(ny - 1)]
    up_x = [(i, i + 1) for i in range(nx - 1)]
    down_x = [(i + 1, i) for i in range(nx - 1)]
    ylo = lax.ppermute(yhi_send, "gy", up_y)
    yhi = lax.ppermute(ylo_send, "gy", down_y)

    coarse = call(
        mlp_kernel, shape(GX, 16, 128),
        [SMEM, VMEM, VMEM, VMEM, VMEM, SMEM],
        (ids, frequencies, hidden_weights, hidden_biases, output_weights.reshape(1, 128), output_bias),
        scratch=[VMEM((16 * GX, 128), f32), VMEM((16 * GX, 128), f32), VMEM((4, 256, 256), jnp.bfloat16)],
        cost=pl.CostEstimate(flops=1500000000, transcendentals=800000, bytes_accessed=300000),
    )
    plane = shape(9 * EY, NZ)
    xlo_send, xhi_send = call(
        planes_kernel, (plane, plane), [VMEM] * 5, (load, free, ylo, yhi, coarse),
    )
    xlo = lax.ppermute(xhi_send, "gx", up_x)
    xhi = lax.ppermute(xlo_send, "gx", down_x)
    young, inverse, density = call(
        density_kernel, (shape(SIZE, NZ), shape(SIZE, NZ), shape(NX * NY, NZ)),
        [SMEM, VMEM], (ids, coarse),
        scratch=[VMEM((NX * NY, NZ), f32), pltpu.SemaphoreType.DMA],
        out_spaces=(VMEM, VMEM, pltpu.HBM),
        cost=pl.CostEstimate(flops=8000000, transcendentals=0, bytes_accessed=1300000),
    )
    tail = VMEM((3 * SIZE + 8, NZ), f32)
    work = VMEM((3 * SIZE, NZ), f32)
    _, _, z, y, dots = call(
        main_kernel, (ext, ext, ext, ext, shape(1, NZ)),
        [VMEM] * 8, (load, free, ylo, yhi, xlo, xhi, young, inverse),
        scratch=[tail, tail, VMEM((6 * EX * TALL, NZ), f32), work, work],
        aliases={0: 0, 1: 1}, limit=20,
    )
    parts = lax.all_to_all(
        jnp.broadcast_to(dots, (nx * ny, NZ)), ("gx", "gy"), 0, 0, tiled=True
    )
    out = call(
        final_kernel, shape(rows, NZ), [VMEM] * 3, (parts, z, y),
        scratch=[VMEM((rows, NZ), f32), pltpu.SemaphoreType.DMA((3,))], out_spaces=pltpu.HBM,
    )
    return out.reshape(3, NX, NY, NZ), density.reshape(NX, NY, NZ)


def solution(mesh):
    return jax.shard_map(
        per_device,
        mesh=mesh,
        in_specs=(P(None, "gx", "gy", None), P(None, "gx", "gy", None)) + (P(),) * 7,
        out_specs=(P(None, "gx", "gy", None), P("gx", "gy", None)),
        check_vma=False,
    )
```

```python
import functools
import math

import jax
import jax.numpy as jnp
from jax import lax
from jax.experimental import pallas as pl
from jax.experimental.pallas import tpu as pltpu
from jax.sharding import PartitionSpec as P

CF = 4
NX, NY, NZ = 16, 32, 128
TOTAL_X, TOTAL_Y = 512, 256
CX, CY, CZ = NX // CF, NY // CF, NZ // CF
GX, GY = CX + 2, CY + 2
EX, EY = GX * CF, GY * CF
SIZE = EX * EY
LOADS = 512
NU, MU = 0.3, 1.0 / 2.6
LAM = 0.3 / (1.3 * 0.4)
RATIO = LAM / MU
DIAG = (LAM + 4.0 * MU) / 9.0
VMEM = pltpu.VMEM
SMEM = pltpu.SMEM
highest = lax.Precision.HIGHEST
f32 = jnp.float32


def spec(space=VMEM):
    return pl.BlockSpec(memory_space=space)


def call(kernel, out_shape, in_spaces, args, scratch=(), cost=None, out_spaces=None, aliases=None, limit=16):
    out_specs = jax.tree.map(lambda _: spec(), out_shape)
    if out_spaces is not None:
        out_specs = jax.tree.map(lambda _, space: spec(space), out_shape, out_spaces)
    args = [
        pltpu.with_memory_space_constraint(a, space) if space is pltpu.HBM else a
        for a, space in zip(args, in_spaces)
    ]
    if out_spaces is not None:
        out_shape = jax.tree.map(
            lambda a, space: pltpu.HBM(a.shape, a.dtype) if space is pltpu.HBM else a, out_shape, out_spaces
        )
    return pl.pallas_call(
        kernel,
        out_shape=out_shape,
        in_specs=[spec(s) for s in in_spaces],
        out_specs=out_specs,
        scratch_shapes=list(scratch),
        input_output_aliases=aliases or {},
        compiler_params=pltpu.CompilerParams(vmem_limit_bytes=limit << 20),
        cost_estimate=cost,
    )(*args)


def shape(*dims):
    return jax.ShapeDtypeStruct(dims, f32)


def pack_kernel(
    ids, nodes, forces, body, fixed,
    load, free, lo_out, hi_out,
    body_v, fixed_v, nodes_v, nodes_s, forces_s, sem,
):
    part = NX * NY
    copies = [
        pltpu.make_async_copy(nodes, nodes_v, sem.at[0]),
        pltpu.make_async_copy(nodes, nodes_s, sem.at[1]),
        pltpu.make_async_copy(forces, forces_s, sem.at[2]),
    ]
    for c in range(3):
        for k, (src, dst) in enumerate(((body, body_v), (fixed, fixed_v))):
            rows = pl.ds(c * part, part)
            copies.append(pltpu.make_async_copy(src.at[rows, :], dst.at[rows, :], sem.at[3 + 2 * c + k]))
    for copy in copies:
        copy.start()

    zero = jnp.zeros((8, NZ), f32)

    def clear(x, carry):
        for c in range(3):
            base = pl.multiple_of(c * SIZE + x * EY, 8)
            for ref in (load, free):
                ref[pl.ds(base, 8), :] = zero
                ref[pl.ds(base + EY - 8, 8), :] = zero
        return carry

    lax.fori_loop(CF, CF + NX, clear, 0, unroll=2)

    start_x = ids[0] * NX
    start_y = ids[1] * NY
    for copy in copies[:3]:
        copy.wait()
    lx = nodes_v[0:1, :] - start_x
    ly = nodes_v[1:2, :] - start_y
    mine = (lx >= 0) & (lx < NX) & (ly >= 0) & (ly < NY)
    index = lax.broadcasted_iota(jnp.int32, (1, LOADS), 1)
    todo = jnp.where(mine, index, LOADS)
    lane = lax.broadcasted_iota(jnp.int32, (1, NZ), 1)
    first = jnp.min(todo)
    for copy in copies[3:]:
        copy.wait()

    def more(p):
        return p < LOADS

    def add_one(p):
        x = nodes_s[0, p] - start_x
        y = nodes_s[1, p] - start_y
        hit = lane == nodes_s[2, p]
        for c in range(3):
            row = pl.ds((c * NX + x) * NY + y, 1)
            body_v[row, :] = body_v[row, :] + jnp.where(hit, forces_s[c, p], 0.0)
        return jnp.min(jnp.where(todo > p, todo, LOADS))

    lax.while_loop(more, add_one, first)

    def mask(x, carry):
        for c in range(3):
            src = pl.ds(pl.multiple_of((c * NX + x) * NY, NY), NY)
            dst = pl.ds(c * SIZE + (x + CF) * EY + CF, NY)
            ok = fixed_v[src, :] == 0
            load[dst, :] = jnp.where(ok, body_v[src, :], 0.0)
            free[dst, :] = jnp.where(ok, 1.0, 0.0)
        return carry

    lax.fori_loop(0, NX, mask, 0, unroll=2)
    for c in range(3):
        base = c * SIZE + CF * EY + CF
        for j in range(2):
            to = pl.ds((c * 2 + j) * NX, NX)
            lo_out[to, :] = load[pl.ds(base + j, NX, stride=EY), :]
            hi_out[to, :] = load[pl.ds(base + NY - 2 + j, NX, stride=EY), :]
        to = pl.ds((6 + c) * NX, NX)
        lo_out[to, :] = free[pl.ds(base, NX, stride=EY), :]
        hi_out[to, :] = free[pl.ds(base + NY - 1, NX, stride=EY), :]


def planes_kernel(load, free, ylo, yhi, coarse, lo_out, hi_out):
    del coarse
    for out, first in ((lo_out, CF), (hi_out, CF + NX - 2)):
        for c in range(3):
            for j in range(2):
                x = first + j
                base = (c * 2 + j) * EY
                out[pl.ds(base, EY), :] = load[pl.ds(c * SIZE + x * EY, EY), :]
                for k in range(2):
                    at = pl.ds((c * 2 + k) * NX + x - CF, 1)
                    out[pl.ds(base + 2 + k, 1), :] = ylo[at, :]
                    out[pl.ds(base + 36 + k, 1), :] = yhi[at, :]
            x = CF if first == CF else CF + NX - 1
            base = (6 + c) * EY
            out[pl.ds(base, EY), :] = free[pl.ds(c * SIZE + x * EY, EY), :]
            at = pl.ds((6 + c) * NX + x - CF, 1)
            out[pl.ds(base + 3, 1), :] = ylo[at, :]
            out[pl.ds(base + 36, 1), :] = yhi[at, :]


def split2(v):
    hi = v.astype(jnp.bfloat16)
    return hi, (v - hi.astype(f32)).astype(jnp.bfloat16)


def doubled(w):
    hi, lo = split2(w)
    both = jnp.concatenate([hi, lo], axis=1)
    return jnp.concatenate([both, both], axis=0)


def sine_of_turns(t):
    t = t - jnp.round(t)
    a = jnp.abs(t)
    x = jnp.minimum(a, 0.5 - a) * (2.0 * math.pi)
    x2 = x * x
    p = 1.0 / 6227020800.0
    for k in (39916800.0, 362880.0, 5040.0, 120.0, 6.0, 1.0):
        p = 1.0 / k - x2 * p
    p = x * p
    return jnp.where(t < 0.0, -p, p)


GROUP = 3


def mlp_kernel(ids, freq, weights, biases, wout, bout, coarse, axy, bxy, w2):
    cx0 = ids[0] * CX - 1
    cy0 = ids[1] * CY - 1
    f = freq[...]
    ff = jnp.concatenate([f, f], axis=1)
    first = lax.broadcasted_iota(jnp.int32, (1, 128), 1) < 64
    quarter = jnp.where(first, 0.0, 0.25)

    def waves(row, start, rows, total):
        i = lax.broadcasted_iota(jnp.int32, (rows, 128), 0) + start
        turns = ff[row : row + 1, :] * ((i.astype(f32) + 0.5) * (1.0 / total))
        turns = turns - jnp.round(turns)
        wave = sine_of_turns(turns + quarter)
        return wave, pltpu.roll(wave, 64, 1)

    wx, ox = waves(0, cx0, 8, TOTAL_X // CF)
    wy, oy = waves(1, cy0, 16, TOTAL_Y // CF)
    wz, oz = waves(2, 0, CZ, CZ)
    cosx, sinx = jnp.where(first, ox, wx), jnp.where(first, wx, ox)
    cosz, sinz = jnp.where(first, oz, wz), jnp.where(first, wz, oz)
    turnedy = jnp.where(first, oy, -oy)
    for i in range(GX):
        c, s = cosx[i : i + 1, :], sinx[i : i + 1, :]
        axy[pl.ds(16 * i, 16), :] = wy * c + turnedy * s
        bxy[pl.ds(16 * i, 16), :] = turnedy * c - wy * s

    for l in range(3):
        w2[l] = doubled(weights[l] * 0.5)
    w2[3] = doubled(jnp.broadcast_to(wout[...], (128, 128)).T)
    pick = lax.broadcasted_iota(jnp.int32, (CZ, 128), 0) == (
        lax.broadcasted_iota(jnp.int32, (CZ, 128), 1) // CF
    )
    row16 = lax.broadcasted_iota(jnp.int32, (16, 128), 0)

    def body(i, carry):
        parts = []
        for k in range(GROUP):
            for j in range(GY):
                at = pl.ds(16 * (GROUP * i + k) + j, 1)
                parts.append(axy[at, :] * cosz + bxy[at, :] * sinz)
        h = jnp.concatenate(parts, axis=0)
        for l in range(4):
            hi, lo = split2(h)
            both = jnp.concatenate([hi, lo], axis=1)
            out = jnp.dot(both, w2[l], preferred_element_type=f32)
            h = out[:, :128] + out[:, 128:]
            if l < 3:
                h = h + biases[l : l + 1, :] * 0.5
                h = h + h * jnp.tanh(h)
        for k in range(GROUP):
            logits = jnp.zeros((16, 128), f32)
            for j in range(GY):
                cell = (k * GY + j) * CZ
                line = jnp.sum(jnp.where(pick, h[cell : cell + CZ, :], 0.0), axis=0, keepdims=True)
                logits = jnp.where(row16 == (j + 15) % 16, line, logits)
            coarse[GROUP * i + k] = 1.0 / (1.0 + jnp.exp(-(logits + bout[0])))
        return carry

    lax.fori_loop(0, GX // GROUP, body, 0)


W0, W1, W2, W3 = 2.0, 1.0, 2.0 - math.sqrt(2.0), 2.0 - math.sqrt(3.0)
SCALE = MU / 16.0


def density_kernel(ids, coarse, young, inverse, density, density_v, sem):
    lane = lax.broadcasted_iota(jnp.int32, (16, NZ), 1)
    not_last, not_first = lane < NZ - 1, lane > 0
    row16 = lax.broadcasted_iota(jnp.int32, (16, NZ), 0)
    y_cell = ids[1] * CY + jnp.where(row16 == 15, -1, row16)
    inside_y = (y_cell >= 0) & (y_cell < TOTAL_Y // CF)

    ri = lax.broadcasted_iota(jnp.int32, (EY + NY, 144), 0)
    ci = lax.broadcasted_iota(jnp.int32, (EY + NY, 144), 1)
    r = jnp.where(ri < EY, ri, ri - EY + CF)
    oy = r & 3
    kind = jnp.where(oy == 0, 0, jnp.where(oy == 3, 2, 1))
    want = kind * 16 + (((r >> 2) + 15) & 15)
    spread = jnp.where(
        (ci == want) | (ci == want + 48) | (ci == want + 96), 1.0, 0.0
    ).astype(jnp.bfloat16)
    y_fine = ids[1] * NY - CF + lax.broadcasted_iota(jnp.int32, (EY, NZ), 0)
    inside_rows = jnp.where((y_fine >= 0) & (y_fine < TOTAL_Y), SCALE, 0.0)

    def layers(v):
        side = jnp.where(not_last, pltpu.roll(v, NZ - 1, 1), 0.0) + jnp.where(
            not_first, pltpu.roll(v, 1, 1), 0.0
        )
        return W0 * v + W1 * side, W1 * v + W2 * side, W2 * v + W3 * side

    side = jnp.where(not_last, 1.0, 0.0) + jnp.where(not_first, 1.0, 0.0)
    ones = (W0 + W1 * side, W1 + W2 * side, W2 + W3 * side)
    rows_in = jnp.where(inside_y, 1.0, 0.0)
    stacks = []
    for i in range(GX):
        x_cell = ids[0] * CX - 1 + i
        ok_x = (x_cell >= 0) & (x_cell < TOTAL_X // CF)
        inside = jnp.where(inside_y & ok_x, 1.0, 0.0)
        stacks.append((
            layers(jnp.where(inside > 0.0, coarse[i], 0.0)),
            [inside * w for w in ones],
            inside > 0.0,
            jnp.where(ok_x, 1.0, 0.0),
        ))

    for i in range(GX):
        for plane_kind in range(3):
            low = max(i - 1, 0) if plane_kind == 0 else i
            high = min(i + 1, GX - 1) if plane_kind == 2 else i
            sums = []
            for which in range(2):
                here, below, over = stacks[i][which], stacks[low][which], stacks[high][which]
                t0 = here[0] + (below[1] + over[1])
                t1 = here[1] + (below[2] + over[2])
                down = pltpu.roll(t1, 1, 0)
                above = pltpu.roll(t1, 15, 0)
                sums.append((t0 + (down + t1), t0 + (t1 + t1), t0 + (t1 + above)))
            rho = jnp.concatenate(
                [a / jnp.where(stacks[i][2], b, 1.0) for a, b in zip(*sums)], axis=0
            )
            hi = rho.astype(jnp.bfloat16)
            rest = rho - hi.astype(f32)
            mid = rest.astype(jnp.bfloat16)
            lo = (rest - mid.astype(f32)).astype(jnp.bfloat16)
            fine = jnp.dot(spread, jnp.concatenate([hi, mid, lo], axis=0), preferred_element_type=f32)
            ext = fine[:EY, :]
            modulus = (0.02 + 0.98 * (ext * ext * ext)) * (inside_rows * stacks[i][3])
            for ox in {0: (0,), 1: (1, 2), 2: (3,)}[plane_kind]:
                x = i * CF + ox
                young[pl.ds(x * EY, EY), :] = modulus
                if 1 <= i <= CX:
                    density_v[pl.ds((x - CF) * NY, NY), :] = fine[EY:, :]

    copy = pltpu.make_async_copy(density_v, density, sem)
    copy.start()
    lane8 = lax.broadcasted_iota(jnp.int32, (8, NZ), 1) > 0

    def plane(x, carry):
        for j in range(EY // 8):
            at = x * EY + 8 * j
            if j == 0:
                at = pl.multiple_of(at, 8)
            total = (young[pl.ds(at, 8), :] + young[pl.ds(at - 1, 8), :]) + (
                young[pl.ds(at - EY, 8), :] + young[pl.ds(at - EY - 1, 8), :]
            )
            total = total + jnp.where(lane8, pltpu.roll(total, 1, 1), 0.0)
            inverse[pl.ds(at, 8), :] = 1.0 / (DIAG / SCALE * total + 1e-30)
        return carry

    lax.fori_loop(2, 22, plane, 0, unroll=2)
    copy.wait()


QUANTITIES = 4
BLOCKS = EY // 8
TALL = EY + 8


def operator_pass(zsum, zdiff, young, above, minus, plus, begin, end, unroll):
    def block(yb, carry):
        r0 = yb * 8

        def transform(x):
            out = []
            for c in range(3):
                at = c * SIZE + x * EY + r0
                pairs = [(t[pl.ds(at, 8), :], t[pl.ds(at + 1, 8), :]) for t in (zsum, zdiff)]
                out += [v + u for v, u in pairs] + [u - v for v, u in pairs]
            return out

        def modal(x, a, b):
            e1 = young[pl.ds(pl.multiple_of(x * EY + r0, 8), 8), :]
            e3 = e1 * (1.0 / 3.0)
            e31 = e1 * 0.5
            e9 = e1 * ((RATIO + 4.0) / 9.0)
            s = [p + q for p, q in zip(a, b)]
            d = [q - p for p, q in zip(a, b)]
            u = lambda c, p, q, r: (d if p else s)[4 * c + 2 * q + r]
            g = {}
            ux, uy, uz = u(0, 1, 0, 0), u(1, 0, 1, 0), u(2, 0, 0, 1)
            trace = RATIO * (ux + uy + uz)
            g[0, 1, 0, 0] = e1 * ((ux + ux) + trace)
            g[1, 0, 1, 0] = e1 * ((uy + uy) + trace)
            g[2, 0, 0, 1] = e1 * ((uz + uz) + trace)
            g[0, 0, 1, 0] = g[1, 1, 0, 0] = e1 * (u(0, 0, 1, 0) + u(1, 1, 0, 0))
            g[0, 0, 0, 1] = g[2, 1, 0, 0] = e1 * (u(0, 0, 0, 1) + u(2, 1, 0, 0))
            g[1, 0, 0, 1] = g[2, 0, 1, 0] = e1 * (u(1, 0, 0, 1) + u(2, 0, 1, 0))
            for one, two in (
                ((0, 1, 0, 1), (1, 0, 1, 1)),
                ((0, 1, 1, 0), (2, 0, 1, 1)),
                ((1, 1, 1, 0), (2, 1, 0, 1)),
            ):
                p, q = u(*one), u(*two)
                g[one] = e31 * (3.0 * p + q)
                g[two] = e31 * (3.0 * q + p)
            p, q, r = u(0, 0, 1, 1), u(1, 1, 0, 1), u(2, 1, 1, 0)
            total = p + q + r
            g[0, 0, 1, 1] = e3 * (p + total)
            g[1, 1, 0, 1] = e3 * (q + total)
            g[2, 1, 1, 0] = e3 * (r + total)
            for c in range(3):
                g[c, 1, 1, 1] = e9 * u(c, 1, 1, 1)
            return g

        def keep(g):
            out = []
            for c in range(3):
                out.append(g[c, 1, 0, 0])
                for q, r in ((0, 1), (1, 0), (1, 1)):
                    out.append(g[c, 0, q, r] + g[c, 1, q, r])
            return out

        def step(x, state):
            a, held = state
            b = transform(x + 1)
            g = modal(x, a, b)
            for c in range(3):
                f = [held[4 * c] - g[c, 1, 0, 0]]
                for k, (q, r) in enumerate(((0, 1), (1, 0), (1, 1))):
                    f.append((g[c, 0, q, r] - g[c, 1, q, r]) + held[4 * c + 1 + k])
                h = []
                for r in range(2):
                    at = ((2 * c + r) * EX + x) * TALL + 8 + r0
                    above[pl.ds(at, 8), :] = f[r] + f[2 + r]
                    h.append((f[r] - f[2 + r]) + above[pl.ds(at - 1, 8), :])
                rows = pl.ds(pl.multiple_of(c * SIZE + x * EY + r0, 8), 8)
                minus[rows, :] = h[0] - h[1]
                plus[rows, :] = h[0] + h[1]
            return b, keep(g)

        a = transform(begin)
        b = transform(begin + 1)
        lax.fori_loop(begin + 1, end, step, (b, keep(modal(begin, a, b))), unroll=unroll)
        return carry

    lax.fori_loop(0, BLOCKS, block, 0)


class Stages:
    def __init__(self, load, free, inverse, field, scaled, minus, plus):
        self.load, self.free, self.inverse = load, free, inverse
        self.field, self.scaled, self.minus, self.plus = field, scaled, minus, plus
        lane = lax.broadcasted_iota(jnp.int32, (8, NZ), 1)
        row = lax.broadcasted_iota(jnp.int32, (8, NZ), 0)
        self.not_last, self.not_first = lane < NZ - 1, lane > 0
        self.first_rows = jnp.where(row >= CF, 1.0, 0.0)
        self.last_rows = jnp.where(row < CF, 1.0, 0.0)

    def z_stage(self, out, at, v):
        n = jnp.where(self.not_last, pltpu.roll(v, NZ - 1, 1), 0.0)
        out[0][at, :] = v + n
        out[1][at, :] = n - v

    def prepare(self, out, x):
        for j in range(BLOCKS):
            base = pl.multiple_of(x * EY, 8) + 8 * j
            inv = self.inverse[pl.ds(base, 8), :]
            for c in range(3):
                at = pl.ds(base + c * SIZE, 8)
                v = self.load[at, :] * inv
                self.field[at, :] = v
                self.z_stage(out, at, v)

    def gather(self, totals, j, terms):
        for k, t in enumerate(terms):
            if j == 0:
                t = t * self.first_rows
            if j == BLOCKS - 1:
                t = t * self.last_rows
            totals[k] = t if totals[k] is None else totals[k] + t

    def force(self, at):
        return self.minus[at, :] + jnp.where(self.not_first, pltpu.roll(self.plus[at, :], 1, 1), 0.0)

    def finish_one(self, out, x, dots):
        totals = [None] * 3
        for j in range(BLOCKS):
            base = pl.multiple_of(x * EY, 8) + 8 * j
            inv = self.inverse[pl.ds(base, 8), :]
            sums = None
            for c in range(3):
                at = pl.ds(base + c * SIZE, 8)
                w = self.free[at, :] * self.force(at)
                y = w * inv
                z = self.field[at, :]
                zt = z - y
                self.scaled[at, :] = y
                self.z_stage(out, at, zt)
                if dots is not None:
                    rt = self.load[at, :] - w
                    terms = (z * w, z * rt, zt * rt)
                    sums = terms if sums is None else [p + q for p, q in zip(sums, terms)]
            if dots is not None:
                self.gather(totals, j, sums)
        return dots if dots is None else [p + q for p, q in zip(dots, totals)]

    def finish_two(self, x, dots):
        totals = [None]
        for j in range(BLOCKS):
            base = pl.multiple_of(x * EY, 8) + 8 * j
            sums = None
            for c in range(3):
                at = pl.ds(base + c * SIZE, 8)
                q = self.free[at, :] * self.force(at)
                terms = ((self.field[at, :] - self.scaled[at, :]) * q,)
                sums = terms if sums is None else [p + r for p, r in zip(sums, terms)]
            self.gather(totals, j, sums)
        return [p + q for p, q in zip(dots, totals)]


def clear_edges(above):
    zero = jnp.zeros((8, NZ), f32)

    def body(i, carry):
        above[pl.ds(pl.multiple_of(i * TALL, 8), 8), :] = zero
        return carry

    lax.fori_loop(0, 6 * EX, body, 0, unroll=8)


def clear_row_past(refs, x):
    for ref in refs:
        for c in range(3):
            ref[pl.ds(c * SIZE + x * EY, 8), :] = jnp.zeros((8, NZ), f32)


LAST = CF + NX - 1


def inner_kernel(
    load_in, free_in, ylo, yhi, young, inverse,
    load, free, field, scaled, zsum, zdiff, zsum2, zdiff2, dots_out,
    above, minus, plus,
):
    del load_in, free_in
    for c in range(3):
        base = c * SIZE + CF * EY
        for k in range(2):
            for strip, row in ((ylo, 2 + k), (yhi, 36 + k)):
                load[pl.ds(base + row, NX, stride=EY), :] = strip[pl.ds((c * 2 + k) * NX, NX), :]
        for strip, row in ((ylo, 3), (yhi, 36)):
            free[pl.ds(base + row, NX, stride=EY), :] = strip[pl.ds((6 + c) * NX, NX), :]
    stages = Stages(load, free, inverse, field, scaled, minus, plus)
    first, second = (zsum, zdiff), (zsum2, zdiff2)

    def prepare(x, carry):
        stages.prepare(first, x)
        return carry

    lax.fori_loop(CF, LAST + 1, prepare, 0, unroll=2)
    clear_row_past(first, LAST + 1)
    clear_edges(above)
    operator_pass(zsum, zdiff, young, above, minus, plus, CF, LAST, 7)
    dots = lax.fori_loop(
        CF + 1, LAST, lambda x, d: stages.finish_one(second, x, d), [jnp.zeros((8, NZ), f32)] * 3, unroll=2
    )
    for k, d in enumerate(dots):
        dots_out[k] = d


def outer_kernel(
    load_in, free_in, field_in, scaled_in, zsum_in, zdiff_in, zsum2_in, zdiff2_in,
    xlo, xhi, young, inverse, dots_in,
    load, free, field, scaled, zsum, zdiff, zsum2, zdiff2, dots_out,
    above, minus, plus,
):
    del load_in, free_in, field_in, scaled_in, zsum_in, zdiff_in, zsum2_in, zdiff2_in
    for c in range(3):
        for k in range(2):
            for plane, x in ((xlo, 2 + k), (xhi, LAST + 1 + k)):
                load[pl.ds(c * SIZE + x * EY, EY), :] = plane[pl.ds((c * 2 + k) * EY, EY), :]
        for plane, x in ((xlo, 3), (xhi, LAST + 1)):
            free[pl.ds(c * SIZE + x * EY, EY), :] = plane[pl.ds((6 + c) * EY, EY), :]
    stages = Stages(load, free, inverse, field, scaled, minus, plus)
    first, second = (zsum, zdiff), (zsum2, zdiff2)
    for start in (2, LAST + 1):
        stages.prepare(first, start)
        stages.prepare(first, start + 1)
    clear_row_past(first, LAST + 3)
    clear_row_past(second, LAST + 2)
    clear_edges(above)
    operator_pass(zsum, zdiff, young, above, minus, plus, 2, CF + 1, 2)
    operator_pass(zsum, zdiff, young, above, minus, plus, LAST - 1, LAST + 2, 2)
    stages.finish_one(second, CF - 1, None)
    stages.finish_one(second, LAST + 1, None)
    dots = [dots_in[k] for k in range(3)]
    for x in (CF, LAST):
        dots = stages.finish_one(second, x, dots)

    operator_pass(zsum2, zdiff2, young, above, minus, plus, CF - 1, LAST + 1, 8)
    dots = dots + lax.fori_loop(CF, LAST + 1, stages.finish_two, [jnp.zeros((8, NZ), f32)], unroll=2)
    one = lax.broadcasted_iota(jnp.int32, (1, NZ), 1)
    line = jnp.zeros((1, NZ), f32)
    for k, d in enumerate(dots):
        line = jnp.where(one == k, jnp.sum(d), line)
    dots_out[...] = line


def final_kernel(parts, z, y, out, out_v, sem):
    total = jnp.sum(parts[...], axis=0, keepdims=True)
    lane = lax.broadcasted_iota(jnp.int32, (1, NZ), 1)
    zw, a, b, c = (
        jnp.sum(jnp.where(lane == k, total, 0.0), axis=1, keepdims=True) for k in range(QUANTITIES)
    )
    rz = zw + a
    alpha = rz / zw
    less = -(a / zw)
    rz1 = alpha * (alpha * b + less * a)
    energy = less * (less * zw) + 2.0 * alpha * (less * (a - b)) + alpha * (alpha * c)
    beta = rz1 / rz
    alpha1 = rz1 / (energy - beta * (rz1 / alpha))
    c1 = jnp.broadcast_to(alpha + alpha1 * (1.0 + beta), (8, NZ))[0:1, :]
    c2 = jnp.broadcast_to(-(alpha * alpha1), (8, NZ))[0:1, :]
    copies = []
    for c in range(3):
        def body(x, carry, c=c):
            src = pl.ds(c * SIZE + (x + CF) * EY + CF, NY)
            to = pl.ds(pl.multiple_of((c * NX + x) * NY, NY), NY)
            out_v[to, :] = c1 * z[src, :] + c2 * y[src, :]
            return carry

        lax.fori_loop(0, NX, body, 0, unroll=4)
        rows = pl.ds(c * NX * NY, NX * NY)
        copy = pltpu.make_async_copy(out_v.at[rows, :], out.at[rows, :], sem.at[c])
        copy.start()
        copies.append(copy)
    for copy in copies:
        copy.wait()


def per_device(
    body_force, fixed_dofs, load_nodes, load_forces, frequencies,
    hidden_weights, hidden_biases, output_weights, output_bias,
):
    bx, by = lax.axis_index("gx"), lax.axis_index("gy")
    ids = jnp.stack([bx, by]).astype(jnp.int32)
    rows = 3 * NX * NY
    body = body_force.reshape(rows, NZ)
    fixed = fixed_dofs.reshape(rows, NZ)
    nodes = load_nodes.T
    strip = shape(9 * NX, NZ)
    ext = shape(3 * SIZE, NZ)
    load, free, ylo_send, yhi_send = call(
        pack_kernel, (ext, ext, strip, strip),
        [SMEM] + [pltpu.HBM] * 4, (ids, nodes, load_forces, body, fixed),
        scratch=[VMEM((rows, NZ), f32), VMEM((rows, NZ), jnp.int32), VMEM((3, LOADS), jnp.int32),
                 SMEM((3, LOADS), jnp.int32), SMEM((3, LOADS), f32), pltpu.SemaphoreType.DMA((9,))],
        cost=pl.CostEstimate(flops=400000, transcendentals=0, bytes_accessed=2400000),
    )
    ny, nx = lax.axis_size("gy"), lax.axis_size("gx")
    up_y = [(i, i + 1) for i in range(ny - 1)]
    down_y = [(i + 1, i) for i in range(ny - 1)]
    up_x = [(i, i + 1) for i in range(nx - 1)]
    down_x = [(i + 1, i) for i in range(nx - 1)]
    ylo = lax.ppermute(yhi_send, "gy", up_y)
    yhi = lax.ppermute(ylo_send, "gy", down_y)

    coarse = call(
        mlp_kernel, shape(GX, 16, 128),
        [SMEM, VMEM, VMEM, VMEM, VMEM, SMEM],
        (ids, frequencies, hidden_weights, hidden_biases, output_weights.reshape(1, 128), output_bias),
        scratch=[VMEM((16 * GX, 128), f32), VMEM((16 * GX, 128), f32), VMEM((4, 256, 256), jnp.bfloat16)],
        cost=pl.CostEstimate(flops=1500000000, transcendentals=800000, bytes_accessed=300000),
    )
    plane = shape(9 * EY, NZ)
    xlo_send, xhi_send = call(
        planes_kernel, (plane, plane), [VMEM] * 5, (load, free, ylo, yhi, coarse),
    )
    xlo = lax.ppermute(xhi_send, "gx", up_x)
    xhi = lax.ppermute(xlo_send, "gx", down_x)
    young, inverse, density = call(
        density_kernel, (shape(SIZE, NZ), shape(SIZE, NZ), shape(NX * NY, NZ)),
        [SMEM, VMEM], (ids, coarse),
        scratch=[VMEM((NX * NY, NZ), f32), pltpu.SemaphoreType.DMA],
        out_spaces=(VMEM, VMEM, pltpu.HBM),
        cost=pl.CostEstimate(flops=8000000, transcendentals=0, bytes_accessed=1300000),
    )
    work = [VMEM((6 * EX * TALL, NZ), f32), VMEM((3 * SIZE, NZ), f32), VMEM((3 * SIZE, NZ), f32)]
    *state, dots = call(
        inner_kernel, (ext,) * 8 + (shape(3, 8, NZ),),
        [VMEM] * 6, (load, free, ylo, yhi, young, inverse),
        scratch=work, aliases={0: 0, 1: 1},
        cost=pl.CostEstimate(flops=60000000, transcendentals=0, bytes_accessed=9000000),
    )
    *state, dots = call(
        outer_kernel, (ext,) * 8 + (shape(1, NZ),),
        [VMEM] * 13, (*state, xlo, xhi, young, inverse, dots),
        scratch=work, aliases={i: i for i in range(8)},
    )
    z, y = state[2], state[3]
    parts = lax.all_to_all(
        jnp.broadcast_to(dots, (nx * ny, NZ)), ("gx", "gy"), 0, 0, tiled=True
    )
    out = call(
        final_kernel, shape(rows, NZ), [VMEM] * 3, (parts, z, y),
        scratch=[VMEM((rows, NZ), f32), pltpu.SemaphoreType.DMA((3,))], out_spaces=pltpu.HBM,
    )
    return out.reshape(3, NX, NY, NZ), density.reshape(NX, NY, NZ)


def solution(mesh):
    return jax.shard_map(
        per_device,
        mesh=mesh,
        in_specs=(P(None, "gx", "gy", None), P(None, "gx", "gy", None)) + (P(),) * 7,
        out_specs=(P(None, "gx", "gy", None), P("gx", "gy", None)),
        check_vma=False,
    )
```

```python
import functools
import math

import jax
import jax.numpy as jnp
from jax import lax
from jax.experimental import pallas as pl
from jax.experimental.pallas import tpu as pltpu
from jax.sharding import PartitionSpec as P

CF = 4
NX, NY, NZ = 16, 32, 128
TOTAL_X, TOTAL_Y = 512, 256
CX, CY, CZ = NX // CF, NY // CF, NZ // CF
GX, GY = CX + 2, CY + 2
EX, EY = GX * CF, GY * CF
SIZE = EX * EY
LOADS = 512
NU, MU = 0.3, 1.0 / 2.6
LAM = 0.3 / (1.3 * 0.4)
RATIO = LAM / MU
DIAG = (LAM + 4.0 * MU) / 9.0
VMEM = pltpu.VMEM
SMEM = pltpu.SMEM
highest = lax.Precision.HIGHEST
f32 = jnp.float32


def spec(space=VMEM):
    return pl.BlockSpec(memory_space=space)


def call(kernel, out_shape, in_spaces, args, scratch=(), cost=None, out_spaces=None, aliases=None, limit=16):
    out_specs = jax.tree.map(lambda _: spec(), out_shape)
    if out_spaces is not None:
        out_specs = jax.tree.map(lambda _, space: spec(space), out_shape, out_spaces)
    args = [
        pltpu.with_memory_space_constraint(a, space) if space is pltpu.HBM else a
        for a, space in zip(args, in_spaces)
    ]
    if out_spaces is not None:
        out_shape = jax.tree.map(
            lambda a, space: pltpu.HBM(a.shape, a.dtype) if space is pltpu.HBM else a, out_shape, out_spaces
        )
    return pl.pallas_call(
        kernel,
        out_shape=out_shape,
        in_specs=[spec(s) for s in in_spaces],
        out_specs=out_specs,
        scratch_shapes=list(scratch),
        input_output_aliases=aliases or {},
        compiler_params=pltpu.CompilerParams(vmem_limit_bytes=limit << 20),
        cost_estimate=cost,
    )(*args)


def place():
    return lax.axis_index("gx"), lax.axis_index("gy")


def shape(*dims):
    return jax.ShapeDtypeStruct(dims, f32)


def pack_kernel(
    nodes, forces, body, fixed,
    load, free, lo_out, hi_out,
    body_v, fixed_v, nodes_v, nodes_s, forces_s, found, sem,
):
    part = NX * NY
    copies = [
        pltpu.make_async_copy(nodes, nodes_v, sem.at[0]),
        pltpu.make_async_copy(nodes, nodes_s, sem.at[1]),
        pltpu.make_async_copy(forces, forces_s, sem.at[2]),
    ]
    for c in range(3):
        for k, (src, dst) in enumerate(((body, body_v), (fixed, fixed_v))):
            rows = pl.ds(c * part, part)
            copies.append(pltpu.make_async_copy(src.at[rows, :], dst.at[rows, :], sem.at[3 + 2 * c + k]))
    for copy in copies:
        copy.start()

    zero = jnp.zeros((8, NZ), f32)

    def clear(x, carry):
        for c in range(3):
            base = pl.multiple_of(c * SIZE + x * EY, 8)
            for ref in (load, free):
                ref[pl.ds(base, 8), :] = zero
                ref[pl.ds(base + EY - 8, 8), :] = zero
        return carry

    lax.fori_loop(CF, CF + NX, clear, 0, unroll=2)

    ids = place()
    start_x = ids[0] * NX
    start_y = ids[1] * NY
    for copy in copies[:3]:
        copy.wait()
    lx = nodes_v[0:1, :] - start_x
    ly = nodes_v[1:2, :] - start_y
    mine = (lx >= 0) & (lx < NX) & (ly >= 0) & (ly < NY)
    index = lax.broadcasted_iota(jnp.int32, (1, LOADS), 1)
    todo = jnp.where(mine, index, LOADS)
    lane = lax.broadcasted_iota(jnp.int32, (1, NZ), 1)

    def more(state):
        return state[0] < LOADS

    def collect(state):
        p, count = state
        found[count] = p
        return jnp.min(jnp.where(todo > p, todo, LOADS)), count + 1

    _, count = lax.while_loop(more, collect, (jnp.min(todo), 0))
    for copy in copies[3:]:
        copy.wait()

    def add_one(i, carry):
        p = found[i]
        x = nodes_s[0, p] - start_x
        y = nodes_s[1, p] - start_y
        hit = lane == nodes_s[2, p]
        for c in range(3):
            row = pl.ds((c * NX + x) * NY + y, 1)
            body_v[row, :] = body_v[row, :] + jnp.where(hit, forces_s[c, p], 0.0)
        return carry

    lax.fori_loop(0, count, add_one, 0)

    def mask(x, carry):
        for c in range(3):
            src = pl.ds(pl.multiple_of((c * NX + x) * NY, NY), NY)
            dst = pl.ds(c * SIZE + (x + CF) * EY + CF, NY)
            ok = fixed_v[src, :] == 0
            load[dst, :] = jnp.where(ok, body_v[src, :], 0.0)
            free[dst, :] = jnp.where(ok, 1.0, 0.0)
        return carry

    lax.fori_loop(0, NX, mask, 0, unroll=2)
    for c in range(3):
        base = c * SIZE + CF * EY + CF
        for j in range(2):
            to = pl.ds((c * 2 + j) * NX, NX)
            lo_out[to, :] = load[pl.ds(base + j, NX, stride=EY), :]
            hi_out[to, :] = load[pl.ds(base + NY - 2 + j, NX, stride=EY), :]
        to = pl.ds((6 + c) * NX, NX)
        lo_out[to, :] = free[pl.ds(base, NX, stride=EY), :]
        hi_out[to, :] = free[pl.ds(base + NY - 1, NX, stride=EY), :]


def planes_kernel(load, free, ylo, yhi, coarse, lo_out, hi_out):
    del coarse
    for out, first in ((lo_out, CF), (hi_out, CF + NX - 2)):
        for c in range(3):
            for j in range(2):
                x = first + j
                base = (c * 2 + j) * EY
                out[pl.ds(base, EY), :] = load[pl.ds(c * SIZE + x * EY, EY), :]
                for k in range(2):
                    at = pl.ds((c * 2 + k) * NX + x - CF, 1)
                    out[pl.ds(base + 2 + k, 1), :] = ylo[at, :]
                    out[pl.ds(base + 36 + k, 1), :] = yhi[at, :]
            x = CF if first == CF else CF + NX - 1
            base = (6 + c) * EY
            out[pl.ds(base, EY), :] = free[pl.ds(c * SIZE + x * EY, EY), :]
            at = pl.ds((6 + c) * NX + x - CF, 1)
            out[pl.ds(base + 3, 1), :] = ylo[at, :]
            out[pl.ds(base + 36, 1), :] = yhi[at, :]


def split2(v):
    hi = v.astype(jnp.bfloat16)
    return hi, (v - hi.astype(f32)).astype(jnp.bfloat16)


def doubled(w):
    hi, lo = split2(w)
    both = jnp.concatenate([hi, lo], axis=1)
    return jnp.concatenate([both, both], axis=0)


def sine_of_turns(t):
    t = t - jnp.round(t)
    a = jnp.abs(t)
    x = jnp.minimum(a, 0.5 - a) * (2.0 * math.pi)
    x2 = x * x
    p = 1.0 / 6227020800.0
    for k in (39916800.0, 362880.0, 5040.0, 120.0, 6.0, 1.0):
        p = 1.0 / k - x2 * p
    p = x * p
    return jnp.where(t < 0.0, -p, p)


GROUP = 3


def mlp_kernel(freq, weights, biases, wout, bout, coarse, axy, bxy, w2):
    ids = place()
    cx0 = ids[0] * CX - 1
    cy0 = ids[1] * CY - 1
    f = freq[...]
    ff = jnp.concatenate([f, f], axis=1)
    first = lax.broadcasted_iota(jnp.int32, (1, 128), 1) < 64
    quarter = jnp.where(first, 0.0, 0.25)

    def waves(row, start, rows, total):
        i = lax.broadcasted_iota(jnp.int32, (rows, 128), 0) + start
        turns = ff[row : row + 1, :] * ((i.astype(f32) + 0.5) * (1.0 / total))
        turns = turns - jnp.round(turns)
        wave = sine_of_turns(turns + quarter)
        return wave, pltpu.roll(wave, 64, 1)

    wx, ox = waves(0, cx0, 8, TOTAL_X // CF)
    wy, oy = waves(1, cy0, 16, TOTAL_Y // CF)
    wz, oz = waves(2, 0, CZ, CZ)
    cosx, sinx = jnp.where(first, ox, wx), jnp.where(first, wx, ox)
    cosz, sinz = jnp.where(first, oz, wz), jnp.where(first, wz, oz)
    turnedy = jnp.where(first, oy, -oy)
    for i in range(GX):
        c, s = cosx[i : i + 1, :], sinx[i : i + 1, :]
        axy[pl.ds(16 * i, 16), :] = wy * c + turnedy * s
        bxy[pl.ds(16 * i, 16), :] = turnedy * c - wy * s

    for l in range(3):
        w2[l] = doubled(weights[l] * 0.5)
    w2[3] = doubled(jnp.broadcast_to(wout[...], (128, 128)).T)
    pick = lax.broadcasted_iota(jnp.int32, (CZ, 128), 0) == (
        lax.broadcasted_iota(jnp.int32, (CZ, 128), 1) // CF
    )
    row16 = lax.broadcasted_iota(jnp.int32, (16, 128), 0)

    def body(i, carry):
        parts = []
        for k in range(GROUP):
            for j in range(GY):
                at = pl.ds(16 * (GROUP * i + k) + j, 1)
                parts.append(axy[at, :] * cosz + bxy[at, :] * sinz)
        h = jnp.concatenate(parts, axis=0)
        for l in range(4):
            hi, lo = split2(h)
            both = jnp.concatenate([hi, lo], axis=1)
            out = jnp.dot(both, w2[l], preferred_element_type=f32)
            h = out[:, :128] + out[:, 128:]
            if l < 3:
                h = h + biases[l : l + 1, :] * 0.5
                h = h + h * jnp.tanh(h)
        for k in range(GROUP):
            logits = jnp.zeros((16, 128), f32)
            for j in range(GY):
                cell = (k * GY + j) * CZ
                line = jnp.sum(jnp.where(pick, h[cell : cell + CZ, :], 0.0), axis=0, keepdims=True)
                logits = jnp.where(row16 == (j + 15) % 16, line, logits)
            coarse[GROUP * i + k] = 1.0 / (1.0 + jnp.exp(-(logits + bout[...])))
        return carry

    lax.fori_loop(0, GX // GROUP, body, 0)


W0, W1, W2, W3 = 2.0, 1.0, 2.0 - math.sqrt(2.0), 2.0 - math.sqrt(3.0)
SCALE = MU / 16.0


def density_kernel(coarse, young, inverse, density, density_v, sem):
    ids = place()
    lane = lax.broadcasted_iota(jnp.int32, (16, NZ), 1)
    not_last, not_first = lane < NZ - 1, lane > 0
    row16 = lax.broadcasted_iota(jnp.int32, (16, NZ), 0)
    y_cell = ids[1] * CY + jnp.where(row16 == 15, -1, row16)
    inside_y = (y_cell >= 0) & (y_cell < TOTAL_Y // CF)

    ri = lax.broadcasted_iota(jnp.int32, (EY + NY, 144), 0)
    ci = lax.broadcasted_iota(jnp.int32, (EY + NY, 144), 1)
    r = jnp.where(ri < EY, ri, ri - EY + CF)
    oy = r & 3
    kind = jnp.where(oy == 0, 0, jnp.where(oy == 3, 2, 1))
    want = kind * 16 + (((r >> 2) + 15) & 15)
    spread = jnp.where(
        (ci == want) | (ci == want + 48) | (ci == want + 96), 1.0, 0.0
    ).astype(jnp.bfloat16)
    y_fine = ids[1] * NY - CF + lax.broadcasted_iota(jnp.int32, (EY, NZ), 0)
    inside_rows = jnp.where((y_fine >= 0) & (y_fine < TOTAL_Y), SCALE, 0.0)

    def layers(v):
        side = jnp.where(not_last, pltpu.roll(v, NZ - 1, 1), 0.0) + jnp.where(
            not_first, pltpu.roll(v, 1, 1), 0.0
        )
        return W0 * v + W1 * side, W1 * v + W2 * side, W2 * v + W3 * side

    side = jnp.where(not_last, 1.0, 0.0) + jnp.where(not_first, 1.0, 0.0)
    ones = (W0 + W1 * side, W1 + W2 * side, W2 + W3 * side)
    rows_in = jnp.where(inside_y, 1.0, 0.0)
    stacks = []
    for i in range(GX):
        x_cell = ids[0] * CX - 1 + i
        ok_x = (x_cell >= 0) & (x_cell < TOTAL_X // CF)
        inside = jnp.where(inside_y & ok_x, 1.0, 0.0)
        stacks.append((
            layers(jnp.where(inside > 0.0, coarse[i], 0.0)),
            [inside * w for w in ones],
            inside > 0.0,
            jnp.where(ok_x, 1.0, 0.0),
        ))

    for i in range(GX):
        for plane_kind in range(3):
            low = max(i - 1, 0) if plane_kind == 0 else i
            high = min(i + 1, GX - 1) if plane_kind == 2 else i
            sums = []
            for which in range(2):
                here, below, over = stacks[i][which], stacks[low][which], stacks[high][which]
                t0 = here[0] + (below[1] + over[1])
                t1 = here[1] + (below[2] + over[2])
                down = pltpu.roll(t1, 1, 0)
                above = pltpu.roll(t1, 15, 0)
                sums.append((t0 + (down + t1), t0 + (t1 + t1), t0 + (t1 + above)))
            rho = jnp.concatenate(
                [a / jnp.where(stacks[i][2], b, 1.0) for a, b in zip(*sums)], axis=0
            )
            hi = rho.astype(jnp.bfloat16)
            rest = rho - hi.astype(f32)
            mid = rest.astype(jnp.bfloat16)
            lo = (rest - mid.astype(f32)).astype(jnp.bfloat16)
            fine = jnp.dot(spread, jnp.concatenate([hi, mid, lo], axis=0), preferred_element_type=f32)
            ext = fine[:EY, :]
            modulus = (0.02 + 0.98 * (ext * ext * ext)) * (inside_rows * stacks[i][3])
            for ox in {0: (0,), 1: (1, 2), 2: (3,)}[plane_kind]:
                x = i * CF + ox
                young[pl.ds(x * EY, EY), :] = modulus
                if 1 <= i <= CX:
                    density_v[pl.ds((x - CF) * NY, NY), :] = fine[EY:, :]

    copy = pltpu.make_async_copy(density_v, density, sem)
    copy.start()
    lane8 = lax.broadcasted_iota(jnp.int32, (8, NZ), 1) > 0

    def plane(x, carry):
        for j in range(EY // 8):
            at = x * EY + 8 * j
            if j == 0:
                at = pl.multiple_of(at, 8)
            total = (young[pl.ds(at, 8), :] + young[pl.ds(at - 1, 8), :]) + (
                young[pl.ds(at - EY, 8), :] + young[pl.ds(at - EY - 1, 8), :]
            )
            total = total + jnp.where(lane8, pltpu.roll(total, 1, 1), 0.0)
            inverse[pl.ds(at, 8), :] = 1.0 / (DIAG / SCALE * total + 1e-30)
        return carry

    lax.fori_loop(2, 22, plane, 0, unroll=2)
    copy.wait()


QUANTITIES = 4
BLOCKS = EY // 8
TALL = EY + 8


def operator_pass(zsum, zdiff, young, above, minus, plus, begin, end, unroll):
    def block(yb, carry):
        r0 = yb * 8

        def transform(x):
            out = []
            for c in range(3):
                at = c * SIZE + x * EY + r0
                pairs = [(t[pl.ds(at, 8), :], t[pl.ds(at + 1, 8), :]) for t in (zsum, zdiff)]
                out += [v + u for v, u in pairs] + [u - v for v, u in pairs]
            return out

        def modal(x, a, b):
            e1 = young[pl.ds(pl.multiple_of(x * EY + r0, 8), 8), :]
            e3 = e1 * (1.0 / 3.0)
            e31 = e1 * 0.5
            e9 = e1 * ((RATIO + 4.0) / 9.0)
            s = [p + q for p, q in zip(a, b)]
            d = [q - p for p, q in zip(a, b)]
            u = lambda c, p, q, r: (d if p else s)[4 * c + 2 * q + r]
            g = {}
            ux, uy, uz = u(0, 1, 0, 0), u(1, 0, 1, 0), u(2, 0, 0, 1)
            trace = RATIO * (ux + uy + uz)
            g[0, 1, 0, 0] = e1 * ((ux + ux) + trace)
            g[1, 0, 1, 0] = e1 * ((uy + uy) + trace)
            g[2, 0, 0, 1] = e1 * ((uz + uz) + trace)
            g[0, 0, 1, 0] = g[1, 1, 0, 0] = e1 * (u(0, 0, 1, 0) + u(1, 1, 0, 0))
            g[0, 0, 0, 1] = g[2, 1, 0, 0] = e1 * (u(0, 0, 0, 1) + u(2, 1, 0, 0))
            g[1, 0, 0, 1] = g[2, 0, 1, 0] = e1 * (u(1, 0, 0, 1) + u(2, 0, 1, 0))
            for one, two in (
                ((0, 1, 0, 1), (1, 0, 1, 1)),
                ((0, 1, 1, 0), (2, 0, 1, 1)),
                ((1, 1, 1, 0), (2, 1, 0, 1)),
            ):
                p, q = u(*one), u(*two)
                g[one] = e31 * (3.0 * p + q)
                g[two] = e31 * (3.0 * q + p)
            p, q, r = u(0, 0, 1, 1), u(1, 1, 0, 1), u(2, 1, 1, 0)
            total = p + q + r
            g[0, 0, 1, 1] = e3 * (p + total)
            g[1, 1, 0, 1] = e3 * (q + total)
            g[2, 1, 1, 0] = e3 * (r + total)
            for c in range(3):
                g[c, 1, 1, 1] = e9 * u(c, 1, 1, 1)
            return g

        def keep(g):
            out = []
            for c in range(3):
                out.append(g[c, 1, 0, 0])
                for q, r in ((0, 1), (1, 0), (1, 1)):
                    out.append(g[c, 0, q, r] + g[c, 1, q, r])
            return out

        def step(x, state):
            a, held = state
            b = transform(x + 1)
            g = modal(x, a, b)
            for c in range(3):
                f = [held[4 * c] - g[c, 1, 0, 0]]
                for k, (q, r) in enumerate(((0, 1), (1, 0), (1, 1))):
                    f.append((g[c, 0, q, r] - g[c, 1, q, r]) + held[4 * c + 1 + k])
                h = []
                for r in range(2):
                    at = ((2 * c + r) * EX + x) * TALL + 8 + r0
                    above[pl.ds(at, 8), :] = f[r] + f[2 + r]
                    h.append((f[r] - f[2 + r]) + above[pl.ds(at - 1, 8), :])
                rows = pl.ds(pl.multiple_of(c * SIZE + x * EY + r0, 8), 8)
                minus[rows, :] = h[0] - h[1]
                plus[rows, :] = h[0] + h[1]
            return b, keep(g)

        a = transform(begin)
        b = transform(begin + 1)
        lax.fori_loop(begin + 1, end, step, (b, keep(modal(begin, a, b))), unroll=unroll)
        return carry

    lax.fori_loop(0, BLOCKS, block, 0)


class Stages:
    def __init__(self, load, free, inverse, field, scaled, minus, plus):
        self.load, self.free, self.inverse = load, free, inverse
        self.field, self.scaled, self.minus, self.plus = field, scaled, minus, plus
        lane = lax.broadcasted_iota(jnp.int32, (8, NZ), 1)
        row = lax.broadcasted_iota(jnp.int32, (8, NZ), 0)
        self.not_last, self.not_first = lane < NZ - 1, lane > 0
        self.first_rows = jnp.where(row >= CF, 1.0, 0.0)
        self.last_rows = jnp.where(row < CF, 1.0, 0.0)

    def z_stage(self, out, at, v):
        n = jnp.where(self.not_last, pltpu.roll(v, NZ - 1, 1), 0.0)
        out[0][at, :] = v + n
        out[1][at, :] = n - v

    def prepare(self, out, x):
        for j in range(BLOCKS):
            base = pl.multiple_of(x * EY, 8) + 8 * j
            inv = self.inverse[pl.ds(base, 8), :]
            for c in range(3):
                at = pl.ds(base + c * SIZE, 8)
                v = self.load[at, :] * inv
                self.field[at, :] = v
                self.z_stage(out, at, v)

    def gather(self, totals, j, terms):
        for k, t in enumerate(terms):
            if j == 0:
                t = t * self.first_rows
            if j == BLOCKS - 1:
                t = t * self.last_rows
            totals[k] = t if totals[k] is None else totals[k] + t

    def force(self, at):
        return self.minus[at, :] + jnp.where(self.not_first, pltpu.roll(self.plus[at, :], 1, 1), 0.0)

    def finish_one(self, out, x, dots):
        totals = [None] * 3
        for j in range(BLOCKS):
            base = pl.multiple_of(x * EY, 8) + 8 * j
            inv = self.inverse[pl.ds(base, 8), :]
            sums = None
            for c in range(3):
                at = pl.ds(base + c * SIZE, 8)
                w = self.free[at, :] * self.force(at)
                y = w * inv
                z = self.field[at, :]
                zt = z - y
                self.scaled[at, :] = y
                self.z_stage(out, at, zt)
                if dots is not None:
                    rt = self.load[at, :] - w
                    terms = (z * w, z * rt, zt * rt)
                    sums = terms if sums is None else [p + q for p, q in zip(sums, terms)]
            if dots is not None:
                self.gather(totals, j, sums)
        return dots if dots is None else [p + q for p, q in zip(dots, totals)]

    def finish_two(self, x, dots):
        totals = [None]
        for j in range(BLOCKS):
            base = pl.multiple_of(x * EY, 8) + 8 * j
            sums = None
            for c in range(3):
                at = pl.ds(base + c * SIZE, 8)
                q = self.free[at, :] * self.force(at)
                terms = ((self.field[at, :] - self.scaled[at, :]) * q,)
                sums = terms if sums is None else [p + r for p, r in zip(sums, terms)]
            self.gather(totals, j, sums)
        return [p + q for p, q in zip(dots, totals)]


def clear_edges(above):
    zero = jnp.zeros((8, NZ), f32)

    def body(i, carry):
        above[pl.ds(pl.multiple_of(i * TALL, 8), 8), :] = zero
        return carry

    lax.fori_loop(0, 6 * EX, body, 0, unroll=8)


def clear_row_past(refs, x):
    for ref in refs:
        for c in range(3):
            ref[pl.ds(c * SIZE + x * EY, 8), :] = jnp.zeros((8, NZ), f32)


LAST = CF + NX - 1


def inner_kernel(
    load_in, free_in, ylo, yhi, young, inverse,
    load, free, field, scaled, zsum, zdiff, zsum2, zdiff2, dots_out,
    above, minus, plus,
):
    del load_in, free_in
    for c in range(3):
        base = c * SIZE + CF * EY
        for k in range(2):
            for strip, row in ((ylo, 2 + k), (yhi, 36 + k)):
                load[pl.ds(base + row, NX, stride=EY), :] = strip[pl.ds((c * 2 + k) * NX, NX), :]
        for strip, row in ((ylo, 3), (yhi, 36)):
            free[pl.ds(base + row, NX, stride=EY), :] = strip[pl.ds((6 + c) * NX, NX), :]
    stages = Stages(load, free, inverse, field, scaled, minus, plus)
    first, second = (zsum, zdiff), (zsum2, zdiff2)

    def prepare(x, carry):
        stages.prepare(first, x)
        return carry

    lax.fori_loop(CF, LAST + 1, prepare, 0, unroll=4)
    clear_row_past(first, LAST + 1)
    clear_edges(above)
    operator_pass(zsum, zdiff, young, above, minus, plus, CF, LAST, 7)
    dots = lax.fori_loop(
        CF + 1, LAST, lambda x, d: stages.finish_one(second, x, d), [jnp.zeros((8, NZ), f32)] * 3, unroll=7
    )
    for k, d in enumerate(dots):
        dots_out[k] = d


def outer_kernel(
    load_in, free_in, field_in, scaled_in, zsum_in, zdiff_in, zsum2_in, zdiff2_in,
    xlo, xhi, young, inverse, dots_in,
    load, free, field, scaled, zsum, zdiff, zsum2, zdiff2, dots_out,
    above, minus, plus,
):
    del load_in, free_in, field_in, scaled_in, zsum_in, zdiff_in, zsum2_in, zdiff2_in
    for c in range(3):
        for k in range(2):
            for plane, x in ((xlo, 2 + k), (xhi, LAST + 1 + k)):
                load[pl.ds(c * SIZE + x * EY, EY), :] = plane[pl.ds((c * 2 + k) * EY, EY), :]
        for plane, x in ((xlo, 3), (xhi, LAST + 1)):
            free[pl.ds(c * SIZE + x * EY, EY), :] = plane[pl.ds((6 + c) * EY, EY), :]
    stages = Stages(load, free, inverse, field, scaled, minus, plus)
    first, second = (zsum, zdiff), (zsum2, zdiff2)
    for start in (2, LAST + 1):
        stages.prepare(first, start)
        stages.prepare(first, start + 1)
    clear_row_past(first, LAST + 3)
    clear_row_past(second, LAST + 2)
    clear_edges(above)
    operator_pass(zsum, zdiff, young, above, minus, plus, 2, CF + 1, 2)
    operator_pass(zsum, zdiff, young, above, minus, plus, LAST - 1, LAST + 2, 2)
    stages.finish_one(second, CF - 1, None)
    stages.finish_one(second, LAST + 1, None)
    dots = [dots_in[k] for k in range(3)]
    for x in (CF, LAST):
        dots = stages.finish_one(second, x, dots)

    operator_pass(zsum2, zdiff2, young, above, minus, plus, CF - 1, LAST + 1, 8)
    dots = dots + lax.fori_loop(CF, LAST + 1, stages.finish_two, [jnp.zeros((8, NZ), f32)], unroll=4)
    one = lax.broadcasted_iota(jnp.int32, (1, NZ), 1)
    line = jnp.zeros((1, NZ), f32)
    for k, d in enumerate(dots):
        line = jnp.where(one == k, jnp.sum(d), line)
    dots_out[...] = line


def final_kernel(parts, z, y, out, out_v, sem):
    total = jnp.sum(parts[...], axis=0, keepdims=True)
    lane = lax.broadcasted_iota(jnp.int32, (1, NZ), 1)
    zw, a, b, c = (
        jnp.sum(jnp.where(lane == k, total, 0.0), axis=1, keepdims=True) for k in range(QUANTITIES)
    )
    rz = zw + a
    alpha = rz / zw
    less = -(a / zw)
    rz1 = alpha * (alpha * b + less * a)
    energy = less * (less * zw) + 2.0 * alpha * (less * (a - b)) + alpha * (alpha * c)
    beta = rz1 / rz
    alpha1 = rz1 / (energy - beta * (rz1 / alpha))
    c1 = jnp.broadcast_to(alpha + alpha1 * (1.0 + beta), (8, NZ))[0:1, :]
    c2 = jnp.broadcast_to(-(alpha * alpha1), (8, NZ))[0:1, :]
    copies = []
    for c in range(3):
        def body(x, carry, c=c):
            src = pl.ds(c * SIZE + (x + CF) * EY + CF, NY)
            to = pl.ds(pl.multiple_of((c * NX + x) * NY, NY), NY)
            out_v[to, :] = c1 * z[src, :] + c2 * y[src, :]
            return carry

        lax.fori_loop(0, NX, body, 0, unroll=4)
        rows = pl.ds(c * NX * NY, NX * NY)
        copy = pltpu.make_async_copy(out_v.at[rows, :], out.at[rows, :], sem.at[c])
        copy.start()
        copies.append(copy)
    for copy in copies:
        copy.wait()


def per_device(
    body_force, fixed_dofs, load_nodes, load_forces, frequencies,
    hidden_weights, hidden_biases, output_weights, output_bias,
):
    bx, by = place()
    rows = 3 * NX * NY
    body = body_force.reshape(rows, NZ)
    fixed = fixed_dofs.reshape(rows, NZ)
    nodes = load_nodes.T
    strip = shape(9 * NX, NZ)
    ext = shape(3 * SIZE, NZ)
    load, free, ylo_send, yhi_send = call(
        pack_kernel, (ext, ext, strip, strip),
        [pltpu.HBM] * 4, (nodes, load_forces, body, fixed),
        scratch=[VMEM((rows, NZ), f32), VMEM((rows, NZ), jnp.int32), VMEM((3, LOADS), jnp.int32),
                 SMEM((3, LOADS), jnp.int32), SMEM((3, LOADS), f32), SMEM((LOADS,), jnp.int32), pltpu.SemaphoreType.DMA((9,))],
        cost=pl.CostEstimate(flops=400000, transcendentals=0, bytes_accessed=2400000),
    )
    ny, nx = lax.axis_size("gy"), lax.axis_size("gx")
    def swap(lo_send, hi_send, axis, count, place):
        even = place % 2 == 0
        one = [(i, i ^ 1) for i in range(count)]
        two = [(i, j) for i in range(1, count - 1) for j in (i + 1 if i % 2 else i - 1,)]
        a = lax.ppermute(jnp.where(even, hi_send, lo_send), axis, one)
        b = lax.ppermute(jnp.where(even, lo_send, hi_send), axis, two)
        return jnp.where(even, b, a), jnp.where(even, a, b)

    ylo, yhi = swap(ylo_send, yhi_send, "gy", ny, by)

    coarse = call(
        mlp_kernel, shape(GX, 16, 128),
        [VMEM] * 5,
        (frequencies, hidden_weights, hidden_biases, output_weights.reshape(1, 128), output_bias.reshape(1, 1)),
        scratch=[VMEM((16 * GX, 128), f32), VMEM((16 * GX, 128), f32), VMEM((4, 256, 256), jnp.bfloat16)],
        cost=pl.CostEstimate(flops=1500000000, transcendentals=800000, bytes_accessed=300000),
    )
    plane = shape(9 * EY, NZ)
    xlo_send, xhi_send = call(
        planes_kernel, (plane, plane), [VMEM] * 5, (load, free, ylo, yhi, coarse),
    )
    xlo, xhi = swap(xlo_send, xhi_send, "gx", nx, bx)
    young, inverse, density = call(
        density_kernel, (shape(SIZE, NZ), shape(SIZE, NZ), shape(NX * NY, NZ)),
        [VMEM], (coarse,),
        scratch=[VMEM((NX * NY, NZ), f32), pltpu.SemaphoreType.DMA],
        out_spaces=(VMEM, VMEM, pltpu.HBM),
        cost=pl.CostEstimate(flops=8000000, transcendentals=0, bytes_accessed=1300000),
    )
    work = [VMEM((6 * EX * TALL, NZ), f32), VMEM((3 * SIZE, NZ), f32), VMEM((3 * SIZE, NZ), f32)]
    *state, dots = call(
        inner_kernel, (ext,) * 8 + (shape(3, 8, NZ),),
        [VMEM] * 6, (load, free, ylo, yhi, young, inverse),
        scratch=work, aliases={0: 0, 1: 1},
        cost=pl.CostEstimate(flops=60000000, transcendentals=0, bytes_accessed=9000000),
    )
    *state, dots = call(
        outer_kernel, (ext,) * 8 + (shape(1, NZ),),
        [VMEM] * 13, (*state, xlo, xhi, young, inverse, dots),
        scratch=work, aliases={i: i for i in range(8)},
    )
    z, y = state[2], state[3]
    parts = lax.all_to_all(
        jnp.broadcast_to(dots, (nx * ny, NZ)), ("gx", "gy"), 0, 0, tiled=True
    )
    out = call(
        final_kernel, shape(rows, NZ), [VMEM] * 3, (parts, z, y),
        scratch=[VMEM((rows, NZ), f32), pltpu.SemaphoreType.DMA((3,))], out_spaces=pltpu.HBM,
    )
    return out.reshape(3, NX, NY, NZ), density.reshape(NX, NY, NZ)


def solution(mesh):
    return jax.shard_map(
        per_device,
        mesh=mesh,
        in_specs=(P(None, "gx", "gy", None), P(None, "gx", "gy", None)) + (P(),) * 7,
        out_specs=(P(None, "gx", "gy", None), P("gx", "gy", None)),
        check_vma=False,
    )
```

```python
import functools
import math

import jax
import jax.numpy as jnp
from jax import lax
from jax.experimental import pallas as pl
from jax.experimental.pallas import tpu as pltpu
from jax.sharding import PartitionSpec as P

CF = 4
NX, NY, NZ = 16, 32, 128
TOTAL_X, TOTAL_Y = 512, 256
CX, CY, CZ = NX // CF, NY // CF, NZ // CF
GX, GY = CX + 2, CY + 2
EX, EY = GX * CF, GY * CF
SIZE = EX * EY
LOADS = 512
NU, MU = 0.3, 1.0 / 2.6
LAM = 0.3 / (1.3 * 0.4)
RATIO = LAM / MU
DIAG = (LAM + 4.0 * MU) / 9.0
VMEM = pltpu.VMEM
SMEM = pltpu.SMEM
highest = lax.Precision.HIGHEST
f32 = jnp.float32


def spec(space=VMEM):
    return pl.BlockSpec(memory_space=space)


def call(kernel, out_shape, in_spaces, args, scratch=(), cost=None, out_spaces=None, aliases=None, limit=16):
    out_specs = jax.tree.map(lambda _: spec(), out_shape)
    if out_spaces is not None:
        out_specs = jax.tree.map(lambda _, space: spec(space), out_shape, out_spaces)
    args = [
        pltpu.with_memory_space_constraint(a, space) if space is pltpu.HBM else a
        for a, space in zip(args, in_spaces)
    ]
    if out_spaces is not None:
        out_shape = jax.tree.map(
            lambda a, space: pltpu.HBM(a.shape, a.dtype) if space is pltpu.HBM else a, out_shape, out_spaces
        )
    return pl.pallas_call(
        kernel,
        out_shape=out_shape,
        in_specs=[spec(s) for s in in_spaces],
        out_specs=out_specs,
        scratch_shapes=list(scratch),
        input_output_aliases=aliases or {},
        compiler_params=pltpu.CompilerParams(vmem_limit_bytes=limit << 20),
        cost_estimate=cost,
    )(*args)


def place():
    return lax.axis_index("gx"), lax.axis_index("gy")


def shape(*dims):
    return jax.ShapeDtypeStruct(dims, f32)


def pack_kernel(
    nodes, forces, body, fixed,
    load, free, lo_out, hi_out,
    body_v, fixed_v, nodes_v, nodes_s, forces_s, found, sem,
):
    part = NX * NY
    copies = [
        pltpu.make_async_copy(nodes, nodes_v, sem.at[0]),
        pltpu.make_async_copy(nodes, nodes_s, sem.at[1]),
        pltpu.make_async_copy(forces, forces_s, sem.at[2]),
    ]
    for c in range(3):
        for k, (src, dst) in enumerate(((body, body_v), (fixed, fixed_v))):
            rows = pl.ds(c * part, part)
            copies.append(pltpu.make_async_copy(src.at[rows, :], dst.at[rows, :], sem.at[3 + 2 * c + k]))
    for copy in copies:
        copy.start()

    zero = jnp.zeros((8, NZ), f32)

    def clear(x, carry):
        for c in range(3):
            base = pl.multiple_of(c * SIZE + x * EY, 8)
            for ref in (load, free):
                ref[pl.ds(base, 8), :] = zero
                ref[pl.ds(base + EY - 8, 8), :] = zero
        return carry

    lax.fori_loop(CF, CF + NX, clear, 0, unroll=2)

    ids = place()
    start_x = ids[0] * NX
    start_y = ids[1] * NY
    for copy in copies[:3]:
        copy.wait()
    lx = nodes_v[0:1, :] - start_x
    ly = nodes_v[1:2, :] - start_y
    mine = (lx >= 0) & (lx < NX) & (ly >= 0) & (ly < NY)
    index = lax.broadcasted_iota(jnp.int32, (1, LOADS), 1)
    todo = jnp.where(mine, index, LOADS)
    lane = lax.broadcasted_iota(jnp.int32, (1, NZ), 1)

    todos = [todo[:, k * 128 : (k + 1) * 128] for k in range(LOADS // 128)]

    def more(state):
        *heads, _ = state
        return functools.reduce(jnp.minimum, heads) < LOADS

    def collect(state):
        *heads, count = state
        for p in heads:
            found[count] = p
            count = count + jnp.where(p < LOADS, 1, 0)
        return (*(jnp.min(jnp.where(t > p, t, LOADS)) for t, p in zip(todos, heads)), count)

    *_, count = lax.while_loop(more, collect, (*(jnp.min(t) for t in todos), 0))
    for c in range(3):
        for copy in copies[3 + 2 * c : 5 + 2 * c]:
            copy.wait()

        def add_one(i, carry, c=c):
            p = found[i]
            row = pl.ds((c * NX + nodes_s[0, p] - start_x) * NY + nodes_s[1, p] - start_y, 1)
            hit = lane == nodes_s[2, p]
            body_v[row, :] = body_v[row, :] + jnp.where(hit, forces_s[c, p], 0.0)
            return carry

        lax.fori_loop(0, count, add_one, 0)

        def mask(x, carry, c=c):
            src = pl.ds(pl.multiple_of((c * NX + x) * NY, NY), NY)
            dst = pl.ds(c * SIZE + (x + CF) * EY + CF, NY)
            ok = fixed_v[src, :] == 0
            load[dst, :] = jnp.where(ok, body_v[src, :], 0.0)
            free[dst, :] = jnp.where(ok, 1.0, 0.0)
            return carry

        lax.fori_loop(0, NX, mask, 0, unroll=4)
    for c in range(3):
        base = c * SIZE + CF * EY + CF
        for j in range(2):
            to = pl.ds((c * 2 + j) * NX, NX)
            lo_out[to, :] = load[pl.ds(base + j, NX, stride=EY), :]
            hi_out[to, :] = load[pl.ds(base + NY - 2 + j, NX, stride=EY), :]
        to = pl.ds((6 + c) * NX, NX)
        lo_out[to, :] = free[pl.ds(base, NX, stride=EY), :]
        hi_out[to, :] = free[pl.ds(base + NY - 1, NX, stride=EY), :]


def planes_kernel(load, free, ylo, yhi, coarse, lo_out, hi_out):
    del coarse
    for out, first in ((lo_out, CF), (hi_out, CF + NX - 2)):
        for c in range(3):
            for j in range(2):
                x = first + j
                base = (c * 2 + j) * EY
                out[pl.ds(base, EY), :] = load[pl.ds(c * SIZE + x * EY, EY), :]
                for k in range(2):
                    at = pl.ds((c * 2 + k) * NX + x - CF, 1)
                    out[pl.ds(base + 2 + k, 1), :] = ylo[at, :]
                    out[pl.ds(base + 36 + k, 1), :] = yhi[at, :]
            x = CF if first == CF else CF + NX - 1
            base = (6 + c) * EY
            out[pl.ds(base, EY), :] = free[pl.ds(c * SIZE + x * EY, EY), :]
            at = pl.ds((6 + c) * NX + x - CF, 1)
            out[pl.ds(base + 3, 1), :] = ylo[at, :]
            out[pl.ds(base + 36, 1), :] = yhi[at, :]


def split2(v):
    hi = v.astype(jnp.bfloat16)
    return hi, (v - hi.astype(f32)).astype(jnp.bfloat16)


def doubled(w):
    hi, lo = split2(w)
    both = jnp.concatenate([hi, lo], axis=1)
    return jnp.concatenate([both, both], axis=0)


def sine_of_turns(t):
    t = t - jnp.round(t)
    a = jnp.abs(t)
    x = jnp.minimum(a, 0.5 - a) * (2.0 * math.pi)
    x2 = x * x
    p = 1.0 / 6227020800.0
    for k in (39916800.0, 362880.0, 5040.0, 120.0, 6.0, 1.0):
        p = 1.0 / k - x2 * p
    p = x * p
    return jnp.where(t < 0.0, -p, p)


GROUP = 3


def mlp_kernel(freq, weights, biases, wout, bout, coarse, axy, bxy, w2):
    ids = place()
    cx0 = ids[0] * CX - 1
    cy0 = ids[1] * CY - 1
    f = freq[...]
    ff = jnp.concatenate([f, f], axis=1)
    first = lax.broadcasted_iota(jnp.int32, (1, 128), 1) < 64
    quarter = jnp.where(first, 0.0, 0.25)

    def waves(row, start, rows, total):
        i = lax.broadcasted_iota(jnp.int32, (rows, 128), 0) + start
        turns = ff[row : row + 1, :] * ((i.astype(f32) + 0.5) * (1.0 / total))
        turns = turns - jnp.round(turns)
        wave = sine_of_turns(turns + quarter)
        return wave, pltpu.roll(wave, 64, 1)

    wx, ox = waves(0, cx0, 8, TOTAL_X // CF)
    wy, oy = waves(1, cy0, 16, TOTAL_Y // CF)
    wz, oz = waves(2, 0, CZ, CZ)
    cosx, sinx = jnp.where(first, ox, wx), jnp.where(first, wx, ox)
    cosz, sinz = jnp.where(first, oz, wz), jnp.where(first, wz, oz)
    turnedy = jnp.where(first, oy, -oy)
    for i in range(GX):
        c, s = cosx[i : i + 1, :], sinx[i : i + 1, :]
        axy[pl.ds(16 * i, 16), :] = wy * c + turnedy * s
        bxy[pl.ds(16 * i, 16), :] = turnedy * c - wy * s

    for l in range(3):
        w2[l] = doubled(weights[l] * 0.5)
    w2[3] = doubled(jnp.broadcast_to(wout[...], (128, 128)).T)
    pick = lax.broadcasted_iota(jnp.int32, (CZ, 128), 0) == (
        lax.broadcasted_iota(jnp.int32, (CZ, 128), 1) // CF
    )
    row16 = lax.broadcasted_iota(jnp.int32, (16, 128), 0)

    def body(i, carry):
        parts = []
        for k in range(GROUP):
            for j in range(GY):
                at = pl.ds(16 * (GROUP * i + k) + j, 1)
                parts.append(axy[at, :] * cosz + bxy[at, :] * sinz)
        h = jnp.concatenate(parts, axis=0)
        for l in range(4):
            hi, lo = split2(h)
            both = jnp.concatenate([hi, lo], axis=1)
            out = jnp.dot(both, w2[l], preferred_element_type=f32)
            h = out[:, :128] + out[:, 128:]
            if l < 3:
                h = h + biases[l : l + 1, :] * 0.5
                h = h + h * jnp.tanh(h)
        for k in range(GROUP):
            logits = jnp.zeros((16, 128), f32)
            for j in range(GY):
                cell = (k * GY + j) * CZ
                line = jnp.sum(jnp.where(pick, h[cell : cell + CZ, :], 0.0), axis=0, keepdims=True)
                logits = jnp.where(row16 == (j + 15) % 16, line, logits)
            coarse[GROUP * i + k] = 1.0 / (1.0 + jnp.exp(-(logits + bout[...])))
        return carry

    lax.fori_loop(0, GX // GROUP, body, 0)


W0, W1, W2, W3 = 2.0, 1.0, 2.0 - math.sqrt(2.0), 2.0 - math.sqrt(3.0)
SCALE = MU / 16.0


def density_kernel(coarse, young, inverse, density, density_v, sem):
    ids = place()
    lane = lax.broadcasted_iota(jnp.int32, (16, NZ), 1)
    not_last, not_first = lane < NZ - 1, lane > 0
    row16 = lax.broadcasted_iota(jnp.int32, (16, NZ), 0)
    y_cell = ids[1] * CY + jnp.where(row16 == 15, -1, row16)
    inside_y = (y_cell >= 0) & (y_cell < TOTAL_Y // CF)

    ri = lax.broadcasted_iota(jnp.int32, (EY + NY, 144), 0)
    ci = lax.broadcasted_iota(jnp.int32, (EY + NY, 144), 1)
    r = jnp.where(ri < EY, ri, ri - EY + CF)
    oy = r & 3
    kind = jnp.where(oy == 0, 0, jnp.where(oy == 3, 2, 1))
    want = kind * 16 + (((r >> 2) + 15) & 15)
    spread = jnp.where(
        (ci == want) | (ci == want + 48) | (ci == want + 96), 1.0, 0.0
    ).astype(jnp.bfloat16)
    y_fine = ids[1] * NY - CF + lax.broadcasted_iota(jnp.int32, (EY, NZ), 0)
    inside_rows = jnp.where((y_fine >= 0) & (y_fine < TOTAL_Y), SCALE, 0.0)

    def layers(v):
        side = jnp.where(not_last, pltpu.roll(v, NZ - 1, 1), 0.0) + jnp.where(
            not_first, pltpu.roll(v, 1, 1), 0.0
        )
        return W0 * v + W1 * side, W1 * v + W2 * side, W2 * v + W3 * side

    side = jnp.where(not_last, 1.0, 0.0) + jnp.where(not_first, 1.0, 0.0)
    ones = (W0 + W1 * side, W1 + W2 * side, W2 + W3 * side)
    rows_in = jnp.where(inside_y, 1.0, 0.0)
    stacks = []
    for i in range(GX):
        x_cell = ids[0] * CX - 1 + i
        ok_x = (x_cell >= 0) & (x_cell < TOTAL_X // CF)
        inside = jnp.where(inside_y & ok_x, 1.0, 0.0)
        stacks.append((
            layers(jnp.where(inside > 0.0, coarse[i], 0.0)),
            [inside * w for w in ones],
            inside > 0.0,
            jnp.where(ok_x, 1.0, 0.0),
        ))

    for i in range(GX):
        for plane_kind in range(3):
            low = max(i - 1, 0) if plane_kind == 0 else i
            high = min(i + 1, GX - 1) if plane_kind == 2 else i
            sums = []
            for which in range(2):
                here, below, over = stacks[i][which], stacks[low][which], stacks[high][which]
                t0 = here[0] + (below[1] + over[1])
                t1 = here[1] + (below[2] + over[2])
                down = pltpu.roll(t1, 1, 0)
                above = pltpu.roll(t1, 15, 0)
                sums.append((t0 + (down + t1), t0 + (t1 + t1), t0 + (t1 + above)))
            rho = jnp.concatenate(
                [a / jnp.where(stacks[i][2], b, 1.0) for a, b in zip(*sums)], axis=0
            )
            hi = rho.astype(jnp.bfloat16)
            rest = rho - hi.astype(f32)
            mid = rest.astype(jnp.bfloat16)
            lo = (rest - mid.astype(f32)).astype(jnp.bfloat16)
            fine = jnp.dot(spread, jnp.concatenate([hi, mid, lo], axis=0), preferred_element_type=f32)
            ext = fine[:EY, :]
            modulus = (0.02 + 0.98 * (ext * ext * ext)) * (inside_rows * stacks[i][3])
            for ox in {0: (0,), 1: (1, 2), 2: (3,)}[plane_kind]:
                x = i * CF + ox
                young[pl.ds(x * EY, EY), :] = modulus
                if 1 <= i <= CX:
                    density_v[pl.ds((x - CF) * NY, NY), :] = fine[EY:, :]

    copy = pltpu.make_async_copy(density_v, density, sem)
    copy.start()
    lane8 = lax.broadcasted_iota(jnp.int32, (8, NZ), 1) > 0

    def plane(x, carry):
        for j in range(EY // 8):
            at = x * EY + 8 * j
            if j == 0:
                at = pl.multiple_of(at, 8)
            total = (young[pl.ds(at, 8), :] + young[pl.ds(at - 1, 8), :]) + (
                young[pl.ds(at - EY, 8), :] + young[pl.ds(at - EY - 1, 8), :]
            )
            total = total + jnp.where(lane8, pltpu.roll(total, 1, 1), 0.0)
            inverse[pl.ds(at, 8), :] = 1.0 / (DIAG / SCALE * total + 1e-30)
        return carry

    lax.fori_loop(2, 22, plane, 0, unroll=2)
    copy.wait()


QUANTITIES = 4
BLOCKS = EY // 8
TALL = EY + 8


def operator_pass(zsum, zdiff, young, above, minus, plus, begin, end, unroll):
    def block(yb, carry):
        r0 = yb * 8

        def transform(x):
            out = []
            for c in range(3):
                at = c * SIZE + x * EY + r0
                pairs = [(t[pl.ds(at, 8), :], t[pl.ds(at + 1, 8), :]) for t in (zsum, zdiff)]
                out += [v + u for v, u in pairs] + [u - v for v, u in pairs]
            return out

        def modal(x, a, b):
            e1 = young[pl.ds(pl.multiple_of(x * EY + r0, 8), 8), :]
            e3 = e1 * (1.0 / 3.0)
            e31 = e1 * 0.5
            e9 = e1 * ((RATIO + 4.0) / 9.0)
            s = [p + q for p, q in zip(a, b)]
            d = [q - p for p, q in zip(a, b)]
            u = lambda c, p, q, r: (d if p else s)[4 * c + 2 * q + r]
            g = {}
            ux, uy, uz = u(0, 1, 0, 0), u(1, 0, 1, 0), u(2, 0, 0, 1)
            trace = RATIO * (ux + uy + uz)
            g[0, 1, 0, 0] = e1 * ((ux + ux) + trace)
            g[1, 0, 1, 0] = e1 * ((uy + uy) + trace)
            g[2, 0, 0, 1] = e1 * ((uz + uz) + trace)
            g[0, 0, 1, 0] = g[1, 1, 0, 0] = e1 * (u(0, 0, 1, 0) + u(1, 1, 0, 0))
            g[0, 0, 0, 1] = g[2, 1, 0, 0] = e1 * (u(0, 0, 0, 1) + u(2, 1, 0, 0))
            g[1, 0, 0, 1] = g[2, 0, 1, 0] = e1 * (u(1, 0, 0, 1) + u(2, 0, 1, 0))
            for one, two in (
                ((0, 1, 0, 1), (1, 0, 1, 1)),
                ((0, 1, 1, 0), (2, 0, 1, 1)),
                ((1, 1, 1, 0), (2, 1, 0, 1)),
            ):
                p, q = u(*one), u(*two)
                g[one] = e31 * (3.0 * p + q)
                g[two] = e31 * (3.0 * q + p)
            p, q, r = u(0, 0, 1, 1), u(1, 1, 0, 1), u(2, 1, 1, 0)
            total = p + q + r
            g[0, 0, 1, 1] = e3 * (p + total)
            g[1, 1, 0, 1] = e3 * (q + total)
            g[2, 1, 1, 0] = e3 * (r + total)
            for c in range(3):
                g[c, 1, 1, 1] = e9 * u(c, 1, 1, 1)
            return g

        def keep(g):
            out = []
            for c in range(3):
                out.append(g[c, 1, 0, 0])
                for q, r in ((0, 1), (1, 0), (1, 1)):
                    out.append(g[c, 0, q, r] + g[c, 1, q, r])
            return out

        def step(x, state):
            a, held = state
            b = transform(x + 1)
            g = modal(x, a, b)
            for c in range(3):
                f = [held[4 * c] - g[c, 1, 0, 0]]
                for k, (q, r) in enumerate(((0, 1), (1, 0), (1, 1))):
                    f.append((g[c, 0, q, r] - g[c, 1, q, r]) + held[4 * c + 1 + k])
                h = []
                for r in range(2):
                    at = ((2 * c + r) * EX + x) * TALL + 8 + r0
                    above[pl.ds(at, 8), :] = f[r] + f[2 + r]
                    h.append((f[r] - f[2 + r]) + above[pl.ds(at - 1, 8), :])
                rows = pl.ds(pl.multiple_of(c * SIZE + x * EY + r0, 8), 8)
                minus[rows, :] = h[0] - h[1]
                plus[rows, :] = h[0] + h[1]
            return b, keep(g)

        a = transform(begin)
        b = transform(begin + 1)
        lax.fori_loop(begin + 1, end, step, (b, keep(modal(begin, a, b))), unroll=unroll)
        return carry

    lax.fori_loop(0, BLOCKS, block, 0)


class Stages:
    def __init__(self, load, free, inverse, field, scaled, minus, plus):
        self.load, self.free, self.inverse = load, free, inverse
        self.field, self.scaled, self.minus, self.plus = field, scaled, minus, plus
        lane = lax.broadcasted_iota(jnp.int32, (8, NZ), 1)
        row = lax.broadcasted_iota(jnp.int32, (8, NZ), 0)
        self.not_last, self.not_first = lane < NZ - 1, lane > 0
        self.first_rows = jnp.where(row >= CF, 1.0, 0.0)
        self.last_rows = jnp.where(row < CF, 1.0, 0.0)

    def z_stage(self, out, at, v):
        n = jnp.where(self.not_last, pltpu.roll(v, NZ - 1, 1), 0.0)
        out[0][at, :] = v + n
        out[1][at, :] = n - v

    def prepare(self, out, x):
        for j in range(BLOCKS):
            base = pl.multiple_of(x * EY, 8) + 8 * j
            inv = self.inverse[pl.ds(base, 8), :]
            for c in range(3):
                at = pl.ds(base + c * SIZE, 8)
                v = self.load[at, :] * inv
                self.field[at, :] = v
                self.z_stage(out, at, v)

    def gather(self, totals, j, terms):
        for k, t in enumerate(terms):
            if j == 0:
                t = t * self.first_rows
            if j == BLOCKS - 1:
                t = t * self.last_rows
            totals[k] = t if totals[k] is None else totals[k] + t

    def force(self, at):
        return self.minus[at, :] + jnp.where(self.not_first, pltpu.roll(self.plus[at, :], 1, 1), 0.0)

    def finish_one(self, out, x, dots):
        totals = [None] * 3
        for j in range(BLOCKS):
            base = pl.multiple_of(x * EY, 8) + 8 * j
            inv = self.inverse[pl.ds(base, 8), :]
            sums = None
            for c in range(3):
                at = pl.ds(base + c * SIZE, 8)
                w = self.free[at, :] * self.force(at)
                y = w * inv
                z = self.field[at, :]
                zt = z - y
                self.scaled[at, :] = y
                self.z_stage(out, at, zt)
                if dots is not None:
                    rt = self.load[at, :] - w
                    terms = (z * w, z * rt, zt * rt)
                    sums = terms if sums is None else [p + q for p, q in zip(sums, terms)]
            if dots is not None:
                self.gather(totals, j, sums)
        return dots if dots is None else [p + q for p, q in zip(dots, totals)]

    def finish_two(self, x, dots):
        totals = [None]
        for j in range(BLOCKS):
            base = pl.multiple_of(x * EY, 8) + 8 * j
            sums = None
            for c in range(3):
                at = pl.ds(base + c * SIZE, 8)
                q = self.free[at, :] * self.force(at)
                terms = ((self.field[at, :] - self.scaled[at, :]) * q,)
                sums = terms if sums is None else [p + r for p, r in zip(sums, terms)]
            self.gather(totals, j, sums)
        return [p + q for p, q in zip(dots, totals)]


def clear_edges(above):
    zero = jnp.zeros((8, NZ), f32)

    def body(i, carry):
        above[pl.ds(pl.multiple_of(i * TALL, 8), 8), :] = zero
        return carry

    lax.fori_loop(0, 6 * EX, body, 0, unroll=8)


def clear_row_past(refs, x):
    for ref in refs:
        for c in range(3):
            ref[pl.ds(c * SIZE + x * EY, 8), :] = jnp.zeros((8, NZ), f32)


LAST = CF + NX - 1


def inner_kernel(
    load_in, free_in, ylo, yhi, young, inverse,
    load, free, field, scaled, zsum, zdiff, zsum2, zdiff2, dots_out,
    above, minus, plus,
):
    del load_in, free_in
    for c in range(3):
        base = c * SIZE + CF * EY
        for k in range(2):
            for strip, row in ((ylo, 2 + k), (yhi, 36 + k)):
                load[pl.ds(base + row, NX, stride=EY), :] = strip[pl.ds((c * 2 + k) * NX, NX), :]
        for strip, row in ((ylo, 3), (yhi, 36)):
            free[pl.ds(base + row, NX, stride=EY), :] = strip[pl.ds((6 + c) * NX, NX), :]
    stages = Stages(load, free, inverse, field, scaled, minus, plus)
    first, second = (zsum, zdiff), (zsum2, zdiff2)

    def prepare(x, carry):
        stages.prepare(first, x)
        return carry

    lax.fori_loop(CF, LAST + 1, prepare, 0, unroll=4)
    clear_row_past(first, LAST + 1)
    clear_edges(above)
    operator_pass(zsum, zdiff, young, above, minus, plus, CF, LAST, 7)
    dots = lax.fori_loop(
        CF + 1, LAST, lambda x, d: stages.finish_one(second, x, d), [jnp.zeros((8, NZ), f32)] * 3, unroll=7
    )
    clear_row_past(second, LAST)
    operator_pass(zsum2, zdiff2, young, above, minus, plus, CF + 1, LAST - 1, 6)
    dots = dots + lax.fori_loop(CF + 2, LAST - 1, stages.finish_two, [jnp.zeros((8, NZ), f32)], unroll=4)
    for k, d in enumerate(dots):
        dots_out[k] = d


def outer_kernel(
    load_in, free_in, field_in, scaled_in, zsum_in, zdiff_in, zsum2_in, zdiff2_in,
    xlo, xhi, young, inverse, dots_in,
    load, free, field, scaled, zsum, zdiff, zsum2, zdiff2, dots_out,
    above, minus, plus,
):
    del load_in, free_in, field_in, scaled_in, zsum_in, zdiff_in, zsum2_in, zdiff2_in
    for c in range(3):
        for k in range(2):
            for plane, x in ((xlo, 2 + k), (xhi, LAST + 1 + k)):
                load[pl.ds(c * SIZE + x * EY, EY), :] = plane[pl.ds((c * 2 + k) * EY, EY), :]
        for plane, x in ((xlo, 3), (xhi, LAST + 1)):
            free[pl.ds(c * SIZE + x * EY, EY), :] = plane[pl.ds((6 + c) * EY, EY), :]
    stages = Stages(load, free, inverse, field, scaled, minus, plus)
    first, second = (zsum, zdiff), (zsum2, zdiff2)
    for start in (2, LAST + 1):
        stages.prepare(first, start)
        stages.prepare(first, start + 1)
    clear_row_past(first, LAST + 3)
    clear_row_past(second, LAST + 2)
    clear_edges(above)
    operator_pass(zsum, zdiff, young, above, minus, plus, 2, CF + 1, 2)
    operator_pass(zsum, zdiff, young, above, minus, plus, LAST - 1, LAST + 2, 2)
    stages.finish_one(second, CF - 1, None)
    stages.finish_one(second, LAST + 1, None)
    dots = [dots_in[k] for k in range(3)]
    for x in (CF, LAST):
        dots = stages.finish_one(second, x, dots)

    operator_pass(zsum2, zdiff2, young, above, minus, plus, CF - 1, CF + 2, 2)
    operator_pass(zsum2, zdiff2, young, above, minus, plus, LAST - 2, LAST + 1, 2)
    last = [dots_in[3]]
    for x in (CF, CF + 1, LAST - 1, LAST):
        last = stages.finish_two(x, last)
    dots = dots + last
    one = lax.broadcasted_iota(jnp.int32, (1, NZ), 1)
    line = jnp.zeros((1, NZ), f32)
    for k, d in enumerate(dots):
        line = jnp.where(one == k, jnp.sum(d), line)
    dots_out[...] = line


def final_kernel(parts, z, y, out, out_v, sem):
    total = jnp.sum(parts[...], axis=0, keepdims=True)
    lane = lax.broadcasted_iota(jnp.int32, (1, NZ), 1)
    zw, a, b, c = (
        jnp.sum(jnp.where(lane == k, total, 0.0), axis=1, keepdims=True) for k in range(QUANTITIES)
    )
    rz = zw + a
    alpha = rz / zw
    less = -(a / zw)
    rz1 = alpha * (alpha * b + less * a)
    energy = less * (less * zw) + 2.0 * alpha * (less * (a - b)) + alpha * (alpha * c)
    beta = rz1 / rz
    alpha1 = rz1 / (energy - beta * (rz1 / alpha))
    c1 = jnp.broadcast_to(alpha + alpha1 * (1.0 + beta), (8, NZ))[0:1, :]
    c2 = jnp.broadcast_to(-(alpha * alpha1), (8, NZ))[0:1, :]
    copies = []
    half = NX // 2
    for k in range(6):
        c, begin = k // 2, (k % 2) * half

        def body(x, carry, c=c):
            src = pl.ds(c * SIZE + (x + CF) * EY + CF, NY)
            to = pl.ds(pl.multiple_of((c * NX + x) * NY, NY), NY)
            out_v[to, :] = c1 * z[src, :] + c2 * y[src, :]
            return carry

        lax.fori_loop(begin, begin + half, body, 0, unroll=4)
        rows = pl.ds(k * half * NY, half * NY)
        copy = pltpu.make_async_copy(out_v.at[rows, :], out.at[rows, :], sem.at[k])
        copy.start()
        copies.append(copy)
    for copy in copies:
        copy.wait()


def per_device(
    body_force, fixed_dofs, load_nodes, load_forces, frequencies,
    hidden_weights, hidden_biases, output_weights, output_bias,
):
    bx, by = place()
    rows = 3 * NX * NY
    body = body_force.reshape(rows, NZ)
    fixed = fixed_dofs.reshape(rows, NZ)
    nodes = load_nodes.T
    strip = shape(9 * NX, NZ)
    ext = shape(3 * SIZE, NZ)
    load, free, ylo_send, yhi_send = call(
        pack_kernel, (ext, ext, strip, strip),
        [pltpu.HBM] * 4, (nodes, load_forces, body, fixed),
        scratch=[VMEM((rows, NZ), f32), VMEM((rows, NZ), jnp.int32), VMEM((3, LOADS), jnp.int32),
                 SMEM((3, LOADS), jnp.int32), SMEM((3, LOADS), f32), SMEM((LOADS + 8,), jnp.int32), pltpu.SemaphoreType.DMA((9,))],
        cost=pl.CostEstimate(flops=400000, transcendentals=0, bytes_accessed=2400000),
    )
    ny, nx = lax.axis_size("gy"), lax.axis_size("gx")
    def swap(lo_send, hi_send, axis, count, place):
        even = place % 2 == 0
        one = [(i, i ^ 1) for i in range(count)]
        two = [(i, j) for i in range(1, count - 1) for j in (i + 1 if i % 2 else i - 1,)]
        a = lax.ppermute(jnp.where(even, hi_send, lo_send), axis, one)
        b = lax.ppermute(jnp.where(even, lo_send, hi_send), axis, two)
        return jnp.where(even, b, a), jnp.where(even, a, b)

    ylo, yhi = swap(ylo_send, yhi_send, "gy", ny, by)

    coarse = call(
        mlp_kernel, shape(GX, 16, 128),
        [VMEM] * 5,
        (frequencies, hidden_weights, hidden_biases, output_weights.reshape(1, 128), output_bias.reshape(1, 1)),
        scratch=[VMEM((16 * GX, 128), f32), VMEM((16 * GX, 128), f32), VMEM((4, 256, 256), jnp.bfloat16)],
        cost=pl.CostEstimate(flops=1500000000, transcendentals=800000, bytes_accessed=300000),
    )
    plane = shape(9 * EY, NZ)
    xlo_send, xhi_send = call(
        planes_kernel, (plane, plane), [VMEM] * 5, (load, free, ylo, yhi, coarse),
    )
    xlo, xhi = swap(xlo_send, xhi_send, "gx", nx, bx)
    young, inverse, density = call(
        density_kernel, (shape(SIZE, NZ), shape(SIZE, NZ), shape(NX * NY, NZ)),
        [VMEM], (coarse,),
        scratch=[VMEM((NX * NY, NZ), f32), pltpu.SemaphoreType.DMA],
        out_spaces=(VMEM, VMEM, pltpu.HBM),
        cost=pl.CostEstimate(flops=8000000, transcendentals=0, bytes_accessed=1300000),
    )
    work = [VMEM((6 * EX * TALL, NZ), f32), VMEM((3 * SIZE, NZ), f32), VMEM((3 * SIZE, NZ), f32)]
    *state, dots = call(
        inner_kernel, (ext,) * 8 + (shape(QUANTITIES, 8, NZ),),
        [VMEM] * 6, (load, free, ylo, yhi, young, inverse),
        scratch=work, aliases={0: 0, 1: 1},
        cost=pl.CostEstimate(flops=60000000, transcendentals=0, bytes_accessed=9000000),
    )
    *state, dots = call(
        outer_kernel, (ext,) * 8 + (shape(1, NZ),),
        [VMEM] * 13, (*state, xlo, xhi, young, inverse, dots),
        scratch=work, aliases={i: i for i in range(8)},
    )
    z, y = state[2], state[3]
    parts = lax.all_to_all(
        jnp.broadcast_to(dots, (nx * ny, NZ)), ("gx", "gy"), 0, 0, tiled=True
    )
    out = call(
        final_kernel, shape(rows, NZ), [VMEM] * 3, (parts, z, y),
        scratch=[VMEM((rows, NZ), f32), pltpu.SemaphoreType.DMA((6,))], out_spaces=pltpu.HBM,
    )
    return out.reshape(3, NX, NY, NZ), density.reshape(NX, NY, NZ)


def solution(mesh):
    return jax.shard_map(
        per_device,
        mesh=mesh,
        in_specs=(P(None, "gx", "gy", None), P(None, "gx", "gy", None)) + (P(),) * 7,
        out_specs=(P(None, "gx", "gy", None), P("gx", "gy", None)),
        check_vma=False,
    )
```

```python
import functools
import math

import jax
import jax.numpy as jnp
from jax import lax
from jax.experimental import pallas as pl
from jax.experimental.pallas import tpu as pltpu
from jax.sharding import PartitionSpec as P

CF = 4
NX, NY, NZ = 16, 32, 128
TOTAL_X, TOTAL_Y = 512, 256
CX, CY, CZ = NX // CF, NY // CF, NZ // CF
GX, GY = CX + 2, CY + 2
EX, EY = GX * CF, GY * CF
SIZE = EX * EY
LOADS = 512
NU, MU = 0.3, 1.0 / 2.6
LAM = 0.3 / (1.3 * 0.4)
RATIO = LAM / MU
DIAG = (LAM + 4.0 * MU) / 9.0
VMEM = pltpu.VMEM
SMEM = pltpu.SMEM
highest = lax.Precision.HIGHEST
f32 = jnp.float32


def spec(space=VMEM):
    return pl.BlockSpec(memory_space=space)


def call(kernel, out_shape, in_spaces, args, scratch=(), cost=None, out_spaces=None, aliases=None, limit=16):
    out_specs = jax.tree.map(lambda _: spec(), out_shape)
    if out_spaces is not None:
        out_specs = jax.tree.map(lambda _, space: spec(space), out_shape, out_spaces)
    args = [
        pltpu.with_memory_space_constraint(a, space) if space is pltpu.HBM else a
        for a, space in zip(args, in_spaces)
    ]
    if out_spaces is not None:
        out_shape = jax.tree.map(
            lambda a, space: pltpu.HBM(a.shape, a.dtype) if space is pltpu.HBM else a, out_shape, out_spaces
        )
    return pl.pallas_call(
        kernel,
        out_shape=out_shape,
        in_specs=[spec(s) for s in in_spaces],
        out_specs=out_specs,
        scratch_shapes=list(scratch),
        input_output_aliases=aliases or {},
        compiler_params=pltpu.CompilerParams(vmem_limit_bytes=limit << 20),
        cost_estimate=cost,
    )(*args)


def place():
    return lax.axis_index("gx"), lax.axis_index("gy")


def shape(*dims):
    return jax.ShapeDtypeStruct(dims, f32)


def pack_kernel(
    nodes, forces, body, fixed,
    load, free, lo_out, hi_out,
    body_v, fixed_v, nodes_v, nodes_s, forces_s, found, sem,
):
    part = NX * NY
    copies = [
        pltpu.make_async_copy(nodes, nodes_v, sem.at[0]),
        pltpu.make_async_copy(nodes, nodes_s, sem.at[1]),
        pltpu.make_async_copy(forces, forces_s, sem.at[2]),
    ]
    for c in range(3):
        for k, (src, dst) in enumerate(((body, body_v), (fixed, fixed_v))):
            rows = pl.ds(c * part, part)
            copies.append(pltpu.make_async_copy(src.at[rows, :], dst.at[rows, :], sem.at[3 + 2 * c + k]))
    for copy in copies:
        copy.start()

    zero = jnp.zeros((8, NZ), f32)

    def clear(x, carry):
        for c in range(3):
            base = pl.multiple_of(c * SIZE + x * EY, 8)
            for ref in (load, free):
                ref[pl.ds(base, 8), :] = zero
                ref[pl.ds(base + EY - 8, 8), :] = zero
        return carry

    lax.fori_loop(CF, CF + NX, clear, 0, unroll=2)

    ids = place()
    start_x = ids[0] * NX
    start_y = ids[1] * NY
    for copy in copies[:3]:
        copy.wait()
    lx = nodes_v[0:1, :] - start_x
    ly = nodes_v[1:2, :] - start_y
    mine = (lx >= 0) & (lx < NX) & (ly >= 0) & (ly < NY)
    index = lax.broadcasted_iota(jnp.int32, (1, LOADS), 1)
    todo = jnp.where(mine, index, LOADS)
    lane = lax.broadcasted_iota(jnp.int32, (1, NZ), 1)

    todos = [todo[:, k * 128 : (k + 1) * 128] for k in range(LOADS // 128)]

    def more(state):
        *heads, _ = state
        return functools.reduce(jnp.minimum, heads) < LOADS

    def collect(state):
        *heads, count = state
        for p in heads:
            found[count] = p
            count = count + jnp.where(p < LOADS, 1, 0)
        return (*(jnp.min(jnp.where(t > p, t, LOADS)) for t, p in zip(todos, heads)), count)

    *_, count = lax.while_loop(more, collect, (*(jnp.min(t) for t in todos), 0))
    for c in range(3):
        for copy in copies[3 + 2 * c : 5 + 2 * c]:
            copy.wait()

        def add_one(i, carry, c=c):
            p = found[i]
            row = pl.ds((c * NX + nodes_s[0, p] - start_x) * NY + nodes_s[1, p] - start_y, 1)
            hit = lane == nodes_s[2, p]
            body_v[row, :] = body_v[row, :] + jnp.where(hit, forces_s[c, p], 0.0)
            return carry

        lax.fori_loop(0, count, add_one, 0)

        def mask(x, carry, c=c):
            src = pl.ds(pl.multiple_of((c * NX + x) * NY, NY), NY)
            dst = pl.ds(c * SIZE + (x + CF) * EY + CF, NY)
            ok = fixed_v[src, :] == 0
            load[dst, :] = jnp.where(ok, body_v[src, :], 0.0)
            free[dst, :] = jnp.where(ok, 1.0, 0.0)
            return carry

        lax.fori_loop(0, NX, mask, 0, unroll=4)
    for c in range(3):
        base = c * SIZE + CF * EY + CF
        for j in range(2):
            to = pl.ds((c * 2 + j) * NX, NX)
            lo_out[to, :] = load[pl.ds(base + j, NX, stride=EY), :]
            hi_out[to, :] = load[pl.ds(base + NY - 2 + j, NX, stride=EY), :]
        to = pl.ds((6 + c) * NX, NX)
        lo_out[to, :] = free[pl.ds(base, NX, stride=EY), :]
        hi_out[to, :] = free[pl.ds(base + NY - 1, NX, stride=EY), :]


def planes_kernel(load, free, ylo, yhi, coarse, lo_out, hi_out):
    del coarse
    for out, first in ((lo_out, CF), (hi_out, CF + NX - 2)):
        for c in range(3):
            for j in range(2):
                x = first + j
                base = (c * 2 + j) * EY
                out[pl.ds(base, EY), :] = load[pl.ds(c * SIZE + x * EY, EY), :]
                for k in range(2):
                    at = pl.ds((c * 2 + k) * NX + x - CF, 1)
                    out[pl.ds(base + 2 + k, 1), :] = ylo[at, :]
                    out[pl.ds(base + 36 + k, 1), :] = yhi[at, :]
            x = CF if first == CF else CF + NX - 1
            base = (6 + c) * EY
            out[pl.ds(base, EY), :] = free[pl.ds(c * SIZE + x * EY, EY), :]
            at = pl.ds((6 + c) * NX + x - CF, 1)
            out[pl.ds(base + 3, 1), :] = ylo[at, :]
            out[pl.ds(base + 36, 1), :] = yhi[at, :]


def split2(v):
    hi = v.astype(jnp.bfloat16)
    return hi, (v - hi.astype(f32)).astype(jnp.bfloat16)


def doubled(w):
    hi, lo = split2(w)
    both = jnp.concatenate([hi, lo], axis=1)
    return jnp.concatenate([both, both], axis=0)


def sine_of_turns(t):
    t = t - jnp.round(t)
    a = jnp.abs(t)
    x = jnp.minimum(a, 0.5 - a) * (2.0 * math.pi)
    x2 = x * x
    p = 1.0 / 6227020800.0
    for k in (39916800.0, 362880.0, 5040.0, 120.0, 6.0, 1.0):
        p = 1.0 / k - x2 * p
    p = x * p
    return jnp.where(t < 0.0, -p, p)


GROUP = 3


def mlp_kernel(freq, weights, biases, wout, bout, coarse, axy, bxy, w2):
    ids = place()
    cx0 = ids[0] * CX - 1
    cy0 = ids[1] * CY - 1
    f = freq[...]
    ff = jnp.concatenate([f, f], axis=1)
    first = lax.broadcasted_iota(jnp.int32, (1, 128), 1) < 64
    quarter = jnp.where(first, 0.0, 0.25)

    def waves(row, start, rows, total):
        i = lax.broadcasted_iota(jnp.int32, (rows, 128), 0) + start
        turns = ff[row : row + 1, :] * ((i.astype(f32) + 0.5) * (1.0 / total))
        turns = turns - jnp.round(turns)
        wave = sine_of_turns(turns + quarter)
        return wave, pltpu.roll(wave, 64, 1)

    wx, ox = waves(0, cx0, 8, TOTAL_X // CF)
    wy, oy = waves(1, cy0, 16, TOTAL_Y // CF)
    wz, oz = waves(2, 0, CZ, CZ)
    cosx, sinx = jnp.where(first, ox, wx), jnp.where(first, wx, ox)
    cosz, sinz = jnp.where(first, oz, wz), jnp.where(first, wz, oz)
    turnedy = jnp.where(first, oy, -oy)
    for i in range(GX):
        c, s = cosx[i : i + 1, :], sinx[i : i + 1, :]
        axy[pl.ds(16 * i, 16), :] = wy * c + turnedy * s
        bxy[pl.ds(16 * i, 16), :] = turnedy * c - wy * s

    for l in range(3):
        w2[l] = doubled(weights[l] * 0.5)
    w2[3] = doubled(jnp.broadcast_to(wout[...], (128, 128)).T)
    pick = lax.broadcasted_iota(jnp.int32, (CZ, 128), 0) == (
        lax.broadcasted_iota(jnp.int32, (CZ, 128), 1) // CF
    )
    row16 = lax.broadcasted_iota(jnp.int32, (16, 128), 0)

    def body(i, carry):
        parts = []
        for k in range(GROUP):
            for j in range(GY):
                at = pl.ds(16 * (GROUP * i + k) + j, 1)
                parts.append(axy[at, :] * cosz + bxy[at, :] * sinz)
        h = jnp.concatenate(parts, axis=0)
        for l in range(4):
            hi, lo = split2(h)
            both = jnp.concatenate([hi, lo], axis=1)
            out = jnp.dot(both, w2[l], preferred_element_type=f32)
            h = out[:, :128] + out[:, 128:]
            if l < 3:
                h = h + biases[l : l + 1, :] * 0.5
                h = h + h * jnp.tanh(h)
        for k in range(GROUP):
            logits = jnp.zeros((16, 128), f32)
            for j in range(GY):
                cell = (k * GY + j) * CZ
                line = jnp.sum(jnp.where(pick, h[cell : cell + CZ, :], 0.0), axis=0, keepdims=True)
                logits = jnp.where(row16 == (j + 15) % 16, line, logits)
            coarse[GROUP * i + k] = 1.0 / (1.0 + jnp.exp(-(logits + bout[...])))
        return carry

    lax.fori_loop(0, GX // GROUP, body, 0)


W0, W1, W2, W3 = 2.0, 1.0, 2.0 - math.sqrt(2.0), 2.0 - math.sqrt(3.0)
SCALE = MU / 16.0


def density_kernel(coarse, young, inverse, density, density_v, sem):
    ids = place()
    lane = lax.broadcasted_iota(jnp.int32, (16, NZ), 1)
    not_last, not_first = lane < NZ - 1, lane > 0
    row16 = lax.broadcasted_iota(jnp.int32, (16, NZ), 0)
    y_cell = ids[1] * CY + jnp.where(row16 == 15, -1, row16)
    inside_y = (y_cell >= 0) & (y_cell < TOTAL_Y // CF)

    ri = lax.broadcasted_iota(jnp.int32, (EY + NY, 144), 0)
    ci = lax.broadcasted_iota(jnp.int32, (EY + NY, 144), 1)
    r = jnp.where(ri < EY, ri, ri - EY + CF)
    oy = r & 3
    kind = jnp.where(oy == 0, 0, jnp.where(oy == 3, 2, 1))
    want = kind * 16 + (((r >> 2) + 15) & 15)
    spread = jnp.where(
        (ci == want) | (ci == want + 48) | (ci == want + 96), 1.0, 0.0
    ).astype(jnp.bfloat16)
    y_fine = ids[1] * NY - CF + lax.broadcasted_iota(jnp.int32, (EY, NZ), 0)
    inside_rows = jnp.where((y_fine >= 0) & (y_fine < TOTAL_Y), SCALE, 0.0)

    def layers(v):
        side = jnp.where(not_last, pltpu.roll(v, NZ - 1, 1), 0.0) + jnp.where(
            not_first, pltpu.roll(v, 1, 1), 0.0
        )
        return W0 * v + W1 * side, W1 * v + W2 * side, W2 * v + W3 * side

    side = jnp.where(not_last, 1.0, 0.0) + jnp.where(not_first, 1.0, 0.0)
    ones = (W0 + W1 * side, W1 + W2 * side, W2 + W3 * side)
    rows_in = jnp.where(inside_y, 1.0, 0.0)
    stacks = []
    for i in range(GX):
        x_cell = ids[0] * CX - 1 + i
        ok_x = (x_cell >= 0) & (x_cell < TOTAL_X // CF)
        inside = jnp.where(inside_y & ok_x, 1.0, 0.0)
        stacks.append((
            layers(jnp.where(inside > 0.0, coarse[i], 0.0)),
            [inside * w for w in ones],
            inside > 0.0,
            jnp.where(ok_x, 1.0, 0.0),
        ))

    for i in range(GX):
        for plane_kind in range(3):
            low = max(i - 1, 0) if plane_kind == 0 else i
            high = min(i + 1, GX - 1) if plane_kind == 2 else i
            sums = []
            for which in range(2):
                here, below, over = stacks[i][which], stacks[low][which], stacks[high][which]
                t0 = here[0] + (below[1] + over[1])
                t1 = here[1] + (below[2] + over[2])
                down = pltpu.roll(t1, 1, 0)
                above = pltpu.roll(t1, 15, 0)
                sums.append((t0 + (down + t1), t0 + (t1 + t1), t0 + (t1 + above)))
            rho = jnp.concatenate(
                [a / jnp.where(stacks[i][2], b, 1.0) for a, b in zip(*sums)], axis=0
            )
            hi = rho.astype(jnp.bfloat16)
            rest = rho - hi.astype(f32)
            mid = rest.astype(jnp.bfloat16)
            lo = (rest - mid.astype(f32)).astype(jnp.bfloat16)
            fine = jnp.dot(spread, jnp.concatenate([hi, mid, lo], axis=0), preferred_element_type=f32)
            ext = fine[:EY, :]
            modulus = (0.02 + 0.98 * (ext * ext * ext)) * (inside_rows * stacks[i][3])
            for ox in {0: (0,), 1: (1, 2), 2: (3,)}[plane_kind]:
                x = i * CF + ox
                young[pl.ds(x * EY, EY), :] = modulus
                if 1 <= i <= CX:
                    density_v[pl.ds((x - CF) * NY, NY), :] = fine[EY:, :]

    copy = pltpu.make_async_copy(density_v, density, sem)
    copy.start()
    lane8 = lax.broadcasted_iota(jnp.int32, (8, NZ), 1) > 0

    def plane(x, carry):
        for j in range(EY // 8):
            at = x * EY + 8 * j
            if j == 0:
                at = pl.multiple_of(at, 8)
            total = (young[pl.ds(at, 8), :] + young[pl.ds(at - 1, 8), :]) + (
                young[pl.ds(at - EY, 8), :] + young[pl.ds(at - EY - 1, 8), :]
            )
            total = total + jnp.where(lane8, pltpu.roll(total, 1, 1), 0.0)
            inverse[pl.ds(at, 8), :] = 1.0 / (DIAG / SCALE * total + 1e-30)
        return carry

    lax.fori_loop(2, 22, plane, 0, unroll=2)
    copy.wait()


QUANTITIES = 4
BLOCKS = EY // 8
TALL = EY + 8


def operator_pass(zsum, zdiff, young, above, minus, plus, begin, end, unroll):
    def block(yb, carry):
        r0 = yb * 8

        def transform(x):
            out = []
            for c in range(3):
                at = c * SIZE + x * EY + r0
                pairs = [(t[pl.ds(at, 8), :], t[pl.ds(at + 1, 8), :]) for t in (zsum, zdiff)]
                out += [v + u for v, u in pairs] + [u - v for v, u in pairs]
            return out

        def modal(x, a, b):
            e1 = young[pl.ds(pl.multiple_of(x * EY + r0, 8), 8), :]
            e3 = e1 * (1.0 / 3.0)
            e31 = e1 * 0.5
            e9 = e1 * ((RATIO + 4.0) / 9.0)
            s = [p + q for p, q in zip(a, b)]
            d = [q - p for p, q in zip(a, b)]
            u = lambda c, p, q, r: (d if p else s)[4 * c + 2 * q + r]
            g = {}
            ux, uy, uz = u(0, 1, 0, 0), u(1, 0, 1, 0), u(2, 0, 0, 1)
            trace = RATIO * (ux + uy + uz)
            g[0, 1, 0, 0] = e1 * ((ux + ux) + trace)
            g[1, 0, 1, 0] = e1 * ((uy + uy) + trace)
            g[2, 0, 0, 1] = e1 * ((uz + uz) + trace)
            g[0, 0, 1, 0] = g[1, 1, 0, 0] = e1 * (u(0, 0, 1, 0) + u(1, 1, 0, 0))
            g[0, 0, 0, 1] = g[2, 1, 0, 0] = e1 * (u(0, 0, 0, 1) + u(2, 1, 0, 0))
            g[1, 0, 0, 1] = g[2, 0, 1, 0] = e1 * (u(1, 0, 0, 1) + u(2, 0, 1, 0))
            for one, two in (
                ((0, 1, 0, 1), (1, 0, 1, 1)),
                ((0, 1, 1, 0), (2, 0, 1, 1)),
                ((1, 1, 1, 0), (2, 1, 0, 1)),
            ):
                p, q = u(*one), u(*two)
                g[one] = e31 * (3.0 * p + q)
                g[two] = e31 * (3.0 * q + p)
            p, q, r = u(0, 0, 1, 1), u(1, 1, 0, 1), u(2, 1, 1, 0)
            total = p + q + r
            g[0, 0, 1, 1] = e3 * (p + total)
            g[1, 1, 0, 1] = e3 * (q + total)
            g[2, 1, 1, 0] = e3 * (r + total)
            for c in range(3):
                g[c, 1, 1, 1] = e9 * u(c, 1, 1, 1)
            return g

        def keep(g):
            out = []
            for c in range(3):
                out.append(g[c, 1, 0, 0])
                for q, r in ((0, 1), (1, 0), (1, 1)):
                    out.append(g[c, 0, q, r] + g[c, 1, q, r])
            return out

        def step(x, state):
            a, held = state
            b = transform(x + 1)
            g = modal(x, a, b)
            for c in range(3):
                f = [held[4 * c] - g[c, 1, 0, 0]]
                for k, (q, r) in enumerate(((0, 1), (1, 0), (1, 1))):
                    f.append((g[c, 0, q, r] - g[c, 1, q, r]) + held[4 * c + 1 + k])
                h = []
                for r in range(2):
                    at = ((2 * c + r) * EX + x) * TALL + 8 + r0
                    above[pl.ds(at, 8), :] = f[r] + f[2 + r]
                    h.append((f[r] - f[2 + r]) + above[pl.ds(at - 1, 8), :])
                rows = pl.ds(pl.multiple_of(c * SIZE + x * EY + r0, 8), 8)
                minus[rows, :] = h[0] - h[1]
                plus[rows, :] = h[0] + h[1]
            return b, keep(g)

        a = transform(begin)
        b = transform(begin + 1)
        lax.fori_loop(begin + 1, end, step, (b, keep(modal(begin, a, b))), unroll=unroll)
        return carry

    lax.fori_loop(0, BLOCKS, block, 0)


class Stages:
    def __init__(self, load, free, inverse, field, scaled, minus, plus):
        self.load, self.free, self.inverse = load, free, inverse
        self.field, self.scaled, self.minus, self.plus = field, scaled, minus, plus
        lane = lax.broadcasted_iota(jnp.int32, (8, NZ), 1)
        row = lax.broadcasted_iota(jnp.int32, (8, NZ), 0)
        self.not_last, self.not_first = lane < NZ - 1, lane > 0
        self.first_rows = jnp.where(row >= CF, 1.0, 0.0)
        self.last_rows = jnp.where(row < CF, 1.0, 0.0)

    def z_stage(self, out, at, v):
        n = jnp.where(self.not_last, pltpu.roll(v, NZ - 1, 1), 0.0)
        out[0][at, :] = v + n
        out[1][at, :] = n - v

    def prepare(self, out, x):
        for j in range(BLOCKS):
            base = pl.multiple_of(x * EY, 8) + 8 * j
            inv = self.inverse[pl.ds(base, 8), :]
            for c in range(3):
                at = pl.ds(base + c * SIZE, 8)
                v = self.load[at, :] * inv
                self.field[at, :] = v
                self.z_stage(out, at, v)

    def gather(self, totals, j, terms):
        for k, t in enumerate(terms):
            if j == 0:
                t = t * self.first_rows
            if j == BLOCKS - 1:
                t = t * self.last_rows
            totals[k] = t if totals[k] is None else totals[k] + t

    def force(self, at):
        return self.minus[at, :] + jnp.where(self.not_first, pltpu.roll(self.plus[at, :], 1, 1), 0.0)

    def finish_one(self, out, x, dots):
        totals = [None] * 3
        for j in range(BLOCKS):
            base = pl.multiple_of(x * EY, 8) + 8 * j
            inv = self.inverse[pl.ds(base, 8), :]
            sums = None
            for c in range(3):
                at = pl.ds(base + c * SIZE, 8)
                w = self.free[at, :] * self.force(at)
                y = w * inv
                z = self.field[at, :]
                zt = z - y
                self.scaled[at, :] = y
                self.z_stage(out, at, zt)
                if dots is not None:
                    rt = self.load[at, :] - w
                    terms = (z * w, z * rt, zt * rt)
                    sums = terms if sums is None else [p + q for p, q in zip(sums, terms)]
            if dots is not None:
                self.gather(totals, j, sums)
        return dots if dots is None else [p + q for p, q in zip(dots, totals)]

    def finish_two(self, x, dots):
        totals = [None]
        for j in range(BLOCKS):
            base = pl.multiple_of(x * EY, 8) + 8 * j
            sums = None
            for c in range(3):
                at = pl.ds(base + c * SIZE, 8)
                q = self.free[at, :] * self.force(at)
                terms = ((self.field[at, :] - self.scaled[at, :]) * q,)
                sums = terms if sums is None else [p + r for p, r in zip(sums, terms)]
            self.gather(totals, j, sums)
        return [p + q for p, q in zip(dots, totals)]


def clear_edges(above):
    zero = jnp.zeros((8, NZ), f32)

    def body(i, carry):
        above[pl.ds(pl.multiple_of(i * TALL, 8), 8), :] = zero
        return carry

    lax.fori_loop(0, 6 * EX, body, 0, unroll=8)


def clear_row_past(refs, x):
    for ref in refs:
        for c in range(3):
            ref[pl.ds(c * SIZE + x * EY, 8), :] = jnp.zeros((8, NZ), f32)


LAST = CF + NX - 1


def inner_kernel(
    load_in, free_in, ylo, yhi, young, inverse,
    load, free, field, scaled, zsum, zdiff, zsum2, zdiff2, dots_out,
    above, minus, plus,
):
    del load_in, free_in
    for c in range(3):
        base = c * SIZE + CF * EY
        for k in range(2):
            for strip, row in ((ylo, 2 + k), (yhi, 36 + k)):
                load[pl.ds(base + row, NX, stride=EY), :] = strip[pl.ds((c * 2 + k) * NX, NX), :]
        for strip, row in ((ylo, 3), (yhi, 36)):
            free[pl.ds(base + row, NX, stride=EY), :] = strip[pl.ds((6 + c) * NX, NX), :]
    stages = Stages(load, free, inverse, field, scaled, minus, plus)
    first, second = (zsum, zdiff), (zsum2, zdiff2)

    def prepare(x, carry):
        stages.prepare(first, x)
        return carry

    lax.fori_loop(CF, LAST + 1, prepare, 0, unroll=4)
    clear_row_past(first, LAST + 1)
    clear_edges(above)
    operator_pass(zsum, zdiff, young, above, minus, plus, CF, LAST, 7)
    dots = lax.fori_loop(
        CF + 1, LAST, lambda x, d: stages.finish_one(second, x, d), [jnp.zeros((8, NZ), f32)] * 3, unroll=7
    )
    clear_row_past(second, LAST)
    operator_pass(zsum2, zdiff2, young, above, minus, plus, CF + 1, LAST - 1, 6)
    dots = dots + lax.fori_loop(CF + 2, LAST - 1, stages.finish_two, [jnp.zeros((8, NZ), f32)], unroll=4)
    for k, d in enumerate(dots):
        dots_out[k] = d


def outer_kernel(
    load_in, free_in, field_in, scaled_in, zsum_in, zdiff_in, zsum2_in, zdiff2_in,
    xlo, xhi, young, inverse, dots_in,
    load, free, field, scaled, zsum, zdiff, zsum2, zdiff2, dots_out,
    above, minus, plus,
):
    del load_in, free_in, field_in, scaled_in, zsum_in, zdiff_in, zsum2_in, zdiff2_in
    for c in range(3):
        for k in range(2):
            for plane, x in ((xlo, 2 + k), (xhi, LAST + 1 + k)):
                load[pl.ds(c * SIZE + x * EY, EY), :] = plane[pl.ds((c * 2 + k) * EY, EY), :]
        for plane, x in ((xlo, 3), (xhi, LAST + 1)):
            free[pl.ds(c * SIZE + x * EY, EY), :] = plane[pl.ds((6 + c) * EY, EY), :]
    stages = Stages(load, free, inverse, field, scaled, minus, plus)
    first, second = (zsum, zdiff), (zsum2, zdiff2)
    for start in (2, LAST + 1):
        stages.prepare(first, start)
        stages.prepare(first, start + 1)
    clear_row_past(first, LAST + 3)
    clear_row_past(second, LAST + 2)
    clear_edges(above)
    operator_pass(zsum, zdiff, young, above, minus, plus, 2, CF + 1, 2)
    operator_pass(zsum, zdiff, young, above, minus, plus, LAST - 1, LAST + 2, 2)
    stages.finish_one(second, CF - 1, None)
    stages.finish_one(second, LAST + 1, None)
    dots = [dots_in[k] for k in range(3)]
    for x in (CF, LAST):
        dots = stages.finish_one(second, x, dots)

    operator_pass(zsum2, zdiff2, young, above, minus, plus, CF - 1, CF + 2, 2)
    operator_pass(zsum2, zdiff2, young, above, minus, plus, LAST - 2, LAST + 1, 2)
    last = [dots_in[3]]
    for x in (CF, CF + 1, LAST - 1, LAST):
        last = stages.finish_two(x, last)
    dots = dots + last
    one = lax.broadcasted_iota(jnp.int32, (1, NZ), 1)
    line = jnp.zeros((1, NZ), f32)
    for k, d in enumerate(dots):
        line = jnp.where(one == k, jnp.sum(d), line)
    dots_out[...] = line


def final_kernel(parts, z, y, out, out_v, sem):
    total = jnp.sum(parts[...], axis=0, keepdims=True)
    lane = lax.broadcasted_iota(jnp.int32, (1, NZ), 1)
    zw, a, b, c = (
        jnp.sum(jnp.where(lane == k, total, 0.0), axis=1, keepdims=True) for k in range(QUANTITIES)
    )
    rz = zw + a
    alpha = rz / zw
    less = -(a / zw)
    rz1 = alpha * (alpha * b + less * a)
    energy = less * (less * zw) + 2.0 * alpha * (less * (a - b)) + alpha * (alpha * c)
    beta = rz1 / rz
    alpha1 = rz1 / (energy - beta * (rz1 / alpha))
    c1 = jnp.broadcast_to(alpha + alpha1 * (1.0 + beta), (8, NZ))[0:1, :]
    c2 = jnp.broadcast_to(-(alpha * alpha1), (8, NZ))[0:1, :]
    copies = []
    half = NX // 2
    for k in range(6):
        c, begin = k // 2, (k % 2) * half

        def body(x, carry, c=c):
            src = pl.ds(c * SIZE + (x + CF) * EY + CF, NY)
            to = pl.ds(pl.multiple_of((c * NX + x) * NY, NY), NY)
            out_v[to, :] = c1 * z[src, :] + c2 * y[src, :]
            return carry

        lax.fori_loop(begin, begin + half, body, 0, unroll=4)
        rows = pl.ds(k * half * NY, half * NY)
        copy = pltpu.make_async_copy(out_v.at[rows, :], out.at[rows, :], sem.at[k])
        copy.start()
        copies.append(copy)
    for copy in copies:
        copy.wait()


def per_device(
    body_force, fixed_dofs, load_nodes, load_forces, frequencies,
    hidden_weights, hidden_biases, output_weights, output_bias,
):
    bx, by = place()
    rows = 3 * NX * NY
    body = body_force.reshape(rows, NZ)
    fixed = fixed_dofs.reshape(rows, NZ)
    nodes = load_nodes.T
    strip = shape(9 * NX, NZ)
    ext = shape(3 * SIZE, NZ)
    load, free, ylo_send, yhi_send = call(
        pack_kernel, (ext, ext, strip, strip),
        [pltpu.HBM] * 4, (nodes, load_forces, body, fixed),
        scratch=[VMEM((rows, NZ), f32), VMEM((rows, NZ), jnp.int32), VMEM((3, LOADS), jnp.int32),
                 SMEM((3, LOADS), jnp.int32), SMEM((3, LOADS), f32), SMEM((LOADS + 8,), jnp.int32), pltpu.SemaphoreType.DMA((9,))],
        cost=pl.CostEstimate(flops=400000, transcendentals=0, bytes_accessed=2400000),
    )
    ny, nx = lax.axis_size("gy"), lax.axis_size("gx")
    def swap(lo_send, hi_send, axis, count, place):
        even = place % 2 == 0
        one = [(i, i ^ 1) for i in range(count)]
        two = [(i, (i + 1 if i % 2 else i - 1) % count) for i in range(count)]
        a = lax.ppermute(jnp.where(even, hi_send, lo_send), axis, one)
        b = lax.ppermute(jnp.where(even, lo_send, hi_send), axis, two)
        b = jnp.where((place == 0) | (place == count - 1), 0.0, b)
        return jnp.where(even, b, a), jnp.where(even, a, b)

    ylo, yhi = swap(ylo_send, yhi_send, "gy", ny, by)

    coarse = call(
        mlp_kernel, shape(GX, 16, 128),
        [VMEM] * 5,
        (frequencies, hidden_weights, hidden_biases, output_weights.reshape(1, 128), output_bias.reshape(1, 1)),
        scratch=[VMEM((16 * GX, 128), f32), VMEM((16 * GX, 128), f32), VMEM((4, 256, 256), jnp.bfloat16)],
        cost=pl.CostEstimate(flops=1500000000, transcendentals=800000, bytes_accessed=300000),
    )
    plane = shape(9 * EY, NZ)
    xlo_send, xhi_send = call(
        planes_kernel, (plane, plane), [VMEM] * 5, (load, free, ylo, yhi, coarse),
    )
    xlo, xhi = swap(xlo_send, xhi_send, "gx", nx, bx)
    young, inverse, density = call(
        density_kernel, (shape(SIZE, NZ), shape(SIZE, NZ), shape(NX * NY, NZ)),
        [VMEM], (coarse,),
        scratch=[VMEM((NX * NY, NZ), f32), pltpu.SemaphoreType.DMA],
        out_spaces=(VMEM, VMEM, pltpu.HBM),
        cost=pl.CostEstimate(flops=8000000, transcendentals=0, bytes_accessed=1300000),
    )
    work = [VMEM((6 * EX * TALL, NZ), f32), VMEM((3 * SIZE, NZ), f32), VMEM((3 * SIZE, NZ), f32)]
    *state, dots = call(
        inner_kernel, (ext,) * 8 + (shape(QUANTITIES, 8, NZ),),
        [VMEM] * 6, (load, free, ylo, yhi, young, inverse),
        scratch=work, aliases={0: 0, 1: 1},
        cost=pl.CostEstimate(flops=60000000, transcendentals=0, bytes_accessed=9000000),
    )
    *state, dots = call(
        outer_kernel, (ext,) * 8 + (shape(1, NZ),),
        [VMEM] * 13, (*state, xlo, xhi, young, inverse, dots),
        scratch=work, aliases={i: i for i in range(8)},
    )
    z, y = state[2], state[3]
    parts = lax.all_to_all(
        jnp.broadcast_to(dots, (nx * ny, NZ)), ("gx", "gy"), 0, 0, tiled=True
    )
    out = call(
        final_kernel, shape(rows, NZ), [VMEM] * 3, (parts, z, y),
        scratch=[VMEM((rows, NZ), f32), pltpu.SemaphoreType.DMA((6,))], out_spaces=pltpu.HBM,
    )
    return out.reshape(3, NX, NY, NZ), density.reshape(NX, NY, NZ)


def solution(mesh):
    return jax.shard_map(
        per_device,
        mesh=mesh,
        in_specs=(P(None, "gx", "gy", None), P(None, "gx", "gy", None)) + (P(),) * 7,
        out_specs=(P(None, "gx", "gy", None), P("gx", "gy", None)),
        check_vma=False,
    )
```

```python
import functools
import math

import jax
import jax.numpy as jnp
from jax import lax
from jax.experimental import pallas as pl
from jax.experimental.pallas import tpu as pltpu
from jax.sharding import PartitionSpec as P

CF = 4
NX, NY, NZ = 16, 32, 128
TOTAL_X, TOTAL_Y = 512, 256
CX, CY, CZ = NX // CF, NY // CF, NZ // CF
GX, GY = CX + 2, CY + 2
EX, EY = GX * CF, GY * CF
SIZE = EX * EY
LOADS = 512
NU, MU = 0.3, 1.0 / 2.6
LAM = 0.3 / (1.3 * 0.4)
RATIO = LAM / MU
DIAG = (LAM + 4.0 * MU) / 9.0
VMEM = pltpu.VMEM
SMEM = pltpu.SMEM
highest = lax.Precision.HIGHEST
f32 = jnp.float32


def spec(space=VMEM):
    return pl.BlockSpec(memory_space=space)


def call(kernel, out_shape, in_spaces, args, scratch=(), cost=None, out_spaces=None, aliases=None, limit=16):
    out_specs = jax.tree.map(lambda _: spec(), out_shape)
    if out_spaces is not None:
        out_specs = jax.tree.map(lambda _, space: spec(space), out_shape, out_spaces)
    args = [
        pltpu.with_memory_space_constraint(a, space) if space is pltpu.HBM else a
        for a, space in zip(args, in_spaces)
    ]
    if out_spaces is not None:
        out_shape = jax.tree.map(
            lambda a, space: pltpu.HBM(a.shape, a.dtype) if space is pltpu.HBM else a, out_shape, out_spaces
        )
    return pl.pallas_call(
        kernel,
        out_shape=out_shape,
        in_specs=[spec(s) for s in in_spaces],
        out_specs=out_specs,
        scratch_shapes=list(scratch),
        input_output_aliases=aliases or {},
        compiler_params=pltpu.CompilerParams(vmem_limit_bytes=limit << 20),
        cost_estimate=cost,
    )(*args)


def place():
    return lax.axis_index("gx"), lax.axis_index("gy")


def in_pairs(position, action, a, b):
    even = (position & 1) == 0

    @pl.when(even)
    def _():
        action(b, a)

    @pl.when(jnp.logical_not(even))
    def _():
        action(a, b)


def shape(*dims):
    return jax.ShapeDtypeStruct(dims, f32)


def pack_kernel(
    nodes, forces, body, fixed,
    load, free, a_out, b_out,
    body_v, fixed_v, nodes_v, nodes_s, forces_s, found, sem,
):
    part = NX * NY
    copies = [
        pltpu.make_async_copy(nodes, nodes_v, sem.at[0]),
        pltpu.make_async_copy(nodes, nodes_s, sem.at[1]),
        pltpu.make_async_copy(forces, forces_s, sem.at[2]),
    ]
    for c in range(3):
        for k, (src, dst) in enumerate(((body, body_v), (fixed, fixed_v))):
            rows = pl.ds(c * part, part)
            copies.append(pltpu.make_async_copy(src.at[rows, :], dst.at[rows, :], sem.at[3 + 2 * c + k]))
    for copy in copies:
        copy.start()

    zero = jnp.zeros((8, NZ), f32)

    def clear(x, carry):
        for c in range(3):
            base = pl.multiple_of(c * SIZE + x * EY, 8)
            for ref in (load, free):
                ref[pl.ds(base, 8), :] = zero
                ref[pl.ds(base + EY - 8, 8), :] = zero
        return carry

    lax.fori_loop(CF, CF + NX, clear, 0, unroll=2)

    ids = place()
    start_x = ids[0] * NX
    start_y = ids[1] * NY
    for copy in copies[:3]:
        copy.wait()
    lx = nodes_v[0:1, :] - start_x
    ly = nodes_v[1:2, :] - start_y
    mine = (lx >= 0) & (lx < NX) & (ly >= 0) & (ly < NY)
    index = lax.broadcasted_iota(jnp.int32, (1, LOADS), 1)
    todo = jnp.where(mine, index, LOADS)
    lane = lax.broadcasted_iota(jnp.int32, (1, NZ), 1)

    todos = [todo[:, k * 128 : (k + 1) * 128] for k in range(LOADS // 128)]

    def more(state):
        *heads, _ = state
        return functools.reduce(jnp.minimum, heads) < LOADS

    def collect(state):
        *heads, count = state
        for p in heads:
            found[count] = p
            count = count + jnp.where(p < LOADS, 1, 0)
        return (*(jnp.min(jnp.where(t > p, t, LOADS)) for t, p in zip(todos, heads)), count)

    *_, count = lax.while_loop(more, collect, (*(jnp.min(t) for t in todos), 0))
    for c in range(3):
        for copy in copies[3 + 2 * c : 5 + 2 * c]:
            copy.wait()

        def add_one(i, carry, c=c):
            p = found[i]
            row = pl.ds((c * NX + nodes_s[0, p] - start_x) * NY + nodes_s[1, p] - start_y, 1)
            hit = lane == nodes_s[2, p]
            body_v[row, :] = body_v[row, :] + jnp.where(hit, forces_s[c, p], 0.0)
            return carry

        lax.fori_loop(0, count, add_one, 0)

        def mask(x, carry, c=c):
            src = pl.ds(pl.multiple_of((c * NX + x) * NY, NY), NY)
            dst = pl.ds(c * SIZE + (x + CF) * EY + CF, NY)
            ok = fixed_v[src, :] == 0
            load[dst, :] = jnp.where(ok, body_v[src, :], 0.0)
            free[dst, :] = jnp.where(ok, 1.0, 0.0)
            return carry

        lax.fori_loop(0, NX, mask, 0, unroll=4)
    def strips(lo_out, hi_out):
        for c in range(3):
            base = c * SIZE + CF * EY + CF
            for j in range(2):
                to = pl.ds((c * 2 + j) * NX, NX)
                lo_out[to, :] = load[pl.ds(base + j, NX, stride=EY), :]
                hi_out[to, :] = load[pl.ds(base + NY - 2 + j, NX, stride=EY), :]
            to = pl.ds((6 + c) * NX, NX)
            lo_out[to, :] = free[pl.ds(base, NX, stride=EY), :]
            hi_out[to, :] = free[pl.ds(base + NY - 1, NX, stride=EY), :]

    in_pairs(ids[1], strips, a_out, b_out)


def planes_kernel(load, free, ylo, yhi, coarse, a_out, b_out):
    del coarse

    def planes(lo_out, hi_out):
        for out, first in ((lo_out, CF), (hi_out, CF + NX - 2)):
            for c in range(3):
                for j in range(2):
                    x = first + j
                    base = (c * 2 + j) * EY
                    out[pl.ds(base, EY), :] = load[pl.ds(c * SIZE + x * EY, EY), :]
                    for k in range(2):
                        at = pl.ds((c * 2 + k) * NX + x - CF, 1)
                        out[pl.ds(base + 2 + k, 1), :] = ylo[at, :]
                        out[pl.ds(base + 36 + k, 1), :] = yhi[at, :]
                x = CF if first == CF else CF + NX - 1
                base = (6 + c) * EY
                out[pl.ds(base, EY), :] = free[pl.ds(c * SIZE + x * EY, EY), :]
                at = pl.ds((6 + c) * NX + x - CF, 1)
                out[pl.ds(base + 3, 1), :] = ylo[at, :]
                out[pl.ds(base + 36, 1), :] = yhi[at, :]

    in_pairs(place()[0], planes, a_out, b_out)


def split2(v):
    hi = v.astype(jnp.bfloat16)
    return hi, (v - hi.astype(f32)).astype(jnp.bfloat16)


def doubled(w):
    hi, lo = split2(w)
    both = jnp.concatenate([hi, lo], axis=1)
    return jnp.concatenate([both, both], axis=0)


def sine_of_turns(t):
    t = t - jnp.round(t)
    a = jnp.abs(t)
    x = jnp.minimum(a, 0.5 - a) * (2.0 * math.pi)
    x2 = x * x
    p = 1.0 / 6227020800.0
    for k in (39916800.0, 362880.0, 5040.0, 120.0, 6.0, 1.0):
        p = 1.0 / k - x2 * p
    p = x * p
    return jnp.where(t < 0.0, -p, p)


GROUP = 3


def mlp_kernel(freq, weights, biases, wout, bout, coarse, axy, bxy, w2):
    ids = place()
    cx0 = ids[0] * CX - 1
    cy0 = ids[1] * CY - 1
    f = freq[...]
    ff = jnp.concatenate([f, f], axis=1)
    first = lax.broadcasted_iota(jnp.int32, (1, 128), 1) < 64
    quarter = jnp.where(first, 0.0, 0.25)

    def waves(row, start, rows, total):
        i = lax.broadcasted_iota(jnp.int32, (rows, 128), 0) + start
        turns = ff[row : row + 1, :] * ((i.astype(f32) + 0.5) * (1.0 / total))
        turns = turns - jnp.round(turns)
        wave = sine_of_turns(turns + quarter)
        return wave, pltpu.roll(wave, 64, 1)

    wx, ox = waves(0, cx0, 8, TOTAL_X // CF)
    wy, oy = waves(1, cy0, 16, TOTAL_Y // CF)
    wz, oz = waves(2, 0, CZ, CZ)
    cosx, sinx = jnp.where(first, ox, wx), jnp.where(first, wx, ox)
    cosz, sinz = jnp.where(first, oz, wz), jnp.where(first, wz, oz)
    turnedy = jnp.where(first, oy, -oy)
    for i in range(GX):
        c, s = cosx[i : i + 1, :], sinx[i : i + 1, :]
        axy[pl.ds(16 * i, 16), :] = wy * c + turnedy * s
        bxy[pl.ds(16 * i, 16), :] = turnedy * c - wy * s

    for l in range(3):
        w2[l] = doubled(weights[l] * 0.5)
    w2[3] = doubled(jnp.broadcast_to(wout[...], (128, 128)).T)
    pick = lax.broadcasted_iota(jnp.int32, (CZ, 128), 0) == (
        lax.broadcasted_iota(jnp.int32, (CZ, 128), 1) // CF
    )
    row16 = lax.broadcasted_iota(jnp.int32, (16, 128), 0)

    def body(i, carry):
        parts = []
        for k in range(GROUP):
            for j in range(GY):
                at = pl.ds(16 * (GROUP * i + k) + j, 1)
                parts.append(axy[at, :] * cosz + bxy[at, :] * sinz)
        h = jnp.concatenate(parts, axis=0)
        for l in range(4):
            hi, lo = split2(h)
            both = jnp.concatenate([hi, lo], axis=1)
            out = jnp.dot(both, w2[l], preferred_element_type=f32)
            h = out[:, :128] + out[:, 128:]
            if l < 3:
                h = h + biases[l : l + 1, :] * 0.5
                h = h + h * jnp.tanh(h)
        for k in range(GROUP):
            logits = jnp.zeros((16, 128), f32)
            for j in range(GY):
                cell = (k * GY + j) * CZ
                line = jnp.sum(jnp.where(pick, h[cell : cell + CZ, :], 0.0), axis=0, keepdims=True)
                logits = jnp.where(row16 == (j + 15) % 16, line, logits)
            coarse[GROUP * i + k] = 1.0 / (1.0 + jnp.exp(-(logits + bout[...])))
        return carry

    lax.fori_loop(0, GX // GROUP, body, 0)


W0, W1, W2, W3 = 2.0, 1.0, 2.0 - math.sqrt(2.0), 2.0 - math.sqrt(3.0)
SCALE = MU / 16.0


def density_kernel(coarse, young, inverse, density, density_v, sem):
    ids = place()
    lane = lax.broadcasted_iota(jnp.int32, (16, NZ), 1)
    not_last, not_first = lane < NZ - 1, lane > 0
    row16 = lax.broadcasted_iota(jnp.int32, (16, NZ), 0)
    y_cell = ids[1] * CY + jnp.where(row16 == 15, -1, row16)
    inside_y = (y_cell >= 0) & (y_cell < TOTAL_Y // CF)

    ri = lax.broadcasted_iota(jnp.int32, (EY + NY, 144), 0)
    ci = lax.broadcasted_iota(jnp.int32, (EY + NY, 144), 1)
    r = jnp.where(ri < EY, ri, ri - EY + CF)
    oy = r & 3
    kind = jnp.where(oy == 0, 0, jnp.where(oy == 3, 2, 1))
    want = kind * 16 + (((r >> 2) + 15) & 15)
    spread = jnp.where(
        (ci == want) | (ci == want + 48) | (ci == want + 96), 1.0, 0.0
    ).astype(jnp.bfloat16)
    y_fine = ids[1] * NY - CF + lax.broadcasted_iota(jnp.int32, (EY, NZ), 0)
    inside_rows = jnp.where((y_fine >= 0) & (y_fine < TOTAL_Y), SCALE, 0.0)

    def layers(v):
        side = jnp.where(not_last, pltpu.roll(v, NZ - 1, 1), 0.0) + jnp.where(
            not_first, pltpu.roll(v, 1, 1), 0.0
        )
        return W0 * v + W1 * side, W1 * v + W2 * side, W2 * v + W3 * side

    side = jnp.where(not_last, 1.0, 0.0) + jnp.where(not_first, 1.0, 0.0)
    ones = (W0 + W1 * side, W1 + W2 * side, W2 + W3 * side)
    rows_in = jnp.where(inside_y, 1.0, 0.0)
    stacks = []
    for i in range(GX):
        x_cell = ids[0] * CX - 1 + i
        ok_x = (x_cell >= 0) & (x_cell < TOTAL_X // CF)
        inside = jnp.where(inside_y & ok_x, 1.0, 0.0)
        stacks.append((
            layers(jnp.where(inside > 0.0, coarse[i], 0.0)),
            [inside * w for w in ones],
            inside > 0.0,
            jnp.where(ok_x, 1.0, 0.0),
        ))

    for i in range(GX):
        for plane_kind in range(3):
            low = max(i - 1, 0) if plane_kind == 0 else i
            high = min(i + 1, GX - 1) if plane_kind == 2 else i
            sums = []
            for which in range(2):
                here, below, over = stacks[i][which], stacks[low][which], stacks[high][which]
                t0 = here[0] + (below[1] + over[1])
                t1 = here[1] + (below[2] + over[2])
                down = pltpu.roll(t1, 1, 0)
                above = pltpu.roll(t1, 15, 0)
                sums.append((t0 + (down + t1), t0 + (t1 + t1), t0 + (t1 + above)))
            rho = jnp.concatenate(
                [a / jnp.where(stacks[i][2], b, 1.0) for a, b in zip(*sums)], axis=0
            )
            hi = rho.astype(jnp.bfloat16)
            rest = rho - hi.astype(f32)
            mid = rest.astype(jnp.bfloat16)
            lo = (rest - mid.astype(f32)).astype(jnp.bfloat16)
            fine = jnp.dot(spread, jnp.concatenate([hi, mid, lo], axis=0), preferred_element_type=f32)
            ext = fine[:EY, :]
            modulus = (0.02 + 0.98 * (ext * ext * ext)) * (inside_rows * stacks[i][3])
            for ox in {0: (0,), 1: (1, 2), 2: (3,)}[plane_kind]:
                x = i * CF + ox
                young[pl.ds(x * EY, EY), :] = modulus
                if 1 <= i <= CX:
                    density_v[pl.ds((x - CF) * NY, NY), :] = fine[EY:, :]

    copy = pltpu.make_async_copy(density_v, density, sem)
    copy.start()
    lane8 = lax.broadcasted_iota(jnp.int32, (8, NZ), 1) > 0

    def plane(x, carry):
        for j in range(EY // 8):
            at = x * EY + 8 * j
            if j == 0:
                at = pl.multiple_of(at, 8)
            total = (young[pl.ds(at, 8), :] + young[pl.ds(at - 1, 8), :]) + (
                young[pl.ds(at - EY, 8), :] + young[pl.ds(at - EY - 1, 8), :]
            )
            total = total + jnp.where(lane8, pltpu.roll(total, 1, 1), 0.0)
            inverse[pl.ds(at, 8), :] = 1.0 / (DIAG / SCALE * total + 1e-30)
        return carry

    lax.fori_loop(2, 22, plane, 0, unroll=2)
    copy.wait()


QUANTITIES = 4
BLOCKS = EY // 8
TALL = EY + 8


def operator_pass(zsum, zdiff, young, above, minus, plus, begin, end, unroll):
    def block(yb, carry):
        r0 = yb * 8

        def transform(x):
            out = []
            for c in range(3):
                at = c * SIZE + x * EY + r0
                pairs = [(t[pl.ds(at, 8), :], t[pl.ds(at + 1, 8), :]) for t in (zsum, zdiff)]
                out += [v + u for v, u in pairs] + [u - v for v, u in pairs]
            return out

        def modal(x, a, b):
            e1 = young[pl.ds(pl.multiple_of(x * EY + r0, 8), 8), :]
            e3 = e1 * (1.0 / 3.0)
            e31 = e1 * 0.5
            e9 = e1 * ((RATIO + 4.0) / 9.0)
            s = [p + q for p, q in zip(a, b)]
            d = [q - p for p, q in zip(a, b)]
            u = lambda c, p, q, r: (d if p else s)[4 * c + 2 * q + r]
            g = {}
            ux, uy, uz = u(0, 1, 0, 0), u(1, 0, 1, 0), u(2, 0, 0, 1)
            trace = RATIO * (ux + uy + uz)
            g[0, 1, 0, 0] = e1 * ((ux + ux) + trace)
            g[1, 0, 1, 0] = e1 * ((uy + uy) + trace)
            g[2, 0, 0, 1] = e1 * ((uz + uz) + trace)
            g[0, 0, 1, 0] = g[1, 1, 0, 0] = e1 * (u(0, 0, 1, 0) + u(1, 1, 0, 0))
            g[0, 0, 0, 1] = g[2, 1, 0, 0] = e1 * (u(0, 0, 0, 1) + u(2, 1, 0, 0))
            g[1, 0, 0, 1] = g[2, 0, 1, 0] = e1 * (u(1, 0, 0, 1) + u(2, 0, 1, 0))
            for one, two in (
                ((0, 1, 0, 1), (1, 0, 1, 1)),
                ((0, 1, 1, 0), (2, 0, 1, 1)),
                ((1, 1, 1, 0), (2, 1, 0, 1)),
            ):
                p, q = u(*one), u(*two)
                g[one] = e31 * (3.0 * p + q)
                g[two] = e31 * (3.0 * q + p)
            p, q, r = u(0, 0, 1, 1), u(1, 1, 0, 1), u(2, 1, 1, 0)
            total = p + q + r
            g[0, 0, 1, 1] = e3 * (p + total)
            g[1, 1, 0, 1] = e3 * (q + total)
            g[2, 1, 1, 0] = e3 * (r + total)
            for c in range(3):
                g[c, 1, 1, 1] = e9 * u(c, 1, 1, 1)
            return g

        def keep(g):
            out = []
            for c in range(3):
                out.append(g[c, 1, 0, 0])
                for q, r in ((0, 1), (1, 0), (1, 1)):
                    out.append(g[c, 0, q, r] + g[c, 1, q, r])
            return out

        def step(x, state):
            a, held = state
            b = transform(x + 1)
            g = modal(x, a, b)
            for c in range(3):
                f = [held[4 * c] - g[c, 1, 0, 0]]
                for k, (q, r) in enumerate(((0, 1), (1, 0), (1, 1))):
                    f.append((g[c, 0, q, r] - g[c, 1, q, r]) + held[4 * c + 1 + k])
                h = []
                for r in range(2):
                    at = ((2 * c + r) * EX + x) * TALL + 8 + r0
                    above[pl.ds(at, 8), :] = f[r] + f[2 + r]
                    h.append((f[r] - f[2 + r]) + above[pl.ds(at - 1, 8), :])
                rows = pl.ds(pl.multiple_of(c * SIZE + x * EY + r0, 8), 8)
                minus[rows, :] = h[0] - h[1]
                plus[rows, :] = h[0] + h[1]
            return b, keep(g)

        a = transform(begin)
        b = transform(begin + 1)
        lax.fori_loop(begin + 1, end, step, (b, keep(modal(begin, a, b))), unroll=unroll)
        return carry

    lax.fori_loop(0, BLOCKS, block, 0)


class Stages:
    def __init__(self, load, free, inverse, field, scaled, minus, plus):
        self.load, self.free, self.inverse = load, free, inverse
        self.field, self.scaled, self.minus, self.plus = field, scaled, minus, plus
        lane = lax.broadcasted_iota(jnp.int32, (8, NZ), 1)
        row = lax.broadcasted_iota(jnp.int32, (8, NZ), 0)
        self.not_last, self.not_first = lane < NZ - 1, lane > 0
        self.first_rows = jnp.where(row >= CF, 1.0, 0.0)
        self.last_rows = jnp.where(row < CF, 1.0, 0.0)

    def z_stage(self, out, at, v):
        n = jnp.where(self.not_last, pltpu.roll(v, NZ - 1, 1), 0.0)
        out[0][at, :] = v + n
        out[1][at, :] = n - v

    def prepare(self, out, x):
        for j in range(BLOCKS):
            base = pl.multiple_of(x * EY, 8) + 8 * j
            inv = self.inverse[pl.ds(base, 8), :]
            for c in range(3):
                at = pl.ds(base + c * SIZE, 8)
                v = self.load[at, :] * inv
                self.field[at, :] = v
                self.z_stage(out, at, v)

    def gather(self, totals, j, terms):
        for k, t in enumerate(terms):
            if j == 0:
                t = t * self.first_rows
            if j == BLOCKS - 1:
                t = t * self.last_rows
            totals[k] = t if totals[k] is None else totals[k] + t

    def force(self, at):
        return self.minus[at, :] + jnp.where(self.not_first, pltpu.roll(self.plus[at, :], 1, 1), 0.0)

    def finish_one(self, out, x, dots):
        totals = [None] * 3
        for j in range(BLOCKS):
            base = pl.multiple_of(x * EY, 8) + 8 * j
            inv = self.inverse[pl.ds(base, 8), :]
            sums = None
            for c in range(3):
                at = pl.ds(base + c * SIZE, 8)
                w = self.free[at, :] * self.force(at)
                y = w * inv
                z = self.field[at, :]
                zt = z - y
                self.scaled[at, :] = y
                self.z_stage(out, at, zt)
                if dots is not None:
                    rt = self.load[at, :] - w
                    terms = (z * w, z * rt, zt * rt)
                    sums = terms if sums is None else [p + q for p, q in zip(sums, terms)]
            if dots is not None:
                self.gather(totals, j, sums)
        return dots if dots is None else [p + q for p, q in zip(dots, totals)]

    def finish_two(self, x, dots):
        totals = [None]
        for j in range(BLOCKS):
            base = pl.multiple_of(x * EY, 8) + 8 * j
            sums = None
            for c in range(3):
                at = pl.ds(base + c * SIZE, 8)
                q = self.free[at, :] * self.force(at)
                terms = ((self.field[at, :] - self.scaled[at, :]) * q,)
                sums = terms if sums is None else [p + r for p, r in zip(sums, terms)]
            self.gather(totals, j, sums)
        return [p + q for p, q in zip(dots, totals)]


def clear_edges(above):
    zero = jnp.zeros((8, NZ), f32)

    def body(i, carry):
        above[pl.ds(pl.multiple_of(i * TALL, 8), 8), :] = zero
        return carry

    lax.fori_loop(0, 6 * EX, body, 0, unroll=8)


def clear_row_past(refs, x):
    for ref in refs:
        for c in range(3):
            ref[pl.ds(c * SIZE + x * EY, 8), :] = jnp.zeros((8, NZ), f32)


LAST = CF + NX - 1


def inner_kernel(
    load_in, free_in, ylo, yhi, young, inverse,
    load, free, field, scaled, zsum, zdiff, zsum2, zdiff2, dots_out,
    above, minus, plus,
):
    del load_in, free_in
    for c in range(3):
        base = c * SIZE + CF * EY
        for k in range(2):
            for strip, row in ((ylo, 2 + k), (yhi, 36 + k)):
                load[pl.ds(base + row, NX, stride=EY), :] = strip[pl.ds((c * 2 + k) * NX, NX), :]
        for strip, row in ((ylo, 3), (yhi, 36)):
            free[pl.ds(base + row, NX, stride=EY), :] = strip[pl.ds((6 + c) * NX, NX), :]
    stages = Stages(load, free, inverse, field, scaled, minus, plus)
    first, second = (zsum, zdiff), (zsum2, zdiff2)

    def prepare(x, carry):
        stages.prepare(first, x)
        return carry

    lax.fori_loop(CF, LAST + 1, prepare, 0, unroll=4)
    clear_row_past(first, LAST + 1)
    clear_edges(above)
    operator_pass(zsum, zdiff, young, above, minus, plus, CF, LAST, 7)
    dots = lax.fori_loop(
        CF + 1, LAST, lambda x, d: stages.finish_one(second, x, d), [jnp.zeros((8, NZ), f32)] * 3, unroll=7
    )
    clear_row_past(second, LAST)
    operator_pass(zsum2, zdiff2, young, above, minus, plus, CF + 1, LAST - 1, 6)
    dots = dots + lax.fori_loop(CF + 2, LAST - 1, stages.finish_two, [jnp.zeros((8, NZ), f32)], unroll=4)
    for k, d in enumerate(dots):
        dots_out[k] = d


def outer_kernel(
    load_in, free_in, field_in, scaled_in, zsum_in, zdiff_in, zsum2_in, zdiff2_in,
    xa, xb, young, inverse, dots_in,
    load, free, field, scaled, zsum, zdiff, zsum2, zdiff2, dots_out,
    above, minus, plus,
):
    del load_in, free_in, field_in, scaled_in, zsum_in, zdiff_in, zsum2_in, zdiff2_in
    bx = place()[0]

    def insert(xlo, xhi):
        for c in range(3):
            for plane, x, k, ok in (
                (xlo, 2, 0, bx > 0),
                (xlo, 3, 1, bx > 0),
                (xhi, LAST + 1, 0, bx < TOTAL_X // NX - 1),
                (xhi, LAST + 2, 1, bx < TOTAL_X // NX - 1),
            ):
                load[pl.ds(c * SIZE + x * EY, EY), :] = jnp.where(
                    ok, plane[pl.ds((c * 2 + k) * EY, EY), :], 0.0
                )
                if x in (3, LAST + 1):
                    free[pl.ds(c * SIZE + x * EY, EY), :] = jnp.where(
                        ok, plane[pl.ds((6 + c) * EY, EY), :], 0.0
                    )

    in_pairs(bx, insert, xa, xb)
    stages = Stages(load, free, inverse, field, scaled, minus, plus)
    first, second = (zsum, zdiff), (zsum2, zdiff2)
    for start in (2, LAST + 1):
        stages.prepare(first, start)
        stages.prepare(first, start + 1)
    clear_row_past(first, LAST + 3)
    clear_row_past(second, LAST + 2)
    clear_edges(above)
    operator_pass(zsum, zdiff, young, above, minus, plus, 2, CF + 1, 2)
    operator_pass(zsum, zdiff, young, above, minus, plus, LAST - 1, LAST + 2, 2)
    stages.finish_one(second, CF - 1, None)
    stages.finish_one(second, LAST + 1, None)
    dots = [dots_in[k] for k in range(3)]
    for x in (CF, LAST):
        dots = stages.finish_one(second, x, dots)

    operator_pass(zsum2, zdiff2, young, above, minus, plus, CF - 1, CF + 2, 2)
    operator_pass(zsum2, zdiff2, young, above, minus, plus, LAST - 2, LAST + 1, 2)
    last = [dots_in[3]]
    for x in (CF, CF + 1, LAST - 1, LAST):
        last = stages.finish_two(x, last)
    dots = dots + last
    one = lax.broadcasted_iota(jnp.int32, (1, NZ), 1)
    line = jnp.zeros((1, NZ), f32)
    for k, d in enumerate(dots):
        line = jnp.where(one == k, jnp.sum(d), line)
    dots_out[...] = line


def final_kernel(parts, z, y, out, out_v, sem):
    total = jnp.sum(parts[...], axis=0, keepdims=True)
    lane = lax.broadcasted_iota(jnp.int32, (1, NZ), 1)
    zw, a, b, c = (
        jnp.sum(jnp.where(lane == k, total, 0.0), axis=1, keepdims=True) for k in range(QUANTITIES)
    )
    rz = zw + a
    alpha = rz / zw
    less = -(a / zw)
    rz1 = alpha * (alpha * b + less * a)
    energy = less * (less * zw) + 2.0 * alpha * (less * (a - b)) + alpha * (alpha * c)
    beta = rz1 / rz
    alpha1 = rz1 / (energy - beta * (rz1 / alpha))
    c1 = jnp.broadcast_to(alpha + alpha1 * (1.0 + beta), (8, NZ))[0:1, :]
    c2 = jnp.broadcast_to(-(alpha * alpha1), (8, NZ))[0:1, :]
    copies = []
    half = NX // 2
    for k in range(6):
        c, begin = k // 2, (k % 2) * half

        def body(x, carry, c=c):
            src = pl.ds(c * SIZE + (x + CF) * EY + CF, NY)
            to = pl.ds(pl.multiple_of((c * NX + x) * NY, NY), NY)
            out_v[to, :] = c1 * z[src, :] + c2 * y[src, :]
            return carry

        lax.fori_loop(begin, begin + half, body, 0, unroll=4)
        rows = pl.ds(k * half * NY, half * NY)
        copy = pltpu.make_async_copy(out_v.at[rows, :], out.at[rows, :], sem.at[k])
        copy.start()
        copies.append(copy)
    for copy in copies:
        copy.wait()


def per_device(
    body_force, fixed_dofs, load_nodes, load_forces, frequencies,
    hidden_weights, hidden_biases, output_weights, output_bias,
):
    bx, by = place()
    rows = 3 * NX * NY
    body = body_force.reshape(rows, NZ)
    fixed = fixed_dofs.reshape(rows, NZ)
    nodes = load_nodes.T
    strip = shape(9 * NX, NZ)
    ext = shape(3 * SIZE, NZ)
    load, free, ya_send, yb_send = call(
        pack_kernel, (ext, ext, strip, strip),
        [pltpu.HBM] * 4, (nodes, load_forces, body, fixed),
        scratch=[VMEM((rows, NZ), f32), VMEM((rows, NZ), jnp.int32), VMEM((3, LOADS), jnp.int32),
                 SMEM((3, LOADS), jnp.int32), SMEM((3, LOADS), f32), SMEM((LOADS + 8,), jnp.int32), pltpu.SemaphoreType.DMA((9,))],
        cost=pl.CostEstimate(flops=400000, transcendentals=0, bytes_accessed=2400000),
    )
    ny, nx = lax.axis_size("gy"), lax.axis_size("gx")
    def swap(a_send, b_send, axis, count):
        one = [(i, i ^ 1) for i in range(count)]
        two = [(i, (i + 1 if i % 2 else i - 1) % count) for i in range(count)]
        return lax.ppermute(a_send, axis, one), lax.ppermute(b_send, axis, two)

    ya, yb = swap(ya_send, yb_send, "gy", ny)
    yb = jnp.where((by == 0) | (by == ny - 1), 0.0, yb)
    ylo, yhi = jnp.where(by % 2 == 0, yb, ya), jnp.where(by % 2 == 0, ya, yb)

    coarse = call(
        mlp_kernel, shape(GX, 16, 128),
        [VMEM] * 5,
        (frequencies, hidden_weights, hidden_biases, output_weights.reshape(1, 128), output_bias.reshape(1, 1)),
        scratch=[VMEM((16 * GX, 128), f32), VMEM((16 * GX, 128), f32), VMEM((4, 256, 256), jnp.bfloat16)],
        cost=pl.CostEstimate(flops=1500000000, transcendentals=800000, bytes_accessed=300000),
    )
    plane = shape(9 * EY, NZ)
    xa_send, xb_send = call(
        planes_kernel, (plane, plane), [VMEM] * 5, (load, free, ylo, yhi, coarse),
    )
    xa, xb = swap(xa_send, xb_send, "gx", nx)
    young, inverse, density = call(
        density_kernel, (shape(SIZE, NZ), shape(SIZE, NZ), shape(NX * NY, NZ)),
        [VMEM], (coarse,),
        scratch=[VMEM((NX * NY, NZ), f32), pltpu.SemaphoreType.DMA],
        out_spaces=(VMEM, VMEM, pltpu.HBM),
        cost=pl.CostEstimate(flops=8000000, transcendentals=0, bytes_accessed=1300000),
    )
    work = [VMEM((6 * EX * TALL, NZ), f32), VMEM((3 * SIZE, NZ), f32), VMEM((3 * SIZE, NZ), f32)]
    *state, dots = call(
        inner_kernel, (ext,) * 8 + (shape(QUANTITIES, 8, NZ),),
        [VMEM] * 6, (load, free, ylo, yhi, young, inverse),
        scratch=work, aliases={0: 0, 1: 1},
        cost=pl.CostEstimate(flops=60000000, transcendentals=0, bytes_accessed=9000000),
    )
    *state, dots = call(
        outer_kernel, (ext,) * 8 + (shape(1, NZ),),
        [VMEM] * 13, (*state, xa, xb, young, inverse, dots),
        scratch=work, aliases={i: i for i in range(8)},
    )
    z, y = state[2], state[3]
    parts = lax.all_to_all(
        jnp.broadcast_to(dots, (nx * ny, NZ)), ("gx", "gy"), 0, 0, tiled=True
    )
    out = call(
        final_kernel, shape(rows, NZ), [VMEM] * 3, (parts, z, y),
        scratch=[VMEM((rows, NZ), f32), pltpu.SemaphoreType.DMA((6,))], out_spaces=pltpu.HBM,
    )
    return out.reshape(3, NX, NY, NZ), density.reshape(NX, NY, NZ)


def solution(mesh):
    return jax.shard_map(
        per_device,
        mesh=mesh,
        in_specs=(P(None, "gx", "gy", None), P(None, "gx", "gy", None)) + (P(),) * 7,
        out_specs=(P(None, "gx", "gy", None), P("gx", "gy", None)),
        check_vma=False,
    )
```

```python
import functools
import math

import jax
import jax.numpy as jnp
from jax import lax
from jax.experimental import pallas as pl
from jax.experimental.pallas import tpu as pltpu
from jax.sharding import PartitionSpec as P

CF = 4
NX, NY, NZ = 16, 32, 128
TOTAL_X, TOTAL_Y = 512, 256
CX, CY, CZ = NX // CF, NY // CF, NZ // CF
GX, GY = CX + 2, CY + 2
EX, EY = GX * CF, GY * CF
SIZE = EX * EY
LOADS = 512
NU, MU = 0.3, 1.0 / 2.6
LAM = 0.3 / (1.3 * 0.4)
RATIO = LAM / MU
DIAG = (LAM + 4.0 * MU) / 9.0
VMEM = pltpu.VMEM
SMEM = pltpu.SMEM
highest = lax.Precision.HIGHEST
f32 = jnp.float32


def spec(space=VMEM):
    return pl.BlockSpec(memory_space=space)


def call(kernel, out_shape, in_spaces, args, scratch=(), cost=None, out_spaces=None, aliases=None, limit=16):
    out_specs = jax.tree.map(lambda _: spec(), out_shape)
    if out_spaces is not None:
        out_specs = jax.tree.map(lambda _, space: spec(space), out_shape, out_spaces)
    args = [
        pltpu.with_memory_space_constraint(a, space) if space is pltpu.HBM else a
        for a, space in zip(args, in_spaces)
    ]
    if out_spaces is not None:
        out_shape = jax.tree.map(
            lambda a, space: pltpu.HBM(a.shape, a.dtype) if space is pltpu.HBM else a, out_shape, out_spaces
        )
    return pl.pallas_call(
        kernel,
        out_shape=out_shape,
        in_specs=[spec(s) for s in in_spaces],
        out_specs=out_specs,
        scratch_shapes=list(scratch),
        input_output_aliases=aliases or {},
        compiler_params=pltpu.CompilerParams(vmem_limit_bytes=limit << 20),
        cost_estimate=cost,
    )(*args)


def place():
    return lax.axis_index("gx"), lax.axis_index("gy")


def in_pairs(position, action, a, b):
    even = (position & 1) == 0

    @pl.when(even)
    def _():
        action(b, a)

    @pl.when(jnp.logical_not(even))
    def _():
        action(a, b)


def shape(*dims):
    return jax.ShapeDtypeStruct(dims, f32)


def pack_kernel(
    nodes, forces, body, fixed,
    load, free, a_out, b_out,
    body_v, fixed_v, nodes_v, nodes_s, forces_s, found, sem,
):
    part = NX * NY
    copies = [
        pltpu.make_async_copy(nodes, nodes_v, sem.at[0]),
        pltpu.make_async_copy(nodes, nodes_s, sem.at[1]),
        pltpu.make_async_copy(forces, forces_s, sem.at[2]),
    ]
    for c in range(3):
        for k, (src, dst) in enumerate(((body, body_v), (fixed, fixed_v))):
            rows = pl.ds(c * part, part)
            copies.append(pltpu.make_async_copy(src.at[rows, :], dst.at[rows, :], sem.at[3 + 2 * c + k]))
    for copy in copies:
        copy.start()

    zero = jnp.zeros((8, NZ), f32)

    def clear(x, carry):
        for c in range(3):
            base = pl.multiple_of(c * SIZE + x * EY, 8)
            for ref in (load, free):
                ref[pl.ds(base, 8), :] = zero
                ref[pl.ds(base + EY - 8, 8), :] = zero
        return carry

    lax.fori_loop(CF, CF + NX, clear, 0, unroll=2)

    ids = place()
    start_x = ids[0] * NX
    start_y = ids[1] * NY
    for copy in copies[:3]:
        copy.wait()
    lx = nodes_v[0:1, :] - start_x
    ly = nodes_v[1:2, :] - start_y
    mine = (lx >= 0) & (lx < NX) & (ly >= 0) & (ly < NY)
    index = lax.broadcasted_iota(jnp.int32, (1, LOADS), 1)
    todo = jnp.where(mine, index, LOADS)
    lane = lax.broadcasted_iota(jnp.int32, (1, NZ), 1)

    todos = [todo[:, k * 128 : (k + 1) * 128] for k in range(LOADS // 128)]

    def more(state):
        *heads, _ = state
        return functools.reduce(jnp.minimum, heads) < LOADS

    def collect(state):
        *heads, count = state
        for p in heads:
            found[count] = p
            count = count + jnp.where(p < LOADS, 1, 0)
        return (*(jnp.min(jnp.where(t > p, t, LOADS)) for t, p in zip(todos, heads)), count)

    *_, count = lax.while_loop(more, collect, (*(jnp.min(t) for t in todos), 0))
    for c in range(3):
        for copy in copies[3 + 2 * c : 5 + 2 * c]:
            copy.wait()

        def add_one(i, carry, c=c):
            p = found[i]
            row = pl.ds((c * NX + nodes_s[0, p] - start_x) * NY + nodes_s[1, p] - start_y, 1)
            hit = lane == nodes_s[2, p]
            body_v[row, :] = body_v[row, :] + jnp.where(hit, forces_s[c, p], 0.0)
            return carry

        lax.fori_loop(0, count, add_one, 0)

        def mask(x, carry, c=c):
            src = pl.ds(pl.multiple_of((c * NX + x) * NY, NY), NY)
            dst = pl.ds(c * SIZE + (x + CF) * EY + CF, NY)
            ok = fixed_v[src, :] == 0
            load[dst, :] = jnp.where(ok, body_v[src, :], 0.0)
            free[dst, :] = jnp.where(ok, 1.0, 0.0)
            return carry

        lax.fori_loop(0, NX, mask, 0, unroll=4)
    def strips(lo_out, hi_out):
        for c in range(3):
            base = c * SIZE + CF * EY + CF
            for j in range(2):
                to = pl.ds((c * 2 + j) * NX, NX)
                lo_out[to, :] = load[pl.ds(base + j, NX, stride=EY), :]
                hi_out[to, :] = load[pl.ds(base + NY - 2 + j, NX, stride=EY), :]
            to = pl.ds((6 + c) * NX, NX)
            lo_out[to, :] = free[pl.ds(base, NX, stride=EY), :]
            hi_out[to, :] = free[pl.ds(base + NY - 1, NX, stride=EY), :]

    in_pairs(ids[1], strips, a_out, b_out)


def planes_kernel(load, free, ylo, yhi, coarse, a_out, b_out):
    del coarse

    def planes(lo_out, hi_out):
        for out, first in ((lo_out, CF), (hi_out, CF + NX - 2)):
            for c in range(3):
                for j in range(2):
                    x = first + j
                    base = (c * 2 + j) * EY
                    out[pl.ds(base, EY), :] = load[pl.ds(c * SIZE + x * EY, EY), :]
                    for k in range(2):
                        at = pl.ds((c * 2 + k) * NX + x - CF, 1)
                        out[pl.ds(base + 2 + k, 1), :] = ylo[at, :]
                        out[pl.ds(base + 36 + k, 1), :] = yhi[at, :]
                x = CF if first == CF else CF + NX - 1
                base = (6 + c) * EY
                out[pl.ds(base, EY), :] = free[pl.ds(c * SIZE + x * EY, EY), :]
                at = pl.ds((6 + c) * NX + x - CF, 1)
                out[pl.ds(base + 3, 1), :] = ylo[at, :]
                out[pl.ds(base + 36, 1), :] = yhi[at, :]

    in_pairs(place()[0], planes, a_out, b_out)


def split2(v):
    hi = v.astype(jnp.bfloat16)
    return hi, (v - hi.astype(f32)).astype(jnp.bfloat16)


def doubled(w):
    hi, lo = split2(w)
    both = jnp.concatenate([hi, lo], axis=1)
    return jnp.concatenate([both, both], axis=0)


def sine_of_turns(t):
    t = t - jnp.round(t)
    a = jnp.abs(t)
    x = jnp.minimum(a, 0.5 - a) * (2.0 * math.pi)
    x2 = x * x
    p = 1.0 / 6227020800.0
    for k in (39916800.0, 362880.0, 5040.0, 120.0, 6.0, 1.0):
        p = 1.0 / k - x2 * p
    p = x * p
    return jnp.where(t < 0.0, -p, p)


GROUP = 3


def mlp_kernel(freq, weights, biases, wout, bout, coarse, axy, bxy, w2):
    ids = place()
    cx0 = ids[0] * CX - 1
    cy0 = ids[1] * CY - 1
    f = freq[...]
    ff = jnp.concatenate([f, f], axis=1)
    first = lax.broadcasted_iota(jnp.int32, (1, 128), 1) < 64
    quarter = jnp.where(first, 0.0, 0.25)

    def waves(row, start, rows, total):
        i = lax.broadcasted_iota(jnp.int32, (rows, 128), 0) + start
        turns = ff[row : row + 1, :] * ((i.astype(f32) + 0.5) * (1.0 / total))
        turns = turns - jnp.round(turns)
        wave = sine_of_turns(turns + quarter)
        return wave, pltpu.roll(wave, 64, 1)

    wx, ox = waves(0, cx0, 8, TOTAL_X // CF)
    wy, oy = waves(1, cy0, 16, TOTAL_Y // CF)
    wz, oz = waves(2, 0, CZ, CZ)
    cosx, sinx = jnp.where(first, ox, wx), jnp.where(first, wx, ox)
    cosz, sinz = jnp.where(first, oz, wz), jnp.where(first, wz, oz)
    turnedy = jnp.where(first, oy, -oy)
    for i in range(GX):
        c, s = cosx[i : i + 1, :], sinx[i : i + 1, :]
        axy[pl.ds(16 * i, 16), :] = wy * c + turnedy * s
        bxy[pl.ds(16 * i, 16), :] = turnedy * c - wy * s

    for l in range(3):
        w2[l] = doubled(weights[l] * 0.5)
    w2[3] = doubled(jnp.broadcast_to(wout[...], (128, 128)).T)
    pick = lax.broadcasted_iota(jnp.int32, (CZ, 128), 0) == (
        lax.broadcasted_iota(jnp.int32, (CZ, 128), 1) // CF
    )
    row16 = lax.broadcasted_iota(jnp.int32, (16, 128), 0)

    def body(i, carry):
        parts = []
        for k in range(GROUP):
            for j in range(GY):
                at = pl.ds(16 * (GROUP * i + k) + j, 1)
                parts.append(axy[at, :] * cosz + bxy[at, :] * sinz)
        h = jnp.concatenate(parts, axis=0)
        for l in range(4):
            hi, lo = split2(h)
            both = jnp.concatenate([hi, lo], axis=1)
            out = jnp.dot(both, w2[l], preferred_element_type=f32)
            h = out[:, :128] + out[:, 128:]
            if l < 3:
                h = h + biases[l : l + 1, :] * 0.5
                h = h + h * jnp.tanh(h)
        for k in range(GROUP):
            logits = jnp.zeros((16, 128), f32)
            for j in range(GY):
                cell = (k * GY + j) * CZ
                line = jnp.sum(jnp.where(pick, h[cell : cell + CZ, :], 0.0), axis=0, keepdims=True)
                logits = jnp.where(row16 == (j + 15) % 16, line, logits)
            coarse[GROUP * i + k] = 1.0 / (1.0 + jnp.exp(-(logits + bout[...])))
        return carry

    lax.fori_loop(0, GX // GROUP, body, 0)


W0, W1, W2, W3 = 2.0, 1.0, 2.0 - math.sqrt(2.0), 2.0 - math.sqrt(3.0)
SCALE = MU / 16.0


def density_kernel(coarse, young, inverse, density, density_v, sem):
    ids = place()
    lane = lax.broadcasted_iota(jnp.int32, (16, NZ), 1)
    not_last, not_first = lane < NZ - 1, lane > 0
    row16 = lax.broadcasted_iota(jnp.int32, (16, NZ), 0)
    y_cell = ids[1] * CY + jnp.where(row16 == 15, -1, row16)
    inside_y = (y_cell >= 0) & (y_cell < TOTAL_Y // CF)

    ri = lax.broadcasted_iota(jnp.int32, (EY + NY, 144), 0)
    ci = lax.broadcasted_iota(jnp.int32, (EY + NY, 144), 1)
    r = jnp.where(ri < EY, ri, ri - EY + CF)
    oy = r & 3
    kind = jnp.where(oy == 0, 0, jnp.where(oy == 3, 2, 1))
    want = kind * 16 + (((r >> 2) + 15) & 15)
    spread = jnp.where(
        (ci == want) | (ci == want + 48) | (ci == want + 96), 1.0, 0.0
    ).astype(jnp.bfloat16)
    y_fine = ids[1] * NY - CF + lax.broadcasted_iota(jnp.int32, (EY, NZ), 0)
    inside_rows = jnp.where((y_fine >= 0) & (y_fine < TOTAL_Y), SCALE, 0.0)

    def layers(v):
        side = jnp.where(not_last, pltpu.roll(v, NZ - 1, 1), 0.0) + jnp.where(
            not_first, pltpu.roll(v, 1, 1), 0.0
        )
        return W0 * v + W1 * side, W1 * v + W2 * side, W2 * v + W3 * side

    side = jnp.where(not_last, 1.0, 0.0) + jnp.where(not_first, 1.0, 0.0)
    ones = (W0 + W1 * side, W1 + W2 * side, W2 + W3 * side)
    rows_in = jnp.where(inside_y, 1.0, 0.0)
    stacks = []
    for i in range(GX):
        x_cell = ids[0] * CX - 1 + i
        ok_x = (x_cell >= 0) & (x_cell < TOTAL_X // CF)
        inside = jnp.where(inside_y & ok_x, 1.0, 0.0)
        stacks.append((
            layers(jnp.where(inside > 0.0, coarse[i], 0.0)),
            [inside * w for w in ones],
            inside > 0.0,
            jnp.where(ok_x, 1.0, 0.0),
        ))

    for i in range(GX):
        for plane_kind in range(3):
            low = max(i - 1, 0) if plane_kind == 0 else i
            high = min(i + 1, GX - 1) if plane_kind == 2 else i
            sums = []
            for which in range(2):
                here, below, over = stacks[i][which], stacks[low][which], stacks[high][which]
                t0 = here[0] + (below[1] + over[1])
                t1 = here[1] + (below[2] + over[2])
                down = pltpu.roll(t1, 1, 0)
                above = pltpu.roll(t1, 15, 0)
                sums.append((t0 + (down + t1), t0 + (t1 + t1), t0 + (t1 + above)))
            rho = jnp.concatenate(
                [a / jnp.where(stacks[i][2], b, 1.0) for a, b in zip(*sums)], axis=0
            )
            hi = rho.astype(jnp.bfloat16)
            rest = rho - hi.astype(f32)
            mid = rest.astype(jnp.bfloat16)
            lo = (rest - mid.astype(f32)).astype(jnp.bfloat16)
            fine = jnp.dot(spread, jnp.concatenate([hi, mid, lo], axis=0), preferred_element_type=f32)
            ext = fine[:EY, :]
            modulus = (0.02 + 0.98 * (ext * ext * ext)) * (inside_rows * stacks[i][3])
            for ox in {0: (0,), 1: (1, 2), 2: (3,)}[plane_kind]:
                x = i * CF + ox
                young[pl.ds(x * EY, EY), :] = modulus
                if 1 <= i <= CX:
                    density_v[pl.ds((x - CF) * NY, NY), :] = fine[EY:, :]

    copy = pltpu.make_async_copy(density_v, density, sem)
    copy.start()
    lane8 = lax.broadcasted_iota(jnp.int32, (8, NZ), 1) > 0

    def plane(x, carry):
        for j in range(EY // 8):
            at = x * EY + 8 * j
            if j == 0:
                at = pl.multiple_of(at, 8)
            total = (young[pl.ds(at, 8), :] + young[pl.ds(at - 1, 8), :]) + (
                young[pl.ds(at - EY, 8), :] + young[pl.ds(at - EY - 1, 8), :]
            )
            total = total + jnp.where(lane8, pltpu.roll(total, 1, 1), 0.0)
            inverse[pl.ds(at, 8), :] = 1.0 / (DIAG / SCALE * total + 1e-30)
        return carry

    lax.fori_loop(2, 22, plane, 0, unroll=2)
    copy.wait()


QUANTITIES = 4
BLOCKS = EY // 8
TALL = EY + 8


def operator_pass(zsum, zdiff, young, above, minus, plus, begin, end, unroll):
    def block(yb, carry):
        r0 = yb * 8

        def transform(x):
            out = []
            for c in range(3):
                at = c * SIZE + x * EY + r0
                pairs = [(t[pl.ds(at, 8), :], t[pl.ds(at + 1, 8), :]) for t in (zsum, zdiff)]
                out += [v + u for v, u in pairs] + [u - v for v, u in pairs]
            return out

        def modal(x, a, b):
            e1 = young[pl.ds(pl.multiple_of(x * EY + r0, 8), 8), :]
            e3 = e1 * (1.0 / 3.0)
            e31 = e1 * 0.5
            e9 = e1 * ((RATIO + 4.0) / 9.0)
            s = [p + q for p, q in zip(a, b)]
            d = [q - p for p, q in zip(a, b)]
            u = lambda c, p, q, r: (d if p else s)[4 * c + 2 * q + r]
            g = {}
            ux, uy, uz = u(0, 1, 0, 0), u(1, 0, 1, 0), u(2, 0, 0, 1)
            trace = RATIO * (ux + uy + uz)
            g[0, 1, 0, 0] = e1 * ((ux + ux) + trace)
            g[1, 0, 1, 0] = e1 * ((uy + uy) + trace)
            g[2, 0, 0, 1] = e1 * ((uz + uz) + trace)
            g[0, 0, 1, 0] = g[1, 1, 0, 0] = e1 * (u(0, 0, 1, 0) + u(1, 1, 0, 0))
            g[0, 0, 0, 1] = g[2, 1, 0, 0] = e1 * (u(0, 0, 0, 1) + u(2, 1, 0, 0))
            g[1, 0, 0, 1] = g[2, 0, 1, 0] = e1 * (u(1, 0, 0, 1) + u(2, 0, 1, 0))
            for one, two in (
                ((0, 1, 0, 1), (1, 0, 1, 1)),
                ((0, 1, 1, 0), (2, 0, 1, 1)),
                ((1, 1, 1, 0), (2, 1, 0, 1)),
            ):
                p, q = u(*one), u(*two)
                g[one] = e31 * (3.0 * p + q)
                g[two] = e31 * (3.0 * q + p)
            p, q, r = u(0, 0, 1, 1), u(1, 1, 0, 1), u(2, 1, 1, 0)
            total = p + q + r
            g[0, 0, 1, 1] = e3 * (p + total)
            g[1, 1, 0, 1] = e3 * (q + total)
            g[2, 1, 1, 0] = e3 * (r + total)
            for c in range(3):
                g[c, 1, 1, 1] = e9 * u(c, 1, 1, 1)
            return g

        def keep(g):
            out = []
            for c in range(3):
                out.append(g[c, 1, 0, 0])
                for q, r in ((0, 1), (1, 0), (1, 1)):
                    out.append(g[c, 0, q, r] + g[c, 1, q, r])
            return out

        def step(x, state):
            a, held = state
            b = transform(x + 1)
            g = modal(x, a, b)
            for c in range(3):
                f = [held[4 * c] - g[c, 1, 0, 0]]
                for k, (q, r) in enumerate(((0, 1), (1, 0), (1, 1))):
                    f.append((g[c, 0, q, r] - g[c, 1, q, r]) + held[4 * c + 1 + k])
                h = []
                for r in range(2):
                    at = ((2 * c + r) * EX + x) * TALL + 8 + r0
                    above[pl.ds(at, 8), :] = f[r] + f[2 + r]
                    h.append((f[r] - f[2 + r]) + above[pl.ds(at - 1, 8), :])
                rows = pl.ds(pl.multiple_of(c * SIZE + x * EY + r0, 8), 8)
                minus[rows, :] = h[0] - h[1]
                plus[rows, :] = h[0] + h[1]
            return b, keep(g)

        a = transform(begin)
        b = transform(begin + 1)
        lax.fori_loop(begin + 1, end, step, (b, keep(modal(begin, a, b))), unroll=unroll)
        return carry

    lax.fori_loop(0, BLOCKS, block, 0)


class Stages:
    def __init__(self, load, free, inverse, field, scaled, minus, plus):
        self.load, self.free, self.inverse = load, free, inverse
        self.field, self.scaled, self.minus, self.plus = field, scaled, minus, plus
        lane = lax.broadcasted_iota(jnp.int32, (8, NZ), 1)
        row = lax.broadcasted_iota(jnp.int32, (8, NZ), 0)
        self.not_last, self.not_first = lane < NZ - 1, lane > 0
        self.first_rows = jnp.where(row >= CF, 1.0, 0.0)
        self.last_rows = jnp.where(row < CF, 1.0, 0.0)

    def z_stage(self, out, at, v):
        n = jnp.where(self.not_last, pltpu.roll(v, NZ - 1, 1), 0.0)
        out[0][at, :] = v + n
        out[1][at, :] = n - v

    def prepare(self, out, x):
        for j in range(BLOCKS):
            base = pl.multiple_of(x * EY, 8) + 8 * j
            inv = self.inverse[pl.ds(base, 8), :]
            for c in range(3):
                at = pl.ds(base + c * SIZE, 8)
                v = self.load[at, :] * inv
                self.field[at, :] = v
                self.z_stage(out, at, v)

    def gather(self, totals, j, terms):
        for k, t in enumerate(terms):
            if j == 0:
                t = t * self.first_rows
            if j == BLOCKS - 1:
                t = t * self.last_rows
            totals[k] = t if totals[k] is None else totals[k] + t

    def force(self, at):
        return self.minus[at, :] + jnp.where(self.not_first, pltpu.roll(self.plus[at, :], 1, 1), 0.0)

    def finish_one(self, out, x, dots):
        totals = [None] * 3
        for j in range(BLOCKS):
            base = pl.multiple_of(x * EY, 8) + 8 * j
            inv = self.inverse[pl.ds(base, 8), :]
            sums = None
            for c in range(3):
                at = pl.ds(base + c * SIZE, 8)
                w = self.free[at, :] * self.force(at)
                y = w * inv
                z = self.field[at, :]
                zt = z - y
                self.scaled[at, :] = y
                self.z_stage(out, at, zt)
                if dots is not None:
                    rt = self.load[at, :] - w
                    terms = (z * w, z * rt, zt * rt)
                    sums = terms if sums is None else [p + q for p, q in zip(sums, terms)]
            if dots is not None:
                self.gather(totals, j, sums)
        return dots if dots is None else [p + q for p, q in zip(dots, totals)]

    def finish_two(self, x, dots):
        totals = [None]
        for j in range(BLOCKS):
            base = pl.multiple_of(x * EY, 8) + 8 * j
            sums = None
            for c in range(3):
                at = pl.ds(base + c * SIZE, 8)
                q = self.free[at, :] * self.force(at)
                terms = ((self.field[at, :] - self.scaled[at, :]) * q,)
                sums = terms if sums is None else [p + r for p, r in zip(sums, terms)]
            self.gather(totals, j, sums)
        return [p + q for p, q in zip(dots, totals)]


def clear_edges(above):
    zero = jnp.zeros((8, NZ), f32)

    def body(i, carry):
        above[pl.ds(pl.multiple_of(i * TALL, 8), 8), :] = zero
        return carry

    lax.fori_loop(0, 6 * EX, body, 0, unroll=8)


def clear_row_past(refs, x):
    for ref in refs:
        for c in range(3):
            ref[pl.ds(c * SIZE + x * EY, 8), :] = jnp.zeros((8, NZ), f32)


LAST = CF + NX - 1


def inner_kernel(
    load_in, free_in, ylo, yhi, young, inverse,
    load, free, field, scaled, zsum, zdiff, zsum2, zdiff2, dots_out,
    above, minus, plus,
):
    del load_in, free_in
    for c in range(3):
        base = c * SIZE + CF * EY
        for k in range(2):
            for strip, row in ((ylo, 2 + k), (yhi, 36 + k)):
                load[pl.ds(base + row, NX, stride=EY), :] = strip[pl.ds((c * 2 + k) * NX, NX), :]
        for strip, row in ((ylo, 3), (yhi, 36)):
            free[pl.ds(base + row, NX, stride=EY), :] = strip[pl.ds((6 + c) * NX, NX), :]
    stages = Stages(load, free, inverse, field, scaled, minus, plus)
    first, second = (zsum, zdiff), (zsum2, zdiff2)

    def prepare(x, carry):
        stages.prepare(first, x)
        return carry

    lax.fori_loop(CF, LAST + 1, prepare, 0, unroll=4)
    clear_row_past(first, LAST + 1)
    clear_edges(above)
    operator_pass(zsum, zdiff, young, above, minus, plus, CF, LAST, 14)
    dots = lax.fori_loop(
        CF + 1, LAST, lambda x, d: stages.finish_one(second, x, d), [jnp.zeros((8, NZ), f32)] * 3, unroll=7
    )
    clear_row_past(second, LAST)
    operator_pass(zsum2, zdiff2, young, above, minus, plus, CF + 1, LAST - 1, 12)
    dots = dots + lax.fori_loop(CF + 2, LAST - 1, stages.finish_two, [jnp.zeros((8, NZ), f32)], unroll=4)
    for k, d in enumerate(dots):
        dots_out[k] = d


def outer_kernel(
    load_in, free_in, field_in, scaled_in, zsum_in, zdiff_in, zsum2_in, zdiff2_in,
    xa, xb, young, inverse, dots_in,
    load, free, field, scaled, zsum, zdiff, zsum2, zdiff2, dots_out,
    above, minus, plus,
):
    del load_in, free_in, field_in, scaled_in, zsum_in, zdiff_in, zsum2_in, zdiff2_in
    bx = place()[0]

    def insert(xlo, xhi):
        for c in range(3):
            for plane, x, k, ok in (
                (xlo, 2, 0, bx > 0),
                (xlo, 3, 1, bx > 0),
                (xhi, LAST + 1, 0, bx < TOTAL_X // NX - 1),
                (xhi, LAST + 2, 1, bx < TOTAL_X // NX - 1),
            ):
                load[pl.ds(c * SIZE + x * EY, EY), :] = jnp.where(
                    ok, plane[pl.ds((c * 2 + k) * EY, EY), :], 0.0
                )
                if x in (3, LAST + 1):
                    free[pl.ds(c * SIZE + x * EY, EY), :] = jnp.where(
                        ok, plane[pl.ds((6 + c) * EY, EY), :], 0.0
                    )

    in_pairs(bx, insert, xa, xb)
    stages = Stages(load, free, inverse, field, scaled, minus, plus)
    first, second = (zsum, zdiff), (zsum2, zdiff2)
    for start in (2, LAST + 1):
        stages.prepare(first, start)
        stages.prepare(first, start + 1)
    clear_row_past(first, LAST + 3)
    clear_row_past(second, LAST + 2)
    clear_edges(above)
    operator_pass(zsum, zdiff, young, above, minus, plus, 2, CF + 1, 2)
    operator_pass(zsum, zdiff, young, above, minus, plus, LAST - 1, LAST + 2, 2)
    stages.finish_one(second, CF - 1, None)
    stages.finish_one(second, LAST + 1, None)
    dots = [dots_in[k] for k in range(3)]
    for x in (CF, LAST):
        dots = stages.finish_one(second, x, dots)

    operator_pass(zsum2, zdiff2, young, above, minus, plus, CF - 1, CF + 2, 2)
    operator_pass(zsum2, zdiff2, young, above, minus, plus, LAST - 2, LAST + 1, 2)
    last = [dots_in[3]]
    for x in (CF, CF + 1, LAST - 1, LAST):
        last = stages.finish_two(x, last)
    dots = dots + last
    one = lax.broadcasted_iota(jnp.int32, (1, NZ), 1)
    line = jnp.zeros((1, NZ), f32)
    for k, d in enumerate(dots):
        line = jnp.where(one == k, jnp.sum(d), line)
    dots_out[...] = line


def final_kernel(parts, z, y, out, out_v, sem):
    total = jnp.sum(parts[...], axis=0, keepdims=True)
    lane = lax.broadcasted_iota(jnp.int32, (1, NZ), 1)
    zw, a, b, c = (
        jnp.sum(jnp.where(lane == k, total, 0.0), axis=1, keepdims=True) for k in range(QUANTITIES)
    )
    rz = zw + a
    alpha = rz / zw
    less = -(a / zw)
    rz1 = alpha * (alpha * b + less * a)
    energy = less * (less * zw) + 2.0 * alpha * (less * (a - b)) + alpha * (alpha * c)
    beta = rz1 / rz
    alpha1 = rz1 / (energy - beta * (rz1 / alpha))
    c1 = jnp.broadcast_to(alpha + alpha1 * (1.0 + beta), (8, NZ))[0:1, :]
    c2 = jnp.broadcast_to(-(alpha * alpha1), (8, NZ))[0:1, :]
    copies = []
    half = NX // 2
    for k in range(6):
        c, begin = k // 2, (k % 2) * half

        def body(x, carry, c=c):
            src = pl.ds(c * SIZE + (x + CF) * EY + CF, NY)
            to = pl.ds(pl.multiple_of((c * NX + x) * NY, NY), NY)
            out_v[to, :] = c1 * z[src, :] + c2 * y[src, :]
            return carry

        lax.fori_loop(begin, begin + half, body, 0, unroll=4)
        rows = pl.ds(k * half * NY, half * NY)
        copy = pltpu.make_async_copy(out_v.at[rows, :], out.at[rows, :], sem.at[k])
        copy.start()
        copies.append(copy)
    for copy in copies:
        copy.wait()


def per_device(
    body_force, fixed_dofs, load_nodes, load_forces, frequencies,
    hidden_weights, hidden_biases, output_weights, output_bias,
):
    bx, by = place()
    rows = 3 * NX * NY
    body = body_force.reshape(rows, NZ)
    fixed = fixed_dofs.reshape(rows, NZ)
    nodes = load_nodes.T
    strip = shape(9 * NX, NZ)
    ext = shape(3 * SIZE, NZ)
    load, free, ya_send, yb_send = call(
        pack_kernel, (ext, ext, strip, strip),
        [pltpu.HBM] * 4, (nodes, load_forces, body, fixed),
        scratch=[VMEM((rows, NZ), f32), VMEM((rows, NZ), jnp.int32), VMEM((3, LOADS), jnp.int32),
                 SMEM((3, LOADS), jnp.int32), SMEM((3, LOADS), f32), SMEM((LOADS + 8,), jnp.int32), pltpu.SemaphoreType.DMA((9,))],
        cost=pl.CostEstimate(flops=400000, transcendentals=0, bytes_accessed=2400000),
    )
    ny, nx = lax.axis_size("gy"), lax.axis_size("gx")
    def swap(a_send, b_send, axis, count):
        one = [(i, i ^ 1) for i in range(count)]
        two = [(i, (i + 1 if i % 2 else i - 1) % count) for i in range(count)]
        return lax.ppermute(a_send, axis, one), lax.ppermute(b_send, axis, two)

    ya, yb = swap(ya_send, yb_send, "gy", ny)
    yb = jnp.where((by == 0) | (by == ny - 1), 0.0, yb)
    ylo, yhi = jnp.where(by % 2 == 0, yb, ya), jnp.where(by % 2 == 0, ya, yb)

    coarse = call(
        mlp_kernel, shape(GX, 16, 128),
        [VMEM] * 5,
        (frequencies, hidden_weights, hidden_biases, output_weights.reshape(1, 128), output_bias.reshape(1, 1)),
        scratch=[VMEM((16 * GX, 128), f32), VMEM((16 * GX, 128), f32), VMEM((4, 256, 256), jnp.bfloat16)],
        cost=pl.CostEstimate(flops=1500000000, transcendentals=800000, bytes_accessed=300000),
    )
    plane = shape(9 * EY, NZ)
    xa_send, xb_send = call(
        planes_kernel, (plane, plane), [VMEM] * 5, (load, free, ylo, yhi, coarse),
    )
    xa, xb = swap(xa_send, xb_send, "gx", nx)
    young, inverse, density = call(
        density_kernel, (shape(SIZE, NZ), shape(SIZE, NZ), shape(NX * NY, NZ)),
        [VMEM], (coarse,),
        scratch=[VMEM((NX * NY, NZ), f32), pltpu.SemaphoreType.DMA],
        out_spaces=(VMEM, VMEM, pltpu.HBM),
        cost=pl.CostEstimate(flops=8000000, transcendentals=0, bytes_accessed=1300000),
    )
    work = [VMEM((6 * EX * TALL, NZ), f32), VMEM((3 * SIZE, NZ), f32), VMEM((3 * SIZE, NZ), f32)]
    *state, dots = call(
        inner_kernel, (ext,) * 8 + (shape(QUANTITIES, 8, NZ),),
        [VMEM] * 6, (load, free, ylo, yhi, young, inverse),
        scratch=work, aliases={0: 0, 1: 1},
        cost=pl.CostEstimate(flops=60000000, transcendentals=0, bytes_accessed=9000000),
    )
    *state, dots = call(
        outer_kernel, (ext,) * 8 + (shape(1, NZ),),
        [VMEM] * 13, (*state, xa, xb, young, inverse, dots),
        scratch=work, aliases={i: i for i in range(8)},
    )
    z, y = state[2], state[3]
    parts = lax.all_to_all(
        jnp.broadcast_to(dots, (nx * ny, NZ)), ("gx", "gy"), 0, 0, tiled=True
    )
    out = call(
        final_kernel, shape(rows, NZ), [VMEM] * 3, (parts, z, y),
        scratch=[VMEM((rows, NZ), f32), pltpu.SemaphoreType.DMA((6,))], out_spaces=pltpu.HBM,
    )
    return out.reshape(3, NX, NY, NZ), density.reshape(NX, NY, NZ)


def solution(mesh):
    return jax.shard_map(
        per_device,
        mesh=mesh,
        in_specs=(P(None, "gx", "gy", None), P(None, "gx", "gy", None)) + (P(),) * 7,
        out_specs=(P(None, "gx", "gy", None), P("gx", "gy", None)),
        check_vma=False,
    )
```
